256 devices in a mesh: dp: 16 (over x, y), shard: 16 (over z, core).
Axes of the slice: x: 4, y: 4, z: 8, core: 2. Of those that a mesh axis runs over, the one named last changes fastest.
Arguments:
- id_table: float32 [2097152, 128], P(('dp', 'shard')), may hold values from -6 to 6
- ada_state: float32 [2097152], P(('dp', 'shard')), may hold values from 0.01 to 1
- user_first: float32 [128, 512], replicated, may hold values from -0.5 to 0.5
- user_second: float32 [512, 128], replicated, may hold values from -0.25 to 0.25
- item_first: float32 [128, 512], replicated, may hold values from -0.5 to 0.5
- item_second: float32 [512, 128], replicated, may hold values from -0.25 to 0.25
- fetch_rows: int32 [256, 16, 16, 9], P(('dp', 'shard')), may hold values from 0 to 8191
- lookup_slots: int32 [256, 1536], P(('dp', 'shard')), may hold values from 0 to 2303
Outputs:
- new_table: float32 [2097152, 128], P(('dp', 'shard'))
- new_state: float32 [2097152], P(('dp', 'shard'))
- user_first_grad: float32 [128, 512], replicated
- user_second_grad: float32 [512, 128], replicated
- item_first_grad: float32 [128, 512], replicated
- item_second_grad: float32 [512, 128], replicated
- mean_loss: float32 [], replicated
The draws below stay inside these ranges and needn't reach their ends.
All inputs are finite; a program needn't handle non-finite values.
Results may differ from the reference program's by a relative error of at most 0.0038.
The reference program's roundings to bfloat16 on the way count: a program that leaves them out, or rounds other values in their place, can miss the bound.
Values may be sent and summed in bfloat16 or wider, within the bound.
A program may use at most 128 MiB of HBM per device.

```python
import math
import jax
import jax.numpy as jnp
import numpy as np
from jax import lax

D = 128
HIDDEN_SIZE = 512
ROWS_DEV = 8192
EXAMPLES_ON_CHIP = 512
LOOK_DEV = 1536
CAND_DEV = 1024
CAP = 9
TABLE_ROWS = 2097152
N_DP = 16
N_SHARD = 16


def with_ends(entries, rng, low, top_value):
    longest = entries.shape.index(max(entries.shape))
    spots = []
    for shift in (0, 1):
        where = [jax.random.randint(jax.random.fold_in(rng, axis), (), 0, length) for axis, length in enumerate(entries.shape)]
        where[longest] = (where[longest] + shift) % entries.shape[longest]
        spots.append(tuple(where))
    return entries.at[spots[0]].set(low).at[spots[1]].set(top_value)


def steps_of(key, extent, split, low, top_value):
    level, own = 1.0, jax.random.fold_in(key, 6)
    for position, blocks in split:
        draws = jnp.exp(jax.random.uniform(jax.random.fold_in(own, position), (blocks,), jnp.float32, low / len(split), top_value / len(split)))
        level = level * jnp.repeat(draws, extent[position] // blocks).reshape([-1 if axis == position else 1 for axis in range(len(extent))])
    return level


def rank_table(number_of, skew):
    weights = [(1 << 20) // math.isqrt(grade ** skew) + 1 for grade in range(1, number_of + 1)]
    scale = 1 + sum(weights) // (1 << 30)
    return np.cumsum(np.array([max(1, weight // scale) for weight in weights]))


def skewed_ids(own_key, shape, count, lean):
    listing = rank_table(count, lean)
    ticket = jax.random.randint(jax.random.fold_in(own_key, 1), shape, 0, int(listing[count - 1]))
    grade = jnp.searchsorted(jnp.asarray(listing, jnp.int32), ticket, side="right")
    return jax.random.permutation(jax.random.fold_in(own_key, 2), count)[grade].astype(jnp.int32)


def bell_draw(key, dims, deviation, limit, cuts=(), held_as=jnp.bfloat16):
    entries = deviation * jax.random.normal(key, dims, jnp.float32)
    if cuts:
        entries = entries * steps_of(key, dims, cuts, -0.22, 0.18)
    return jnp.clip(entries, -limit, limit).astype(held_as)


def setup_inputs(seed: int = 0) -> dict:
    seeds = jax.random.split(jax.random.key(seed), 9)
    id_table = bell_draw(seeds[0], (TABLE_ROWS, D), 1.0, 6.0, ((0, 256),), jnp.float32)
    ada_state = jnp.clip(jnp.exp(math.log(1.0) - 4.6051702 * jax.random.uniform(seeds[1], (TABLE_ROWS,), jnp.float32) ** steps_of(seeds[1], (TABLE_ROWS,), ((0, 256),), -0.2, 0.2)), 0.01, 1.0)
    user_first = bell_draw(seeds[2], (D, HIDDEN_SIZE), D ** -0.5, 0.5, (), jnp.float32)
    user_second = bell_draw(seeds[3], (HIDDEN_SIZE, D), HIDDEN_SIZE ** -0.5, 0.25, (), jnp.float32)
    item_first = bell_draw(seeds[4], (D, HIDDEN_SIZE), D ** -0.5, 0.5, (), jnp.float32)
    item_second = bell_draw(seeds[5], (HIDDEN_SIZE, D), HIDDEN_SIZE ** -0.5, 0.25, (), jnp.float32)
    fetch_rows = with_ends(jax.random.randint(seeds[6], (N_DP * N_SHARD, N_DP, N_SHARD, CAP), 0, ROWS_DEV), jax.random.fold_in(seeds[6], 1), 0, ROWS_DEV - 1).astype(jnp.int32)
    lookup_slots = with_ends(skewed_ids(seeds[7], (N_DP * N_SHARD, LOOK_DEV), N_DP * N_SHARD * CAP, 1), jax.random.fold_in(seeds[7], 3), 0, (N_DP * N_SHARD * CAP) - 1).astype(jnp.int32)
    return {"id_table": id_table, "ada_state": ada_state, "user_first": user_first, "user_second": user_second, "item_first": item_first, "item_second": item_second, "fetch_rows": fetch_rows, "lookup_slots": lookup_slots}


highest = lax.Precision.HIGHEST
logit_divisor = 0.025
learn_rate = 0.1
epsilon = 1e-08

def tower_pass(looked, first_w, second_w):
    hidden_act = jax.nn.silu(jnp.dot(looked, first_w, precision=highest, preferred_element_type=jnp.float32))
    tower_out = jnp.dot(hidden_act, second_w, precision=highest, preferred_element_type=jnp.float32)
    return tower_out / jnp.sqrt(lax.optimization_barrier(jnp.sum(tower_out * tower_out, axis=1, keepdims=True)) + 1e-06)

def one_group(pair):
    pooled_queries, pooled_targets = pair
    logit_table = jnp.dot(pooled_queries, pooled_targets.T, preferred_element_type=jnp.float32) / logit_divisor
    exponent = jnp.exp(logit_table)
    reduced_aggregates = lax.optimization_barrier(jnp.sum(exponent, axis=1))
    collected_entries = jnp.dot(exponent.astype(jnp.bfloat16), pooled_targets, preferred_element_type=jnp.float32)
    log_z = jnp.log(reduced_aggregates)
    softmax = jnp.exp(logit_table - log_z[:, None]).astype(jnp.bfloat16)
    target_derivative_accrual = jnp.dot(softmax.T, pooled_queries, preferred_element_type=jnp.float32)
    return (reduced_aggregates, collected_entries, log_z, target_derivative_accrual)

def reference(id_table, ada_state, user_first, user_second, item_first, item_second, fetch_rows, lookup_slots):
    shard_number = N_DP * N_SHARD
    target_index_vector = id_table.shape[1]
    owners = jnp.arange(shard_number * CAP, dtype=jnp.int32) // CAP * ROWS_DEV
    row_map = fetch_rows.reshape(shard_number, shard_number * CAP) + owners[None, :]
    row_ids = jnp.take_along_axis(row_map, lookup_slots, axis=1)
    looked = jnp.take(id_table, row_ids.reshape(-1), axis=0).reshape(shard_number, LOOK_DEV, target_index_vector)
    user_in = looked[:, :EXAMPLES_ON_CHIP].reshape(-1, target_index_vector)
    item_in = looked[:, EXAMPLES_ON_CHIP:].reshape(-1, target_index_vector)
    user_vec, user_pull = jax.vjp(tower_pass, user_in, user_first, user_second)
    item_vec, item_pull = jax.vjp(tower_pass, item_in, item_first, item_second)
    user_half_precision = user_vec.astype(jnp.bfloat16)
    item_bf = item_vec.astype(jnp.bfloat16)
    pooled_queries = user_half_precision.reshape(N_DP, N_SHARD, EXAMPLES_ON_CHIP, target_index_vector).transpose(1, 0, 2, 3).reshape(N_SHARD, N_DP * EXAMPLES_ON_CHIP, target_index_vector)
    pooled_targets = item_bf.reshape(N_DP, N_SHARD, CAND_DEV, target_index_vector).transpose(1, 0, 2, 3).reshape(N_SHARD, N_DP * CAND_DEV, target_index_vector)
    reduced_aggregates, collected_entries, log_z, target_derivative_accrual = lax.map(one_group, (pooled_queries, pooled_targets))
    reduced_aggregates = reduced_aggregates.reshape(N_SHARD, N_DP, EXAMPLES_ON_CHIP).transpose(1, 0, 2).reshape(-1)
    log_z = log_z.reshape(N_SHARD, N_DP, EXAMPLES_ON_CHIP).transpose(1, 0, 2).reshape(-1)
    collected_entries = collected_entries.reshape(N_SHARD, N_DP, EXAMPLES_ON_CHIP, target_index_vector).transpose(1, 0, 2, 3).reshape(-1, target_index_vector)
    target_derivative_accrual = target_derivative_accrual.reshape(N_SHARD, N_DP, CAND_DEV, target_index_vector).transpose(1, 0, 2, 3).reshape(shard_number, CAND_DEV, target_index_vector)
    resident_target_entries = item_bf.reshape(shard_number, CAND_DEV, target_index_vector)[:, :EXAMPLES_ON_CHIP].reshape(-1, target_index_vector).astype(jnp.float32)
    query_single_float = user_half_precision.astype(jnp.float32)
    matching_pair_logit = lax.optimization_barrier(jnp.sum(query_single_float * resident_target_entries, axis=1)) / logit_divisor
    query_adjoint = (collected_entries / reduced_aggregates[:, None] - resident_target_entries) / logit_divisor
    target_adjoint = target_derivative_accrual.at[:, :EXAMPLES_ON_CHIP].add(-query_single_float.reshape(shard_number, EXAMPLES_ON_CHIP, target_index_vector)).reshape(-1, target_index_vector) / logit_divisor
    user_look, user_first_g, user_second_g = user_pull(query_adjoint)
    item_look, item_first_g, item_second_g = item_pull(target_adjoint)
    look_grads = jnp.concatenate([user_look.reshape(shard_number, EXAMPLES_ON_CHIP, target_index_vector), item_look.reshape(shard_number, CAND_DEV, target_index_vector)], axis=1).reshape(-1, target_index_vector)
    grad_rows = jnp.zeros_like(id_table).at[row_ids.reshape(-1)].add(look_grads)
    new_state = ada_state + lax.optimization_barrier(jnp.mean(grad_rows * grad_rows, axis=1))
    new_table = id_table - learn_rate * grad_rows / (jnp.sqrt(new_state)[:, None] + epsilon)
    mean_loss = jnp.sum(log_z - matching_pair_logit) / (shard_number * EXAMPLES_ON_CHIP)
    return (new_table, new_state, user_first_g / shard_number, user_second_g / shard_number, item_first_g / shard_number, item_second_g / shard_number, mean_loss)
```

```python
import functools
import math

import jax
import jax.numpy as jnp
from jax import lax
from jax.experimental import pallas as pl
from jax.experimental.pallas import tpu as pltpu
from jax.sharding import Mesh
from jax.sharding import PartitionSpec as P

DP_SHARD = ("dp_0", "dp_1", "shard_0", "shard_1")
DP = ("dp_0", "dp_1")
SHARD = ("shard_0", "shard_1")
MESH = pl.DeviceIdType.MESH
EXAMPLES = 512

highest = lax.Precision.HIGHEST
logit_divisor = 0.025
learn_rate = 0.1
epsilon = 1e-08
LOG2_SCALE = math.log2(math.e) / logit_divisor


def in_blocks(shard, dim, size):
    shape = shard.shape
    blocks = shard.reshape(*shape[:dim], size, shape[dim] // size, *shape[dim + 1 :])
    return jnp.moveaxis(blocks, dim, 0)


def laid_out(blocks, dim):
    blocks = jnp.moveaxis(blocks, 0, dim)
    shape = blocks.shape
    return blocks.reshape(*shape[:dim], shape[dim] * shape[dim + 1], *shape[dim + 2 :])


def one_exchange(shard, axis, axes, splits, concats):
    sizes = [lax.axis_size(a) for a in axes]
    blocks = in_blocks(shard, splits[0], sizes[0])
    blocks = jnp.moveaxis(in_blocks(blocks, splits[1] + 1, sizes[1]), 0, 1)
    inside = blocks.shape[2:]
    blocks = blocks.reshape(-1, *inside)
    blocks = lax.all_to_all(blocks, axis, split_axis=0, concat_axis=0, tiled=True)
    blocks = laid_out(blocks.reshape(*sizes, *inside), concats[0] + 1)
    return laid_out(blocks, concats[1])


def tower_pass(looked, first_w, second_w):
    hidden_act = jax.nn.silu(
        jnp.dot(looked, first_w, precision=highest, preferred_element_type=jnp.float32)
    )
    tower_out = jnp.dot(hidden_act, second_w, precision=highest, preferred_element_type=jnp.float32)
    return tower_out / jnp.sqrt(jnp.sum(tower_out * tower_out, axis=1, keepdims=True) + 1e-06)


UT = 256
CT = 512
IT = 256

USER_GATHER, ITEM_GATHER, TOTALS, PULLED, ITEM_SUMS = range(5)


def nt(a, b):
    return lax.dot_general(a, b, (((1,), (1,)), ((), ())), preferred_element_type=jnp.float32)


def score_kernel(
    user_ref,
    item_ref,
    pulled_ref,
    totals_ref,
    isum_ref,
    users,
    items,
    acc,
    pull,
    pull_in,
    tot,
    tot_in,
    lz,
    part,
    part_in,
    send_sem,
    recv_sem,
):
    n_user = user_ref.shape[0]
    n_item = item_ref.shape[0]
    side = 4
    x = lax.axis_index("dp_0")
    y = lax.axis_index("dp_1")

    def peer(axis, k):
        if axis == "dp_0":
            return {"dp_0": lax.rem(x + k, side)}
        return {"dp_1": lax.rem(y + k, side)}

    def push(kind, axis, k, src, dst):
        copy = pltpu.make_async_remote_copy(
            src_ref=src,
            dst_ref=dst,
            send_sem=send_sem.at[kind, k - 1],
            recv_sem=recv_sem.at[kind, k - 1],
            device_id=peer(axis, k),
            device_id_type=MESH,
        )
        copy.start()
        return copy

    barrier = pltpu.get_barrier_semaphore()
    for axis in ("dp_0", "dp_1"):
        for k in range(1, side):
            pl.semaphore_signal(barrier, inc=1, device_id=peer(axis, k), device_id_type=MESH)
    pl.semaphore_wait(barrier, 2 * (side - 1))

    item_copies, user_copies = {}, {}
    for k in (1, 3, 2):
        user_copies[side - k] = push(
            USER_GATHER, "dp_0", k, user_ref, users.at[pl.ds((side - k) * n_user, n_user)]
        )
        item_copies[side - k] = push(
            ITEM_GATHER, "dp_1", k, item_ref, items.at[pl.ds((side - k) * n_item, n_item)]
        )
    users[pl.ds(0, n_user), :] = user_ref[...]
    items[pl.ds(0, n_item), :] = item_ref[...]

    def pass_one(j, low, high):
        def step(n, carry):
            rows = pl.ds(pl.multiple_of(n * UT, UT), UT)
            u = users[rows, :]
            total = jnp.zeros((UT, 128), jnp.float32) if j == 0 else acc[rows, :]
            pulled = jnp.zeros((UT, 128), jnp.float32) if j == 0 else pull[rows, :]
            for c in range(n_item // CT):
                cand = items[pl.ds(j * n_item + c * CT, CT), :]
                e = jnp.exp2(nt(u, cand) * LOG2_SCALE)
                for lane in range(CT // 128):
                    total += e[:, lane * 128 : (lane + 1) * 128]
                pulled += jnp.dot(
                    e.astype(jnp.bfloat16), cand, preferred_element_type=jnp.float32
                )
            acc[rows, :] = total
            pull[rows, :] = pulled
            return carry

        lax.fori_loop(low, high, step, 0)

    per = n_user // UT
    pass_one(0, 0, per)
    for i in (3, 1, 2):
        user_copies[i].wait_recv()
    pass_one(0, per, side * per)
    for j in (3, 1, 2):
        item_copies[j].wait_recv()
        pass_one(j, 0, side * per)

    for s in range(side):
        sums = acc[pl.ds(s * n_user, n_user), :]
        tot[pl.ds(s, 1), :] = jnp.sum(sums.T, axis=0, keepdims=True)
    total_copies = [push(TOTALS, "dp_0", k, tot, tot_in.at[k - 1]) for k in (1, 3, 2)]
    pull_copies = [
        push(PULLED, "dp_0", k, pull.at[pl.ds(k * n_user, n_user)], pull_in.at[k - 1])
        for k in (1, 3, 2)
    ]
    for copy in total_copies:
        copy.wait_recv()
    for s in range(side):
        whole = tot[pl.ds(s, 1), :]
        for k in range(1, side):
            whole += tot_in[k - 1, pl.ds((s + k) % side, 1), :]
        if s == 0:
            totals_ref[...] = whole
        lz[pl.ds(s, 1), :] = jnp.log2(whole)

    def pass_two(j):
        def step(n, carry):
            rows = pl.ds(pl.multiple_of(n * IT, IT), IT)
            cand = items[pl.ds(pl.multiple_of(j * n_item + n * IT, IT), IT), :]
            sums = jnp.zeros((IT, 128), jnp.float32)
            for s in range(side):
                u = users[pl.ds(s * n_user, n_user), :]
                p = jnp.exp2(nt(cand, u) * LOG2_SCALE - lz[pl.ds(s, 1), :])
                sums += jnp.dot(p.astype(jnp.bfloat16), u, preferred_element_type=jnp.float32)
            part[j, rows, :] = sums
            return carry

        lax.fori_loop(0, n_item // IT, step, 0)

    sum_copies = []
    for j in (2, 1, 3):
        pass_two(j)
        sum_copies.append(push(ITEM_SUMS, "dp_1", j, part.at[j], part_in.at[j - 1]))
    pass_two(0)
    for copy in pull_copies:
        copy.wait_recv()
    pulled_ref[...] = pull[pl.ds(0, n_user), :] + pull_in[0] + pull_in[1] + pull_in[2]
    for copy in sum_copies:
        copy.wait_recv()
    isum_ref[...] = part[0] + part_in[0] + part_in[1] + part_in[2]
    for copy in [
        *user_copies.values(),
        *item_copies.values(),
        *total_copies,
        *pull_copies,
        *sum_copies,
    ]:
        copy.wait_send()


def group_scores(user_bf, item_bf):
    n_user, width = user_bf.shape
    n_item = item_bf.shape[0]
    f32, bf16 = jnp.float32, jnp.bfloat16
    vmem = pl.BlockSpec(memory_space=pltpu.VMEM)
    return pl.pallas_call(
        score_kernel,
        out_shape=(
            jax.ShapeDtypeStruct((n_user, width), f32),
            jax.ShapeDtypeStruct((1, n_user), f32),
            jax.ShapeDtypeStruct((n_item, width), f32),
        ),
        in_specs=[vmem] * 2,
        out_specs=(vmem,) * 3,
        scratch_shapes=[
            pltpu.VMEM((4 * n_user, width), bf16),
            pltpu.VMEM((4 * n_item, width), bf16),
            pltpu.VMEM((4 * n_user, width), f32),
            pltpu.VMEM((4 * n_user, width), f32),
            pltpu.VMEM((3, n_user, width), f32),
            pltpu.VMEM((4, n_user), f32),
            pltpu.VMEM((3, 4, n_user), f32),
            pltpu.VMEM((4, n_user), f32),
            pltpu.VMEM((4, n_item, width), f32),
            pltpu.VMEM((3, n_item, width), f32),
            pltpu.SemaphoreType.DMA((5, 3)),
            pltpu.SemaphoreType.DMA((5, 3)),
        ],
        compiler_params=pltpu.CompilerParams(
            collective_id=0, has_side_effects=True, vmem_limit_bytes=40 * 2**20
        ),
        name="group_scores",
    )(user_bf, item_bf)


ST = 256


def slot_kernel(slots_ref, grads_ref, out_ref, pieces):
    step = pl.program_id(0)

    @pl.when(step == 0)
    def _():
        grads = grads_ref[...]
        high = grads.astype(jnp.bfloat16)
        pieces[:, 0:128] = high
        pieces[:, 128:256] = (grads - high.astype(jnp.float32)).astype(jnp.bfloat16)

    wanted = slots_ref[...] - step * ST
    mine = lax.broadcasted_iota(jnp.int32, (ST, wanted.shape[1]), 0) == wanted
    picks = jnp.where(mine, 1.0, 0.0).astype(jnp.bfloat16)
    both = jnp.dot(picks, pieces[...], preferred_element_type=jnp.float32)
    out_ref[...] = (both[:, 0:128] + both[:, 128:256]).astype(out_ref.dtype)


def slot_sums(slot_index, look_grads, n_slots):
    n_look, width = look_grads.shape
    return pl.pallas_call(
        slot_kernel,
        out_shape=jax.ShapeDtypeStruct((n_slots, width), jnp.bfloat16),
        grid=(n_slots // ST,),
        in_specs=[
            pl.BlockSpec((1, n_look), lambda i: (0, 0)),
            pl.BlockSpec((n_look, width), lambda i: (0, 0)),
        ],
        out_specs=pl.BlockSpec((ST, width), lambda i: (i, 0)),
        scratch_shapes=[pltpu.VMEM((n_look, 2 * width), jnp.bfloat16)],
        compiler_params=pltpu.CompilerParams(vmem_limit_bytes=32 * 2**20),
        name="slot_sums",
    )(slot_index.reshape(1, n_look), look_grads)


GROUPS = 4
RT = 256


def update_kernel(row_ref, column_ref, grads_ref, table_ref, state_ref, out_ref, state_out, spread):
    step = pl.program_id(0)
    width = grads_ref.shape[1]
    group_rows = RT * pl.num_programs(0)

    @pl.when(step == 0)
    def _():
        grads = grads_ref[...].astype(jnp.float32)
        group = column_ref[...] // group_rows
        for g in range(GROUPS):
            spread[:, g * width : (g + 1) * width] = jnp.where(group == g, grads, 0.0).astype(
                jnp.bfloat16
            )

    wanted = lax.rem(row_ref[...], group_rows) - step * RT
    mine = lax.broadcasted_iota(jnp.int32, (RT, wanted.shape[1]), 0) == wanted
    picks = jnp.where(mine, 1.0, 0.0).astype(jnp.bfloat16)
    for g in range(GROUPS):
        total = jnp.dot(
            picks, spread[:, g * width : (g + 1) * width], preferred_element_type=jnp.float32
        )
        before = jnp.broadcast_to(state_ref[pl.ds(g, 1), :], (width, RT)).T
        after = before + jnp.sum(total * total, axis=1, keepdims=True) * (1.0 / width)
        out_ref[g] = table_ref[g] - learn_rate * total / (jnp.sqrt(after) + epsilon)
        state_out[pl.ds(g, 1), :] = after.T[0:1, :]


def table_update(rows, grads, table, state):
    n, width = grads.shape
    n_rows = table.shape[0]
    group_rows = n_rows // GROUPS
    new_table, new_state = pl.pallas_call(
        update_kernel,
        out_shape=(
            jax.ShapeDtypeStruct((GROUPS, group_rows, width), jnp.float32),
            jax.ShapeDtypeStruct((GROUPS, group_rows), jnp.float32),
        ),
        grid=(group_rows // RT,),
        in_specs=[
            pl.BlockSpec((1, n), lambda i: (0, 0)),
            pl.BlockSpec((n, 1), lambda i: (0, 0)),
            pl.BlockSpec((n, width), lambda i: (0, 0)),
            pl.BlockSpec((GROUPS, RT, width), lambda i: (0, i, 0)),
            pl.BlockSpec((GROUPS, RT), lambda i: (0, i)),
        ],
        out_specs=(
            pl.BlockSpec((GROUPS, RT, width), lambda i: (0, i, 0)),
            pl.BlockSpec((GROUPS, RT), lambda i: (0, i)),
        ),
        scratch_shapes=[pltpu.VMEM((n, GROUPS * width), jnp.bfloat16)],
        compiler_params=pltpu.CompilerParams(vmem_limit_bytes=40 * 2**20),
        name="table_update",
    )(
        rows.reshape(1, n),
        rows.reshape(n, 1),
        grads,
        table.reshape(GROUPS, group_rows, width),
        state.reshape(GROUPS, group_rows),
    )
    return new_table.reshape(n_rows, width), new_state.reshape(n_rows)


def per_device(
    id_table, ada_state, user_first, user_second, item_first, item_second, fetch_rows, lookup_slots
):
    width = id_table.shape[1]
    asked_rows = one_exchange(fetch_rows[0], DP_SHARD, (DP, SHARD), (0, 1), (0, 1))
    flat_rows = asked_rows.reshape(-1)
    fetched = jnp.take(id_table, flat_rows, axis=0, mode="clip").reshape(
        asked_rows.shape + (width,)
    )
    returned = one_exchange(fetched, DP_SHARD, (DP, SHARD), (0, 1), (0, 1))
    slot_rows = returned.reshape(-1, width)
    slot_index = lookup_slots[0]
    looked = jnp.take(slot_rows, slot_index, axis=0, mode="clip")
    user_vec, user_pull = jax.vjp(tower_pass, looked[:EXAMPLES], user_first, user_second)
    item_vec, item_pull = jax.vjp(tower_pass, looked[EXAMPLES:], item_first, item_second)
    user_bf = user_vec.astype(jnp.bfloat16)
    item_bf = item_vec.astype(jnp.bfloat16)
    user_f32 = user_bf.astype(jnp.float32)
    positive = item_bf[:EXAMPLES].astype(jnp.float32)
    pos_score = jnp.sum(user_f32 * positive, axis=1) / logit_divisor
    pulled, totals, item_sum = group_scores(user_bf, item_bf)
    totals = totals.reshape(-1)
    user_cot = (pulled / totals[:, None] - positive) / logit_divisor
    item_cot = item_sum.at[:EXAMPLES].add(-user_f32) / logit_divisor
    user_look, user_first_g, user_second_g = user_pull(user_cot)
    item_look, item_first_g, item_second_g = item_pull(item_cot)
    look_grads = jnp.concatenate([user_look, item_look], axis=0)
    slot_grads = slot_sums(slot_index, look_grads, slot_rows.shape[0])
    sent_back = one_exchange(
        slot_grads.reshape(returned.shape), DP_SHARD, (DP, SHARD), (0, 1), (0, 1)
    ).reshape(-1, width)
    new_table, new_state = table_update(flat_rows, sent_back, id_table, ada_state)
    loss_part = jnp.sum(jnp.log(totals) - pos_score)
    summed = lax.psum(
        (user_first_g, user_second_g, item_first_g, item_second_g, loss_part), DP_SHARD
    )
    n_dev = lax.axis_size(DP) * lax.axis_size(SHARD)
    return (
        new_table,
        new_state,
        summed[0] / n_dev,
        summed[1] / n_dev,
        summed[2] / n_dev,
        summed[3] / n_dev,
        summed[4] / (n_dev * EXAMPLES),
    )


def solution(mesh):
    finer = Mesh(mesh.devices.reshape(4, 4, 8, 2), DP_SHARD)
    in_specs = (
        P(DP_SHARD, None),
        P(DP_SHARD),
        P(),
        P(),
        P(),
        P(),
        P(DP_SHARD, None, None, None),
        P(DP_SHARD, None),
    )
    out_specs = (P(DP_SHARD, None), P(DP_SHARD), P(), P(), P(), P(), P())
    return jax.shard_map(
        per_device, mesh=finer, in_specs=in_specs, out_specs=out_specs, check_vma=False
    )
```

```python
import functools
import math

import jax
import jax.numpy as jnp
from jax import lax
from jax.experimental import pallas as pl
from jax.experimental.pallas import tpu as pltpu
from jax.sharding import Mesh
from jax.sharding import PartitionSpec as P

DP_SHARD = ("dp_0", "dp_1", "shard_0", "shard_1")
DP = ("dp_0", "dp_1")
SHARD = ("shard_0", "shard_1")
MESH = pl.DeviceIdType.MESH
EXAMPLES = 512

highest = lax.Precision.HIGHEST
logit_divisor = 0.025
learn_rate = 0.1
epsilon = 1e-08
LOG2_SCALE = math.log2(math.e) / logit_divisor


def tower_pass(looked, first_t, second_w):
    hidden_act = jax.nn.silu(
        lax.dot_general(
            looked,
            first_t,
            (((1,), (1,)), ((), ())),
            precision=highest,
            preferred_element_type=jnp.float32,
        )
    )
    tower_out = jnp.dot(hidden_act, second_w, precision=highest, preferred_element_type=jnp.float32)
    return tower_out / jnp.sqrt(jnp.sum(tower_out * tower_out, axis=1, keepdims=True) + 1e-06)


CHUNKS = (2, 1, 3, 0)


class Place:
    def __init__(self):
        self.x, self.y = lax.axis_index("dp_0"), lax.axis_index("dp_1")
        self.z, self.core = lax.axis_index("shard_0"), lax.axis_index("shard_1")
        self.dp = self.x * 4 + self.y
        self.shard = self.z * 2 + self.core

    def shard_peer(self, k):
        p = lax.rem(self.shard + k, 16)
        return p, {"shard_0": lax.div(p, 2), "shard_1": lax.rem(p, 2)}

    def dp_peer(self, c, m):
        px, py = lax.rem(self.x + c, 4), lax.rem(self.y + m, 4)
        return px * 4 + py, {"dp_0": px, "dp_1": py}

    def greet(self):
        barrier = pltpu.get_barrier_semaphore()
        for k in range(1, 16):
            pl.semaphore_signal(
                barrier, inc=1, device_id=self.shard_peer(k)[1], device_id_type=MESH
            )
        for k in range(1, 16):
            pl.semaphore_signal(
                barrier, inc=1, device_id=self.dp_peer(k // 4, k % 4)[1], device_id_type=MESH
            )
        pl.semaphore_wait(barrier, 30)


def remote(src, dst, send, recv, device):
    copy = pltpu.make_async_remote_copy(
        src_ref=src,
        dst_ref=dst,
        send_sem=send,
        recv_sem=recv,
        device_id=device,
        device_id_type=MESH,
    )
    copy.start()
    return copy


def to_shards(place, c, src, held, send, recv, local):
    near = pl.ds(lax.rem(place.x + c, 4) * 4, 4)
    own = pltpu.make_async_copy(src.at[near, place.shard], held.at[place.shard, near], local.at[c])
    own.start()
    copies = []
    for k in range(1, 16):
        p, device = place.shard_peer(k)
        copies.append(
            remote(
                src.at[near, p],
                held.at[place.shard, near],
                send.at[c, k],
                recv.at[c, k],
                device,
            )
        )
    return own, copies


def to_groups(place, c, held, out, send, recv, local):
    own, copies = None, []
    for m in (2, 1, 3, 0):
        d, device = place.dp_peer(c, m)
        if c == 0 and m == 0:
            own = pltpu.make_async_copy(held.at[:, d], out.at[d], local.at[4])
            own.start()
        else:
            copies.append(
                remote(
                    held.at[:, d],
                    out.at[place.dp],
                    send.at[c * 4 + m],
                    recv.at[c * 4 + m],
                    device,
                )
            )
    return own, copies


def two_steps(place, src, held, out, sems, before=None, between=()):
    send_s, recv_s, send_d, recv_d, local = sems
    firsts, sent, ends = {}, [], []
    for c in CHUNKS:
        if before is not None:
            before(c)
        firsts[c] = to_shards(place, c, src, held, send_s, recv_s, local)
    for n, c in enumerate(CHUNKS):
        own, copies = firsts[c]
        own.wait()
        for copy in copies:
            copy.wait_recv()
        sent += copies
        own, copies = to_groups(place, c, held, out, send_d, recv_d, local)
        ends += copies
        sent += copies
        if own is not None:
            last = own
        if n < len(between):
            between[n]()
    return last, ends, sent


def exchange_sems():
    dma = pltpu.SemaphoreType.DMA
    return [dma((4, 16)), dma((4, 16)), dma((16,)), dma((16,)), dma((5,))]


def fetch_kernel(
    ids_ref, table_ref, rows_ref, asked_ref, table, held_ids, wanted, fetched, held, load_sem, *sems
):
    place = Place()
    cap = rows_ref.shape[2]
    whole = pltpu.make_async_copy(table_ref, table, load_sem.at[0])
    whole.start()
    place.greet()
    last, ends, sent = two_steps(place, ids_ref, held_ids, asked_ref, sems[:5])
    last.wait()
    for copy in ends:
        copy.wait_recv()
    for copy in sent:
        copy.wait_send()
    scalars = pltpu.make_async_copy(asked_ref, wanted, load_sem.at[1])
    scalars.start()
    scalars.wait()
    whole.wait()

    def gather(c):
        first = lax.rem(place.x + c, 4) * 4

        def step(n, carry):
            d, s = first + lax.div(n, 16), lax.rem(n, 16)
            for k in range(cap):
                fetched[d, s, k] = table[wanted[d, s, 0, k]]
            return carry

        lax.fori_loop(0, 64, step, 0, unroll=2)

    last, ends, sent = two_steps(place, fetched, held, rows_ref, sems[5:], before=gather)
    last.wait()
    for copy in ends:
        copy.wait_recv()
    for copy in sent:
        copy.wait_send()


def fetch(ids, table):
    n_dp, n_shard, cap = ids.shape
    n_rows, width = table.shape
    vmem = pl.BlockSpec(memory_space=pltpu.VMEM)
    padded = jnp.pad(ids, ((0, 0), (0, 0), (0, 128 - cap))).reshape(n_dp, n_shard, 1, 128)
    rows, asked = pl.pallas_call(
        fetch_kernel,
        out_shape=(
            jax.ShapeDtypeStruct((n_dp, n_shard, cap, 1, width), jnp.float32),
            jax.ShapeDtypeStruct((n_dp, n_shard, 1, 128), jnp.int32),
        ),
        in_specs=[vmem, pl.BlockSpec(memory_space=pl.ANY)],
        out_specs=(vmem, vmem),
        scratch_shapes=[
            pltpu.VMEM((n_rows, 1, width), jnp.float32),
            pltpu.VMEM((n_shard, n_dp, 1, 128), jnp.int32),
            pltpu.SMEM((n_dp, n_shard, 1, 128), jnp.int32),
            pltpu.VMEM((n_dp, n_shard, cap, 1, width), jnp.float32),
            pltpu.VMEM((n_shard, n_dp, cap, 1, width), jnp.float32),
            pltpu.SemaphoreType.DMA((2,)),
            *exchange_sems(),
            *exchange_sems(),
        ],
        compiler_params=pltpu.CompilerParams(
            collective_id=1, has_side_effects=True, vmem_limit_bytes=40 * 2**20
        ),
        name="fetch",
    )(padded, table.reshape(n_rows, 1, width))
    return rows.reshape(-1, width), asked[:, :, 0, :cap].reshape(-1)


SIDES = (("shard_1", 2), ("dp_0", 4), ("dp_1", 4), ("shard_0", 8))


def return_kernel(
    grads_ref,
    w0,
    w1,
    w2,
    w3,
    loss_ref,
    back_ref,
    weights_ref,
    loss_out,
    held,
    mine,
    arrived,
    losses,
    wsend,
    wrecv,
    gsend,
    grecv,
    lsend,
    lrecv,
    *sems,
):
    place = Place()
    at = {"shard_1": place.core, "dp_0": place.x, "dp_1": place.y, "shard_0": place.z}
    n = sum(w.shape[0] for w in (w0, w1, w2, w3))
    row = 0
    for w in (w0, w1, w2, w3):
        mine[pl.ds(row, w.shape[0]), :] = w[...]
        row += w.shape[0]
    losses[0, pl.ds(place.core, 1)] = loss_ref[...][None]
    place.greet()

    sizes, size, low = [], n, 0
    lows = []
    for axis, side in SIDES:
        size //= side
        sizes.append(size)
        lows.append(low)
        low = low + at[axis] * size
    lows.append(low)
    shifts = [0, 1, 4, 7]
    started, scatter, gather, loss_copies = [], {}, {}, {}

    def push_sums(stage):
        axis, side = SIDES[stage]
        part = sizes[stage]
        scatter[stage], loss_copies[stage] = [], []
        for k in range(1, side):
            p = lax.rem(at[axis] + k, side)
            sem = shifts[stage] + k - 1
            start = pl.multiple_of(lows[stage] + p * part, 8)
            copy = remote(
                mine.at[pl.ds(start, part)],
                arrived.at[pl.ds(land[stage] + (k - 1) * part, part)],
                wsend.at[sem],
                wrecv.at[sem],
                {axis: p},
            )
            scatter[stage].append(copy)
            copy = remote(
                losses.at[stage, at[axis]],
                losses.at[stage, at[axis]],
                lsend.at[sem],
                lrecv.at[sem],
                {axis: p},
            )
            loss_copies[stage].append(copy)
        started.extend(scatter[stage] + loss_copies[stage])

    land, place_row = [], 0
    for (axis, side), part in zip(SIDES, sizes):
        land.append(place_row)
        place_row += (side - 1) * part

    def add_sums(stage):
        axis, side = SIDES[stage]
        part = sizes[stage]
        for copy in scatter[stage] + loss_copies[stage]:
            copy.wait_recv()
        here = pl.ds(pl.multiple_of(lows[stage + 1], 8), part)
        total = mine[here, :]
        for k in range(1, side):
            total += arrived[pl.ds(land[stage] + (k - 1) * part, part), :]
        loss = losses[stage, 0]
        for p in range(1, side):
            loss += losses[stage, p]
        if stage + 1 < len(SIDES):
            mine[here, :] = total
            losses[stage + 1, pl.ds(at[SIDES[stage + 1][0]], 1)] = loss[None]
        else:
            weights_ref[here, :] = total * (1.0 / 256)
            loss_out[...] = loss

    def push_whole(stage):
        axis, side = SIDES[stage]
        here = pl.ds(pl.multiple_of(lows[stage + 1], 8), sizes[stage])
        gather[stage] = []
        for k in range(1, side):
            sem = shifts[stage] + k - 1
            copy = remote(
                weights_ref.at[here],
                weights_ref.at[here],
                gsend.at[sem],
                grecv.at[sem],
                {axis: lax.rem(at[axis] + k, side)},
            )
            gather[stage].append(copy)
        started.extend(gather[stage])

    def wait_whole(stage):
        for copy in gather[stage]:
            copy.wait_recv()

    push_sums(0)

    def first():
        add_sums(0)
        push_sums(1)

    def second():
        add_sums(1)
        push_sums(2)

    def third():
        add_sums(2)
        push_sums(3)

    last, ends, sent = two_steps(
        place, grads_ref, held, back_ref, sems, between=(first, second, third)
    )
    add_sums(3)
    push_whole(3)
    wait_whole(3)
    push_whole(2)
    wait_whole(2)
    push_whole(1)
    wait_whole(1)
    push_whole(0)
    last.wait()
    for copy in ends:
        copy.wait_recv()
    wait_whole(0)
    for copy in sent + started:
        copy.wait_send()


def gradients_back(slot_grads, weights, loss_part):
    n_dp, n_shard, width = 16, 16, slot_grads.shape[-1]
    f32 = jnp.float32
    n = sum(w.shape[0] for w in weights)
    blocks = slot_grads.reshape(n_dp, n_shard, -1, 2, width)
    landed, size = 0, n
    for _, side in SIDES:
        size //= side
        landed += (side - 1) * size
    vmem = pl.BlockSpec(memory_space=pltpu.VMEM)
    dma = pltpu.SemaphoreType.DMA
    back, summed, loss = pl.pallas_call(
        return_kernel,
        out_shape=(
            jax.ShapeDtypeStruct(blocks.shape, blocks.dtype),
            jax.ShapeDtypeStruct((n, width), f32),
            jax.ShapeDtypeStruct((8, 128), f32),
        ),
        in_specs=[vmem] * 6,
        out_specs=(vmem,) * 3,
        scratch_shapes=[
            pltpu.VMEM(blocks.shape, blocks.dtype),
            pltpu.VMEM((n, width), f32),
            pltpu.VMEM((landed, width), f32),
            pltpu.VMEM((4, 8, 8, 128), f32),
            *[dma((14,)) for _ in range(6)],
            *exchange_sems(),
        ],
        compiler_params=pltpu.CompilerParams(
            collective_id=2, has_side_effects=True, vmem_limit_bytes=40 * 2**20
        ),
        name="gradients_back",
    )(blocks, *weights, jnp.broadcast_to(loss_part, (8, 128)))
    return back.reshape(-1, width), summed, loss[0, 0]


UT = 256
CT = 512
IT = 256

USER_GATHER, ITEM_GATHER, TOTALS, PULLED, ITEM_SUMS = range(5)


def nt(a, b):
    return lax.dot_general(a, b, (((1,), (1,)), ((), ())), preferred_element_type=jnp.float32)


def score_kernel(
    user_ref,
    item_ref,
    pulled_ref,
    totals_ref,
    isum_ref,
    users,
    items,
    acc,
    pull,
    pull_in,
    tot,
    tot_in,
    lz,
    part,
    part_in,
    send_sem,
    recv_sem,
):
    n_user = user_ref.shape[0]
    n_item = item_ref.shape[0]
    side = 4
    x = lax.axis_index("dp_0")
    y = lax.axis_index("dp_1")

    def peer(axis, k):
        if axis == "dp_0":
            return {"dp_0": lax.rem(x + k, side)}
        return {"dp_1": lax.rem(y + k, side)}

    def push(kind, axis, k, src, dst):
        copy = pltpu.make_async_remote_copy(
            src_ref=src,
            dst_ref=dst,
            send_sem=send_sem.at[kind, k - 1],
            recv_sem=recv_sem.at[kind, k - 1],
            device_id=peer(axis, k),
            device_id_type=MESH,
        )
        copy.start()
        return copy

    barrier = pltpu.get_barrier_semaphore()
    for axis in ("dp_0", "dp_1"):
        for k in range(1, side):
            pl.semaphore_signal(barrier, inc=1, device_id=peer(axis, k), device_id_type=MESH)
    pl.semaphore_wait(barrier, 2 * (side - 1))

    item_copies, user_copies = {}, {}
    for k in (1, 3, 2):
        user_copies[side - k] = push(
            USER_GATHER, "dp_0", k, user_ref, users.at[pl.ds((side - k) * n_user, n_user)]
        )
        item_copies[side - k] = push(
            ITEM_GATHER, "dp_1", k, item_ref, items.at[pl.ds((side - k) * n_item, n_item)]
        )
    users[pl.ds(0, n_user), :] = user_ref[...]
    items[pl.ds(0, n_item), :] = item_ref[...]

    def pass_one(j, low, high):
        def step(n, carry):
            rows = pl.ds(pl.multiple_of(n * UT, UT), UT)
            u = users[rows, :]
            total = jnp.zeros((UT, 128), jnp.float32) if j == 0 else acc[rows, :]
            pulled = jnp.zeros((UT, 128), jnp.float32) if j == 0 else pull[rows, :]
            for c in range(n_item // CT):
                cand = items[pl.ds(j * n_item + c * CT, CT), :]
                e = jnp.exp2(nt(u, cand) * LOG2_SCALE)
                for lane in range(CT // 128):
                    total += e[:, lane * 128 : (lane + 1) * 128]
                pulled += jnp.dot(
                    e.astype(jnp.bfloat16), cand, preferred_element_type=jnp.float32
                )
            acc[rows, :] = total
            pull[rows, :] = pulled
            return carry

        lax.fori_loop(low, high, step, 0)

    per = n_user // UT
    pass_one(0, 0, per)
    for i in (3, 1, 2):
        user_copies[i].wait_recv()
    pass_one(0, per, side * per)
    for j in (3, 1, 2):
        item_copies[j].wait_recv()
        pass_one(j, 0, side * per)

    for s in range(side):
        sums = acc[pl.ds(s * n_user, n_user), :]
        tot[pl.ds(s, 1), :] = jnp.sum(sums.T, axis=0, keepdims=True)
    total_copies = [push(TOTALS, "dp_0", k, tot, tot_in.at[k - 1]) for k in (1, 3, 2)]
    pull_copies = [
        push(PULLED, "dp_0", k, pull.at[pl.ds(k * n_user, n_user)], pull_in.at[k - 1])
        for k in (1, 3, 2)
    ]
    for copy in total_copies:
        copy.wait_recv()
    for s in range(side):
        whole = tot[pl.ds(s, 1), :]
        for k in range(1, side):
            whole += tot_in[k - 1, pl.ds((s + k) % side, 1), :]
        if s == 0:
            totals_ref[...] = whole
        lz[pl.ds(s, 1), :] = jnp.log2(whole)

    def pass_two(j):
        def step(n, carry):
            rows = pl.ds(pl.multiple_of(n * IT, IT), IT)
            cand = items[pl.ds(pl.multiple_of(j * n_item + n * IT, IT), IT), :]
            sums = jnp.zeros((IT, 128), jnp.float32)
            for s in range(side):
                u = users[pl.ds(s * n_user, n_user), :]
                p = jnp.exp2(nt(cand, u) * LOG2_SCALE - lz[pl.ds(s, 1), :])
                sums += jnp.dot(p.astype(jnp.bfloat16), u, preferred_element_type=jnp.float32)
            part[j, rows, :] = sums
            return carry

        lax.fori_loop(0, n_item // IT, step, 0)

    sum_copies = []
    for j in (2, 1, 3):
        pass_two(j)
        sum_copies.append(push(ITEM_SUMS, "dp_1", j, part.at[j], part_in.at[j - 1]))
    pass_two(0)
    for copy in pull_copies:
        copy.wait_recv()
    pulled_ref[...] = pull[pl.ds(0, n_user), :] + pull_in[0] + pull_in[1] + pull_in[2]
    for copy in sum_copies:
        copy.wait_recv()
    isum_ref[...] = part[0] + part_in[0] + part_in[1] + part_in[2]
    for copy in [
        *user_copies.values(),
        *item_copies.values(),
        *total_copies,
        *pull_copies,
        *sum_copies,
    ]:
        copy.wait_send()


def group_scores(user_bf, item_bf):
    n_user, width = user_bf.shape
    n_item = item_bf.shape[0]
    f32, bf16 = jnp.float32, jnp.bfloat16
    vmem = pl.BlockSpec(memory_space=pltpu.VMEM)
    return pl.pallas_call(
        score_kernel,
        out_shape=(
            jax.ShapeDtypeStruct((n_user, width), f32),
            jax.ShapeDtypeStruct((1, n_user), f32),
            jax.ShapeDtypeStruct((n_item, width), f32),
        ),
        in_specs=[vmem] * 2,
        out_specs=(vmem,) * 3,
        scratch_shapes=[
            pltpu.VMEM((4 * n_user, width), bf16),
            pltpu.VMEM((4 * n_item, width), bf16),
            pltpu.VMEM((4 * n_user, width), f32),
            pltpu.VMEM((4 * n_user, width), f32),
            pltpu.VMEM((3, n_user, width), f32),
            pltpu.VMEM((4, n_user), f32),
            pltpu.VMEM((3, 4, n_user), f32),
            pltpu.VMEM((4, n_user), f32),
            pltpu.VMEM((4, n_item, width), f32),
            pltpu.VMEM((3, n_item, width), f32),
            pltpu.SemaphoreType.DMA((5, 3)),
            pltpu.SemaphoreType.DMA((5, 3)),
        ],
        compiler_params=pltpu.CompilerParams(
            collective_id=0, has_side_effects=True, vmem_limit_bytes=40 * 2**20
        ),
        name="group_scores",
    )(user_bf, item_bf)


ST = 256


def slot_kernel(slots_ref, grads_ref, out_ref, pieces):
    step = pl.program_id(0)

    @pl.when(step == 0)
    def _():
        grads = grads_ref[...]
        high = grads.astype(jnp.bfloat16)
        pieces[:, 0:128] = high
        pieces[:, 128:256] = (grads - high.astype(jnp.float32)).astype(jnp.bfloat16)

    wanted = slots_ref[...] - step * ST
    mine = lax.broadcasted_iota(jnp.int32, (ST, wanted.shape[1]), 0) == wanted
    picks = jnp.where(mine, 1.0, 0.0).astype(jnp.bfloat16)
    both = jnp.dot(picks, pieces[...], preferred_element_type=jnp.float32)
    out_ref[...] = (both[:, 0:128] + both[:, 128:256]).astype(out_ref.dtype)


def slot_sums(slot_index, look_grads, n_slots):
    n_look, width = look_grads.shape
    return pl.pallas_call(
        slot_kernel,
        out_shape=jax.ShapeDtypeStruct((n_slots, width), jnp.bfloat16),
        grid=(n_slots // ST,),
        in_specs=[
            pl.BlockSpec((1, n_look), lambda i: (0, 0)),
            pl.BlockSpec((n_look, width), lambda i: (0, 0)),
        ],
        out_specs=pl.BlockSpec((ST, width), lambda i: (i, 0)),
        scratch_shapes=[pltpu.VMEM((n_look, 2 * width), jnp.bfloat16)],
        compiler_params=pltpu.CompilerParams(vmem_limit_bytes=32 * 2**20),
        name="slot_sums",
    )(slot_index.reshape(1, n_look), look_grads)


GROUPS = 4
RT = 256


def update_kernel(row_ref, column_ref, grads_ref, table_ref, state_ref, out_ref, state_out, spread):
    step = pl.program_id(0)
    width = grads_ref.shape[1]
    group_rows = RT * pl.num_programs(0)

    @pl.when(step == 0)
    def _():
        grads = grads_ref[...].astype(jnp.float32)
        group = column_ref[...] // group_rows
        for g in range(GROUPS):
            spread[:, g * width : (g + 1) * width] = jnp.where(group == g, grads, 0.0).astype(
                jnp.bfloat16
            )

    wanted = lax.rem(row_ref[...], group_rows) - step * RT
    mine = lax.broadcasted_iota(jnp.int32, (RT, wanted.shape[1]), 0) == wanted
    picks = jnp.where(mine, 1.0, 0.0).astype(jnp.bfloat16)
    for g in range(GROUPS):
        total = jnp.dot(
            picks, spread[:, g * width : (g + 1) * width], preferred_element_type=jnp.float32
        )
        before = jnp.broadcast_to(state_ref[pl.ds(g, 1), :], (width, RT)).T
        after = before + jnp.sum(total * total, axis=1, keepdims=True) * (1.0 / width)
        out_ref[g] = table_ref[g] - learn_rate * total / (jnp.sqrt(after) + epsilon)
        state_out[pl.ds(g, 1), :] = after.T[0:1, :]


def table_update(rows, grads, table, state):
    n, width = grads.shape
    n_rows = table.shape[0]
    group_rows = n_rows // GROUPS
    new_table, new_state = pl.pallas_call(
        update_kernel,
        out_shape=(
            jax.ShapeDtypeStruct((GROUPS, group_rows, width), jnp.float32),
            jax.ShapeDtypeStruct((GROUPS, group_rows), jnp.float32),
        ),
        grid=(group_rows // RT,),
        in_specs=[
            pl.BlockSpec((1, n), lambda i: (0, 0)),
            pl.BlockSpec((n, 1), lambda i: (0, 0)),
            pl.BlockSpec((n, width), lambda i: (0, 0)),
            pl.BlockSpec((GROUPS, RT, width), lambda i: (0, i, 0)),
            pl.BlockSpec((GROUPS, RT), lambda i: (0, i)),
        ],
        out_specs=(
            pl.BlockSpec((GROUPS, RT, width), lambda i: (0, i, 0)),
            pl.BlockSpec((GROUPS, RT), lambda i: (0, i)),
        ),
        scratch_shapes=[pltpu.VMEM((n, GROUPS * width), jnp.bfloat16)],
        compiler_params=pltpu.CompilerParams(vmem_limit_bytes=40 * 2**20),
        name="table_update",
    )(
        rows.reshape(1, n),
        rows.reshape(n, 1),
        grads,
        table.reshape(GROUPS, group_rows, width),
        state.reshape(GROUPS, group_rows),
    )
    return new_table.reshape(n_rows, width), new_state.reshape(n_rows)


PITCH = 10


def per_device(
    id_table, ada_state, user_first, user_second, item_first, item_second, fetch_rows, lookup_slots
):
    cap = fetch_rows.shape[3]
    hidden = user_first.shape[1]
    slot_rows, asked = fetch(fetch_rows[0], id_table)
    slot_index = lookup_slots[0]
    looked = jnp.take(slot_rows, slot_index, axis=0, mode="clip")
    user_vec, user_pull = jax.vjp(tower_pass, looked[:EXAMPLES], user_first.T, user_second)
    item_vec, item_pull = jax.vjp(tower_pass, looked[EXAMPLES:], item_first.T, item_second)
    user_bf = user_vec.astype(jnp.bfloat16)
    item_bf = item_vec.astype(jnp.bfloat16)
    user_f32 = user_bf.astype(jnp.float32)
    positive = item_bf[:EXAMPLES].astype(jnp.float32)
    pos_score = jnp.sum(user_f32 * positive, axis=1) / logit_divisor
    pulled, totals, item_sum = group_scores(user_bf, item_bf)
    totals = totals.reshape(-1)
    user_cot = (pulled / totals[:, None] - positive) / logit_divisor
    item_cot = item_sum.at[:EXAMPLES].add(-user_f32) / logit_divisor
    user_look, user_first_g, user_second_g = user_pull(user_cot)
    item_look, item_first_g, item_second_g = item_pull(item_cot)
    look_grads = jnp.concatenate([user_look, item_look], axis=0)
    n_dev = slot_rows.shape[0] // cap
    wide_index = slot_index // cap * PITCH + slot_index % cap
    slot_grads = slot_sums(wide_index, look_grads, n_dev * PITCH)
    loss_part = jnp.sum(jnp.log(totals) - pos_score)
    sent_back, weights, loss = gradients_back(
        slot_grads, (user_first_g, user_second_g, item_first_g, item_second_g), loss_part
    )
    wide_rows = jnp.pad(
        asked.reshape(n_dev, cap), ((0, 0), (0, PITCH - cap)), constant_values=id_table.shape[0]
    ).reshape(-1)
    new_table, new_state = table_update(wide_rows, sent_back, id_table, ada_state)
    return (
        new_table,
        new_state,
        weights[:hidden].T,
        weights[hidden : 2 * hidden],
        weights[2 * hidden : 3 * hidden].T,
        weights[3 * hidden :],
        loss / (n_dev * EXAMPLES),
    )


def solution(mesh):
    finer = Mesh(mesh.devices.reshape(4, 4, 8, 2), DP_SHARD)
    in_specs = (
        P(DP_SHARD, None),
        P(DP_SHARD),
        P(),
        P(),
        P(),
        P(),
        P(DP_SHARD, None, None, None),
        P(DP_SHARD, None),
    )
    out_specs = (P(DP_SHARD, None), P(DP_SHARD), P(), P(), P(), P(), P())
    return jax.shard_map(
        per_device, mesh=finer, in_specs=in_specs, out_specs=out_specs, check_vma=False
    )
```

```python
import functools
import math

import jax
import jax.numpy as jnp
from jax import lax
from jax.experimental import pallas as pl
from jax.experimental.pallas import tpu as pltpu
from jax.sharding import Mesh
from jax.sharding import PartitionSpec as P

DP_SHARD = ("dp_0", "dp_1", "shard_0", "shard_1")
DP = ("dp_0", "dp_1")
SHARD = ("shard_0", "shard_1")
MESH = pl.DeviceIdType.MESH
EXAMPLES = 512

precise = lax.Precision.HIGH
logit_divisor = 0.025
learn_rate = 0.1
epsilon = 1e-08
LOG2_SCALE = math.log2(math.e) / logit_divisor


def tower_pass(looked, first_t, second_w):
    hidden_act = jax.nn.silu(
        lax.dot_general(
            looked,
            first_t,
            (((1,), (1,)), ((), ())),
            precision=precise,
            preferred_element_type=jnp.float32,
        )
    )
    tower_out = jnp.dot(hidden_act, second_w, precision=precise, preferred_element_type=jnp.float32)
    return tower_out / jnp.sqrt(jnp.sum(tower_out * tower_out, axis=1, keepdims=True) + 1e-06)


class Place:
    def __init__(self):
        self.x, self.y = lax.axis_index("dp_0"), lax.axis_index("dp_1")
        self.z, self.core = lax.axis_index("shard_0"), lax.axis_index("shard_1")
        self.dp = self.x * 4 + self.y
        self.shard = self.z * 2 + self.core
        self.dev = self.dp * 16 + self.shard

    def shard_peer(self, k):
        p = lax.rem(self.shard + k, 16)
        return p, {"shard_0": lax.div(p, 2), "shard_1": lax.rem(p, 2)}

    def dp_peer(self, k):
        px, py = lax.rem(self.x + k // 4, 4), lax.rem(self.y + k % 4, 4)
        return px * 4 + py, {"dp_0": px, "dp_1": py}

    def any_peer(self, n):
        px = lax.rem(self.x + lax.div(n, 64), 4)
        py = lax.rem(self.y + lax.rem(lax.div(n, 16), 4), 4)
        pz = lax.rem(self.z + lax.div(lax.rem(n, 16), 2), 8)
        pc = lax.rem(self.core + lax.rem(n, 2), 2)
        device = {"dp_0": px, "dp_1": py, "shard_0": pz, "shard_1": pc}
        return (px * 4 + py) * 16 + pz * 2 + pc, device

    def greet(self):
        barrier = pltpu.get_barrier_semaphore()
        for peer in (self.shard_peer, self.dp_peer):
            for k in range(1, 16):
                pl.semaphore_signal(barrier, inc=1, device_id=peer(k)[1], device_id_type=MESH)
        pl.semaphore_wait(barrier, 30)

    def pass_on(self, sem):
        for k in range(1, 16):
            pl.semaphore_signal(sem, inc=1, device_id=self.dp_peer(k)[1], device_id_type=MESH)


def remote(src, dst, send, recv, device):
    copy = pltpu.make_async_remote_copy(
        src_ref=src,
        dst_ref=dst,
        send_sem=send,
        recv_sem=recv,
        device_id=device,
        device_id_type=MESH,
    )
    copy.start()
    return copy


def wait_all(ref, sem):
    others = ref.at[pl.ds(0, ref.shape[0] - 1)]
    pltpu.make_async_copy(others, others, sem).wait()


LANES = 16


def fetch_kernel(
    ids_ref,
    table_ref,
    rows_ref,
    asked_ref,
    table,
    held,
    sorted_ids,
    wanted,
    fetched,
    load_sem,
    all_in,
    send_s,
    recv_s,
    send_d,
    recv_d,
    send_rows,
    recv_rows,
):
    place = Place()
    cap = rows_ref.shape[1]
    whole = pltpu.make_async_copy(table_ref, table, load_sem.at[0])
    whole.start()
    place.greet()
    copies = []
    for k in range(1, 16):
        p, device = place.shard_peer(k)
        copies.append(
            remote(ids_ref.at[p], held.at[place.shard], send_s.at[k], recv_s.at[k], device)
        )
    place.pass_on(all_in)
    held[pl.ds(place.shard, 1)] = ids_ref[pl.ds(place.shard, 1)]
    for copy in copies:
        copy.wait_recv()
    per = 128 // LANES
    for half in range(2):
        lines = held[:, half, :]
        for d in range(per):
            sorted_ids[half * per + d] = (
                lines if d == 0 else pltpu.roll(lines, 128 - d * LANES, axis=1)
            )
    late = []
    for k in range(1, 16):
        d, device = place.dp_peer(k)
        late.append(
            remote(
                sorted_ids.at[d], asked_ref.at[place.dp], send_d.at[k], recv_d.at[k], device
            )
        )
    asked_ref[pl.ds(place.dp, 1)] = sorted_ids[pl.ds(place.dp, 1)]
    for copy in late:
        copy.wait_recv()
    scalars = pltpu.make_async_copy(asked_ref, wanted, load_sem.at[1])
    scalars.start()
    pl.semaphore_wait(all_in, 15)
    scalars.wait()
    whole.wait()

    def step(n, carry):
        dev, device = place.any_peer(n)
        d, s = lax.div(dev, 16), lax.rem(dev, 16)
        for k in range(cap):
            fetched[dev, k] = table[wanted[d, s, k]]
        remote(
            fetched.at[dev], rows_ref.at[place.dev], send_rows.at[0], recv_rows.at[0], device
        )
        return carry

    lax.fori_loop(1, 256, step, 0, unroll=3)
    for k in range(cap):
        rows_ref[place.dev, k] = table[wanted[place.dp, place.shard, k]]
    for copy in copies + late:
        copy.wait_send()
    wait_all(rows_ref, recv_rows.at[0])
    wait_all(rows_ref, send_rows.at[0])


def fetch(ids, table):
    n_dp, n_shard, cap = ids.shape
    n_rows, width = table.shape
    n_dev = n_dp * n_shard
    vmem = pl.BlockSpec(memory_space=pltpu.VMEM)
    dma = pltpu.SemaphoreType.DMA
    lines = jnp.pad(ids, ((0, 0), (0, 0), (0, LANES - cap)))
    lines = jnp.swapaxes(lines, 0, 1).reshape(n_shard, n_dp * LANES // 128, 128)
    rows, asked = pl.pallas_call(
        fetch_kernel,
        out_shape=(
            jax.ShapeDtypeStruct((n_dev, cap, 1, width), jnp.float32),
            jax.ShapeDtypeStruct((n_dp, n_shard, 128), jnp.int32),
        ),
        in_specs=[vmem, pl.BlockSpec(memory_space=pltpu.HBM)],
        out_specs=(vmem, vmem),
        scratch_shapes=[
            pltpu.VMEM((n_rows, 1, width), jnp.float32),
            pltpu.VMEM(lines.shape, jnp.int32),
            pltpu.VMEM((n_dp, n_shard, 128), jnp.int32),
            pltpu.SMEM((n_dp, n_shard, 128), jnp.int32),
            pltpu.VMEM((n_dev, cap, 1, width), jnp.float32),
            dma((2,)),
            pltpu.SemaphoreType.REGULAR,
            *[dma((16,)) for _ in range(4)],
            *[dma((1,)) for _ in range(2)],
        ],
        compiler_params=pltpu.CompilerParams(
            collective_id=1, has_side_effects=True, vmem_limit_bytes=40 * 2**20
        ),
        name="fetch",
    )(lines, table.reshape(n_rows, 1, width))
    return rows.reshape(-1, width), asked[:, :, :cap].reshape(-1)


SIDES = (("shard_1", 2), ("dp_0", 4), ("dp_1", 4), ("shard_0", 8))


def return_kernel(
    grads_ref,
    w0,
    w1,
    w2,
    w3,
    loss_ref,
    back_ref,
    weights_ref,
    loss_out,
    mine,
    arrived,
    losses,
    wsend,
    wrecv,
    gsend,
    grecv,
    lsend,
    lrecv,
    all_in,
    send_rows,
    recv_rows,
):
    place = Place()
    at = {"shard_1": place.core, "dp_0": place.x, "dp_1": place.y, "shard_0": place.z}
    n = sum(w.shape[0] for w in (w0, w1, w2, w3))
    row = 0
    for w in (w0, w1, w2, w3):
        mine[pl.ds(row, w.shape[0]), :] = w[...]
        row += w.shape[0]
    losses[0, pl.ds(place.core, 1)] = loss_ref[...][None]
    place.greet()

    sizes, size, low = [], n, 0
    lows = []
    for axis, side in SIDES:
        size //= side
        sizes.append(size)
        lows.append(low)
        low = low + at[axis] * size
    lows.append(low)
    shifts = [0, 1, 4, 7]
    started, scatter, gather, loss_copies = [], {}, {}, {}

    def push_sums(stage):
        axis, side = SIDES[stage]
        part = sizes[stage]
        scatter[stage], loss_copies[stage] = [], []
        for k in range(1, side):
            p = lax.rem(at[axis] + k, side)
            sem = shifts[stage] + k - 1
            start = pl.multiple_of(lows[stage] + p * part, 8)
            copy = remote(
                mine.at[pl.ds(start, part)],
                arrived.at[pl.ds(land[stage] + (k - 1) * part, part)],
                wsend.at[sem],
                wrecv.at[sem],
                {axis: p},
            )
            scatter[stage].append(copy)
            copy = remote(
                losses.at[stage, at[axis]],
                losses.at[stage, at[axis]],
                lsend.at[sem],
                lrecv.at[sem],
                {axis: p},
            )
            loss_copies[stage].append(copy)
        started.extend(scatter[stage] + loss_copies[stage])

    land, place_row = [], 0
    for (axis, side), part in zip(SIDES, sizes):
        land.append(place_row)
        place_row += (side - 1) * part

    def add_sums(stage):
        axis, side = SIDES[stage]
        part = sizes[stage]
        for copy in scatter[stage] + loss_copies[stage]:
            copy.wait_recv()
        here = pl.ds(pl.multiple_of(lows[stage + 1], 8), part)
        total = mine[here, :]
        for k in range(1, side):
            total += arrived[pl.ds(land[stage] + (k - 1) * part, part), :]
        loss = losses[stage, 0]
        for p in range(1, side):
            loss += losses[stage, p]
        if stage + 1 < len(SIDES):
            mine[here, :] = total
            losses[stage + 1, pl.ds(at[SIDES[stage + 1][0]], 1)] = loss[None]
        else:
            weights_ref[here, :] = total * (1.0 / 256)
            loss_out[...] = loss

    def push_whole(stage):
        axis, side = SIDES[stage]
        here = pl.ds(pl.multiple_of(lows[stage + 1], 8), sizes[stage])
        gather[stage] = []
        for k in range(1, side):
            sem = shifts[stage] + k - 1
            copy = remote(
                weights_ref.at[here],
                weights_ref.at[here],
                gsend.at[sem],
                grecv.at[sem],
                {axis: lax.rem(at[axis] + k, side)},
            )
            gather[stage].append(copy)
        started.extend(gather[stage])

    def wait_whole(stage):
        for copy in gather[stage]:
            copy.wait_recv()

    def send_rows_of(part):
        def step(n, carry):
            dev, device = place.any_peer(n)
            remote(
                grads_ref.at[dev], back_ref.at[place.dev], send_rows.at[0], recv_rows.at[0], device
            )
            return carry

        lax.fori_loop(1 + part * 51, 52 + part * 51, step, 0, unroll=3)

    push_sums(0)
    place.pass_on(all_in)
    back_ref[pl.ds(place.dev, 1)] = grads_ref[pl.ds(place.dev, 1)]
    pl.semaphore_wait(all_in, 15)
    for stage in range(4):
        send_rows_of(stage)
        add_sums(stage)
        if stage < 3:
            push_sums(stage + 1)
    push_whole(3)
    send_rows_of(4)
    for stage in (3, 2, 1):
        wait_whole(stage)
        push_whole(stage - 1)
    for copy in started:
        copy.wait_send()
    wait_all(back_ref, recv_rows.at[0])
    wait_all(back_ref, send_rows.at[0])
    wait_whole(0)


def gradients_back(slot_grads, weights, loss_part):
    n_dev, width = 256, slot_grads.shape[-1]
    f32 = jnp.float32
    n = sum(w.shape[0] for w in weights)
    blocks = slot_grads.reshape(n_dev, -1, 2, width)
    landed, size = 0, n
    for _, side in SIDES:
        size //= side
        landed += (side - 1) * size
    vmem = pl.BlockSpec(memory_space=pltpu.VMEM)
    dma = pltpu.SemaphoreType.DMA
    back, summed, loss = pl.pallas_call(
        return_kernel,
        out_shape=(
            jax.ShapeDtypeStruct(blocks.shape, blocks.dtype),
            jax.ShapeDtypeStruct((n, width), f32),
            jax.ShapeDtypeStruct((8, 128), f32),
        ),
        in_specs=[vmem] * 6,
        out_specs=(vmem,) * 3,
        scratch_shapes=[
            pltpu.VMEM((n, width), f32),
            pltpu.VMEM((landed, width), f32),
            pltpu.VMEM((4, 8, 8, 128), f32),
            *[dma((14,)) for _ in range(6)],
            pltpu.SemaphoreType.REGULAR,
            *[dma((1,)) for _ in range(2)],
        ],
        compiler_params=pltpu.CompilerParams(
            collective_id=2, has_side_effects=True, vmem_limit_bytes=40 * 2**20
        ),
        name="gradients_back",
    )(blocks, *weights, jnp.broadcast_to(loss_part, (8, 128)))
    return back.reshape(-1, width), summed, loss[0, 0]


UT = 1024
CT = 256
IT = 1024

USER_GATHER, ITEM_GATHER, TOTALS, PULLED, ITEM_SUMS = range(5)


def nt(a, b):
    return lax.dot_general(a, b, (((1,), (1,)), ((), ())), preferred_element_type=jnp.float32)


def score_kernel(
    user_ref,
    item_ref,
    pulled_ref,
    totals_ref,
    isum_ref,
    users,
    items,
    acc,
    pull,
    pull_in,
    tot,
    tot_in,
    lz,
    part,
    part_in,
    send_sem,
    recv_sem,
):
    n_user = user_ref.shape[0]
    n_item = item_ref.shape[0]
    side = 4
    x = lax.axis_index("dp_0")
    y = lax.axis_index("dp_1")

    def peer(axis, k):
        if axis == "dp_0":
            return {"dp_0": lax.rem(x + k, side)}
        return {"dp_1": lax.rem(y + k, side)}

    def push(kind, axis, k, src, dst):
        copy = pltpu.make_async_remote_copy(
            src_ref=src,
            dst_ref=dst,
            send_sem=send_sem.at[kind, k - 1],
            recv_sem=recv_sem.at[kind, k - 1],
            device_id=peer(axis, k),
            device_id_type=MESH,
        )
        copy.start()
        return copy

    barrier = pltpu.get_barrier_semaphore()
    for axis in ("dp_0", "dp_1"):
        for k in range(1, side):
            pl.semaphore_signal(barrier, inc=1, device_id=peer(axis, k), device_id_type=MESH)
    pl.semaphore_wait(barrier, 2 * (side - 1))

    item_copies, user_copies = {}, {}
    for k in (1, 3, 2):
        user_copies[side - k] = push(
            USER_GATHER, "dp_0", k, user_ref, users.at[pl.ds((side - k) * n_user, n_user)]
        )
        item_copies[side - k] = push(
            ITEM_GATHER, "dp_1", k, item_ref, items.at[pl.ds((side - k) * n_item, n_item)]
        )
    users[pl.ds(0, n_user), :] = user_ref[...]
    items[pl.ds(0, n_item), :] = item_ref[...]

    def pass_one(j, low, high):
        def step(n, carry):
            rows = pl.ds(pl.multiple_of(n * UT, UT), UT)
            u = users[rows, :]
            total = jnp.zeros((UT, 128), jnp.float32) if j == 0 else acc[rows, :]
            pulled = jnp.zeros((UT, 128), jnp.float32) if j == 0 else pull[rows, :]
            for c in range(n_item // CT):
                cand = items[pl.ds(j * n_item + c * CT, CT), :]
                e = jnp.exp2(nt(u, cand) * LOG2_SCALE)
                for lane in range(CT // 128):
                    total += e[:, lane * 128 : (lane + 1) * 128]
                pulled += jnp.dot(
                    e.astype(jnp.bfloat16), cand, preferred_element_type=jnp.float32
                )
            acc[rows, :] = total
            pull[rows, :] = pulled
            return carry

        lax.fori_loop(low, high, step, 0)

    steps = side * n_user // UT
    for i in (3, 1, 2):
        user_copies[i].wait_recv()
    pass_one(0, 0, steps)
    for j in (3, 1, 2):
        item_copies[j].wait_recv()
        pass_one(j, 0, steps)

    for s in range(side):
        sums = acc[pl.ds(s * n_user, n_user), :]
        tot[pl.ds(s, 1), :] = jnp.sum(sums.T, axis=0, keepdims=True)
    total_copies = [push(TOTALS, "dp_0", k, tot, tot_in.at[k - 1]) for k in (1, 3, 2)]
    pull_copies = [
        push(PULLED, "dp_0", k, pull.at[pl.ds(k * n_user, n_user)], pull_in.at[k - 1])
        for k in (1, 3, 2)
    ]
    for copy in total_copies:
        copy.wait_recv()
    for s in range(side):
        whole = tot[pl.ds(s, 1), :]
        for k in range(1, side):
            whole += tot_in[k - 1, pl.ds((s + k) % side, 1), :]
        if s == 0:
            totals_ref[...] = whole
        lz[pl.ds(s, 1), :] = jnp.log2(whole)

    def pass_two(j):
        def step(n, carry):
            rows = pl.ds(pl.multiple_of(n * IT, IT), IT)
            cand = items[pl.ds(pl.multiple_of(j * n_item + n * IT, IT), IT), :]
            sums = jnp.zeros((IT, 128), jnp.float32)
            for s in range(side):
                u = users[pl.ds(s * n_user, n_user), :]
                p = jnp.exp2(nt(cand, u) * LOG2_SCALE - lz[pl.ds(s, 1), :])
                sums += jnp.dot(p.astype(jnp.bfloat16), u, preferred_element_type=jnp.float32)
            if j == 0:
                isum_ref[rows, :] = sums
            else:
                part[j - 1, rows, :] = sums.astype(jnp.bfloat16)
            return carry

        lax.fori_loop(0, n_item // IT, step, 0)

    sum_copies = []
    for j in (2, 1, 3):
        pass_two(j)
        sum_copies.append(push(ITEM_SUMS, "dp_1", j, part.at[j - 1], part_in.at[j - 1]))
    pass_two(0)
    for copy in pull_copies:
        copy.wait_recv()
    pulled_ref[...] = pull[pl.ds(0, n_user), :] + pull_in[0] + pull_in[1] + pull_in[2]
    for copy in sum_copies:
        copy.wait_recv()
    isum_ref[...] += (
        part_in[0].astype(jnp.float32)
        + part_in[1].astype(jnp.float32)
        + part_in[2].astype(jnp.float32)
    )
    for copy in [
        *user_copies.values(),
        *item_copies.values(),
        *total_copies,
        *pull_copies,
        *sum_copies,
    ]:
        copy.wait_send()


def group_scores(user_bf, item_bf):
    n_user, width = user_bf.shape
    n_item = item_bf.shape[0]
    f32, bf16 = jnp.float32, jnp.bfloat16
    vmem = pl.BlockSpec(memory_space=pltpu.VMEM)
    return pl.pallas_call(
        score_kernel,
        out_shape=(
            jax.ShapeDtypeStruct((n_user, width), f32),
            jax.ShapeDtypeStruct((1, n_user), f32),
            jax.ShapeDtypeStruct((n_item, width), f32),
        ),
        in_specs=[vmem] * 2,
        out_specs=(vmem,) * 3,
        scratch_shapes=[
            pltpu.VMEM((4 * n_user, width), bf16),
            pltpu.VMEM((4 * n_item, width), bf16),
            pltpu.VMEM((4 * n_user, width), f32),
            pltpu.VMEM((4 * n_user, width), f32),
            pltpu.VMEM((3, n_user, width), f32),
            pltpu.VMEM((4, n_user), f32),
            pltpu.VMEM((3, 4, n_user), f32),
            pltpu.VMEM((4, n_user), f32),
            pltpu.VMEM((3, n_item, width), bf16),
            pltpu.VMEM((3, n_item, width), bf16),
            pltpu.SemaphoreType.DMA((5, 3)),
            pltpu.SemaphoreType.DMA((5, 3)),
        ],
        compiler_params=pltpu.CompilerParams(
            collective_id=0, has_side_effects=True, vmem_limit_bytes=40 * 2**20
        ),
        name="group_scores",
    )(user_bf, item_bf)


ST = 256


def slot_kernel(slots_ref, grads_ref, out_ref, pieces):
    step = pl.program_id(0)

    @pl.when(step == 0)
    def _():
        grads = grads_ref[...]
        high = grads.astype(jnp.bfloat16)
        pieces[:, 0:128] = high
        pieces[:, 128:256] = (grads - high.astype(jnp.float32)).astype(jnp.bfloat16)

    wanted = slots_ref[...] - step * ST
    mine = lax.broadcasted_iota(jnp.int32, (ST, wanted.shape[1]), 0) == wanted
    picks = jnp.where(mine, 1.0, 0.0).astype(jnp.bfloat16)
    both = jnp.dot(picks, pieces[...], preferred_element_type=jnp.float32)
    out_ref[...] = (both[:, 0:128] + both[:, 128:256]).astype(out_ref.dtype)


def slot_sums(slot_index, look_grads, n_slots):
    n_look, width = look_grads.shape
    return pl.pallas_call(
        slot_kernel,
        out_shape=jax.ShapeDtypeStruct((n_slots, width), jnp.bfloat16),
        grid=(n_slots // ST,),
        in_specs=[
            pl.BlockSpec((1, n_look), lambda i: (0, 0)),
            pl.BlockSpec((n_look, width), lambda i: (0, 0)),
        ],
        out_specs=pl.BlockSpec((ST, width), lambda i: (i, 0)),
        scratch_shapes=[pltpu.VMEM((n_look, 2 * width), jnp.bfloat16)],
        compiler_params=pltpu.CompilerParams(vmem_limit_bytes=32 * 2**20),
        name="slot_sums",
    )(slot_index.reshape(1, n_look), look_grads)


GROUPS = 4
RT = 1024


def update_kernel(row_ref, column_ref, grads_ref, table_ref, state_ref, out_ref, state_out, spread):
    step = pl.program_id(0)
    width = grads_ref.shape[1]
    group_rows = RT * pl.num_programs(0)

    @pl.when(step == 0)
    def _():
        grads = grads_ref[...].astype(jnp.float32)
        group = column_ref[...] // group_rows
        for g in range(GROUPS):
            spread[:, g * width : (g + 1) * width] = jnp.where(group == g, grads, 0.0).astype(
                jnp.bfloat16
            )

    wanted = lax.rem(row_ref[...], group_rows) - step * RT
    mine = lax.broadcasted_iota(jnp.int32, (RT, wanted.shape[1]), 0) == wanted
    picks = jnp.where(mine, 1.0, 0.0).astype(jnp.bfloat16)
    every = jnp.dot(picks, spread[...], preferred_element_type=jnp.float32)
    for g in range(GROUPS):
        total = every[:, g * width : (g + 1) * width]
        before = jnp.broadcast_to(state_ref[pl.ds(g, 1), :], (width, RT)).T
        after = before + jnp.sum(total * total, axis=1, keepdims=True) * (1.0 / width)
        out_ref[g] = table_ref[g] - learn_rate * total / (jnp.sqrt(after) + epsilon)
        state_out[pl.ds(g, 1), :] = after.T[0:1, :]


def table_update(rows, grads, table, state):
    n, width = grads.shape
    n_rows = table.shape[0]
    group_rows = n_rows // GROUPS
    new_table, new_state = pl.pallas_call(
        update_kernel,
        out_shape=(
            jax.ShapeDtypeStruct((GROUPS, group_rows, width), jnp.float32),
            jax.ShapeDtypeStruct((GROUPS, group_rows), jnp.float32),
        ),
        grid=(group_rows // RT,),
        in_specs=[
            pl.BlockSpec((1, n), lambda i: (0, 0)),
            pl.BlockSpec((n, 1), lambda i: (0, 0)),
            pl.BlockSpec((n, width), lambda i: (0, 0)),
            pl.BlockSpec((GROUPS, RT, width), lambda i: (0, i, 0)),
            pl.BlockSpec((GROUPS, RT), lambda i: (0, i)),
        ],
        out_specs=(
            pl.BlockSpec((GROUPS, RT, width), lambda i: (0, i, 0)),
            pl.BlockSpec((GROUPS, RT), lambda i: (0, i)),
        ),
        scratch_shapes=[pltpu.VMEM((n, GROUPS * width), jnp.bfloat16)],
        compiler_params=pltpu.CompilerParams(vmem_limit_bytes=40 * 2**20),
        name="table_update",
    )(
        rows.reshape(1, n),
        rows.reshape(n, 1),
        grads,
        table.reshape(GROUPS, group_rows, width),
        state.reshape(GROUPS, group_rows),
    )
    return new_table.reshape(n_rows, width), new_state.reshape(n_rows)


PITCH = 10


def per_device(
    id_table, ada_state, user_first, user_second, item_first, item_second, fetch_rows, lookup_slots
):
    cap = fetch_rows.shape[3]
    hidden = user_first.shape[1]
    slot_rows, asked = fetch(fetch_rows[0], id_table)
    slot_index = lookup_slots[0]
    looked = jnp.take(slot_rows, slot_index, axis=0, mode="clip")
    user_vec, user_pull = jax.vjp(tower_pass, looked[:EXAMPLES], user_first.T, user_second)
    item_vec, item_pull = jax.vjp(tower_pass, looked[EXAMPLES:], item_first.T, item_second)
    user_bf = user_vec.astype(jnp.bfloat16)
    item_bf = item_vec.astype(jnp.bfloat16)
    user_f32 = user_bf.astype(jnp.float32)
    positive = item_bf[:EXAMPLES].astype(jnp.float32)
    pos_score = jnp.sum(user_f32 * positive, axis=1) / logit_divisor
    pulled, totals, item_sum = group_scores(user_bf, item_bf)
    totals = totals.reshape(-1)
    user_cot = (pulled / totals[:, None] - positive) / logit_divisor
    item_cot = item_sum.at[:EXAMPLES].add(-user_f32) / logit_divisor
    user_look, user_first_g, user_second_g = user_pull(user_cot)
    item_look, item_first_g, item_second_g = item_pull(item_cot)
    look_grads = jnp.concatenate([user_look, item_look], axis=0)
    n_dev = slot_rows.shape[0] // cap
    wide_index = slot_index // cap * PITCH + slot_index % cap
    slot_grads = slot_sums(wide_index, look_grads, n_dev * PITCH)
    loss_part = jnp.sum(jnp.log(totals) - pos_score)
    sent_back, weights, loss = gradients_back(
        slot_grads, (user_first_g, user_second_g, item_first_g, item_second_g), loss_part
    )
    wide_rows = jnp.pad(
        asked.reshape(n_dev, cap), ((0, 0), (0, PITCH - cap)), constant_values=id_table.shape[0]
    ).reshape(-1)
    new_table, new_state = table_update(wide_rows, sent_back, id_table, ada_state)
    return (
        new_table,
        new_state,
        weights[:hidden].T,
        weights[hidden : 2 * hidden],
        weights[2 * hidden : 3 * hidden].T,
        weights[3 * hidden :],
        loss / (n_dev * EXAMPLES),
    )


def solution(mesh):
    finer = Mesh(mesh.devices.reshape(4, 4, 8, 2), DP_SHARD)
    in_specs = (
        P(DP_SHARD, None),
        P(DP_SHARD),
        P(),
        P(),
        P(),
        P(),
        P(DP_SHARD, None, None, None),
        P(DP_SHARD, None),
    )
    out_specs = (P(DP_SHARD, None), P(DP_SHARD), P(), P(), P(), P(), P())
    return jax.shard_map(
        per_device, mesh=finer, in_specs=in_specs, out_specs=out_specs, check_vma=False
    )
```

```python
import functools
import math

import jax
import jax.numpy as jnp
from jax import lax
from jax.experimental import pallas as pl
from jax.experimental.pallas import tpu as pltpu
from jax.sharding import Mesh
from jax.sharding import PartitionSpec as P

DP_SHARD = ("dp_0", "dp_1", "shard_0", "shard_1")
DP = ("dp_0", "dp_1")
SHARD = ("shard_0", "shard_1")
MESH = pl.DeviceIdType.MESH
EXAMPLES = 512

precise = lax.Precision.HIGH
logit_divisor = 0.025
learn_rate = 0.1
epsilon = 1e-08
LOG2_SCALE = math.log2(math.e) / logit_divisor


def tower_pass(looked, first_t, second_w):
    hidden_act = jax.nn.silu(
        lax.dot_general(
            looked,
            first_t,
            (((1,), (1,)), ((), ())),
            precision=precise,
            preferred_element_type=jnp.float32,
        )
    )
    tower_out = jnp.dot(hidden_act, second_w, precision=precise, preferred_element_type=jnp.float32)
    return tower_out / jnp.sqrt(jnp.sum(tower_out * tower_out, axis=1, keepdims=True) + 1e-06)


class Place:
    def __init__(self):
        self.x, self.y = lax.axis_index("dp_0"), lax.axis_index("dp_1")
        self.z, self.core = lax.axis_index("shard_0"), lax.axis_index("shard_1")
        self.dp = self.x * 4 + self.y
        self.shard = self.z * 2 + self.core
        self.dev = self.dp * 16 + self.shard

    def shard_peer(self, k):
        p = lax.rem(self.shard + k, 16)
        return p, {"shard_0": lax.div(p, 2), "shard_1": lax.rem(p, 2)}

    def dp_peer(self, k):
        px, py = lax.rem(self.x + k // 4, 4), lax.rem(self.y + k % 4, 4)
        return px * 4 + py, {"dp_0": px, "dp_1": py}

    def any_peer(self, n):
        px = lax.rem(self.x + lax.div(n, 64), 4)
        py = lax.rem(self.y + lax.rem(lax.div(n, 16), 4), 4)
        pz = lax.rem(self.z + lax.div(lax.rem(n, 16), 2), 8)
        pc = lax.rem(self.core + lax.rem(n, 2), 2)
        device = {"dp_0": px, "dp_1": py, "shard_0": pz, "shard_1": pc}
        return (px * 4 + py) * 16 + pz * 2 + pc, device

    def greet(self, meanwhile=lambda: None):
        barrier = pltpu.get_barrier_semaphore()
        for peer in (self.shard_peer, self.dp_peer):
            for k in range(1, 16):
                pl.semaphore_signal(barrier, inc=1, device_id=peer(k)[1], device_id_type=MESH)
        meanwhile()
        pl.semaphore_wait(barrier, 30)

    def pass_on(self, sem):
        for k in range(1, 16):
            pl.semaphore_signal(sem, inc=1, device_id=self.dp_peer(k)[1], device_id_type=MESH)


def remote(src, dst, send, recv, device):
    copy = pltpu.make_async_remote_copy(
        src_ref=src,
        dst_ref=dst,
        send_sem=send,
        recv_sem=recv,
        device_id=device,
        device_id_type=MESH,
    )
    copy.start()
    return copy


def wait_all(ref, sem):
    others = ref.at[pl.ds(0, ref.shape[0] - 1)]
    pltpu.make_async_copy(others, others, sem).wait()


LANES = 16


def fetch_kernel(
    ids_ref,
    table_ref,
    rows_ref,
    asked_ref,
    table,
    held,
    sorted_ids,
    arrived,
    wanted,
    fetched,
    load_sem,
    all_in,
    send_s,
    recv_s,
    send_d,
    recv_d,
    send_rows,
    recv_rows,
):
    place = Place()
    cap = rows_ref.shape[1]
    whole = pltpu.make_async_copy(table_ref, table, load_sem.at[0])
    whole.start()
    place.greet()
    copies = []
    for k in range(1, 16):
        p, device = place.shard_peer(k)
        copies.append(
            remote(ids_ref.at[p], held.at[place.shard], send_s.at[k], recv_s.at[k], device)
        )
    place.pass_on(all_in)
    held[pl.ds(place.shard, 1)] = ids_ref[pl.ds(place.shard, 1)]
    for copy in copies:
        copy.wait_recv()
    per = 128 // LANES
    for half in range(2):
        lines = held[:, half, :]
        for d in range(per):
            sorted_ids[half * per + d] = (
                lines if d == 0 else pltpu.roll(lines, 128 - d * LANES, axis=1)
            )
    late = []
    for k in range(1, 16):
        d, device = place.dp_peer(k)
        late.append(
            remote(
                sorted_ids.at[d], arrived.at[place.dp], send_d.at[k], recv_d.at[k], device
            )
        )
    arrived[pl.ds(place.dp, 1)] = sorted_ids[pl.ds(place.dp, 1)]
    for copy in late:
        copy.wait_recv()
    n_dp = sorted_ids.shape[0]
    field = lax.broadcasted_iota(jnp.int32, (n_dp, 128), 1) // LANES
    for half in range(2):
        lines = arrived[:, half * per, :]
        for q in range(1, per):
            line = pltpu.roll(arrived[:, half * per + q, :], q * LANES, axis=1)
            lines = jnp.where(field == q, line, lines)
        asked_ref[half] = lines
    scalars = pltpu.make_async_copy(asked_ref, wanted, load_sem.at[1])
    scalars.start()
    pl.semaphore_wait(all_in, 15)
    scalars.wait()
    whole.wait()

    def asked_at(dev):
        s = lax.rem(dev, 16)
        return lax.div(s, per), lax.div(dev, 16), lax.rem(s, per) * LANES

    def step(n, carry):
        dev, device = place.any_peer(n)
        half, d, low = asked_at(dev)
        for k in range(cap):
            fetched[dev, k] = table[wanted[half, d, low + k]]
        remote(
            fetched.at[dev], rows_ref.at[place.dev], send_rows.at[0], recv_rows.at[0], device
        )
        return carry

    lax.fori_loop(1, 256, step, 0, unroll=3)
    half, d, low = asked_at(place.dev)
    for k in range(cap):
        rows_ref[place.dev, k] = table[wanted[half, d, low + k]]
    for copy in copies + late:
        copy.wait_send()
    wait_all(rows_ref, recv_rows.at[0])
    wait_all(rows_ref, send_rows.at[0])


def fetch(ids, table):
    n_dp, n_shard, cap = ids.shape
    n_rows, width = table.shape
    n_dev = n_dp * n_shard
    vmem = pl.BlockSpec(memory_space=pltpu.VMEM)
    dma = pltpu.SemaphoreType.DMA
    lines = jnp.pad(ids, ((0, 0), (0, 0), (0, LANES - cap)), constant_values=n_rows)
    lines = jnp.swapaxes(lines, 0, 1).reshape(n_shard, n_dp * LANES // 128, 128)
    rows, asked = pl.pallas_call(
        fetch_kernel,
        out_shape=(
            jax.ShapeDtypeStruct((n_dev, cap, 1, width), jnp.float32),
            jax.ShapeDtypeStruct((2, n_dp, 128), jnp.int32),
        ),
        in_specs=[vmem, pl.BlockSpec(memory_space=pltpu.HBM)],
        out_specs=(vmem, vmem),
        scratch_shapes=[
            pltpu.VMEM((n_rows, 1, width), jnp.float32),
            pltpu.VMEM(lines.shape, jnp.int32),
            pltpu.VMEM((n_dp, n_shard, 128), jnp.int32),
            pltpu.VMEM((n_dp, n_shard, 128), jnp.int32),
            pltpu.SMEM((2, n_dp, 128), jnp.int32),
            pltpu.VMEM((n_dev, cap, 1, width), jnp.float32),
            dma((2,)),
            pltpu.SemaphoreType.REGULAR,
            *[dma((16,)) for _ in range(4)],
            *[dma((1,)) for _ in range(2)],
        ],
        compiler_params=pltpu.CompilerParams(
            collective_id=1, has_side_effects=True, vmem_limit_bytes=60 * 2**20
        ),
        name="fetch",
    )(lines, table.reshape(n_rows, 1, width))
    asked = jnp.swapaxes(asked, 0, 1).reshape(n_dev, LANES)
    return rows.reshape(-1, width), asked


PITCH = 10
GROUPS = 4
RT = 1024


def stages_of(place):
    def core_peer(k):
        p = lax.rem(place.core + k, 2)
        return p, {"shard_1": p}

    def z_peer(k):
        p = lax.rem(place.z + k, 8)
        return p, {"shard_0": p}

    return (place.core, 2, core_peer), (place.dp, 16, place.dp_peer), (place.z, 8, z_peer)


def tail_kernel(
    slots_ref,
    grads_ref,
    w0,
    w1,
    w2,
    w3,
    loss_ref,
    row_ref,
    column_ref,
    state_ref,
    delta_ref,
    state_out,
    weights_ref,
    loss_out,
    pieces,
    leaving,
    back,
    spread,
    mine,
    arrived,
    losses,
    wsend,
    wrecv,
    gsend,
    grecv,
    lsend,
    lrecv,
    all_in,
    send_rows,
    recv_rows,
):
    place = Place()
    width = grads_ref.shape[1]
    stages = stages_of(place)
    n = sum(w.shape[0] for w in (w0, w1, w2, w3))

    def prepare():
        row = 0
        for w in (w0, w1, w2, w3):
            mine[pl.ds(row, w.shape[0]), :] = w[...]
            row += w.shape[0]
        losses[0, pl.ds(place.core, 1)] = loss_ref[...][None]
        grads = grads_ref[...]
        high = grads.astype(jnp.bfloat16)
        pieces[:, 0:width] = high
        pieces[:, width : 2 * width] = (grads - high.astype(jnp.float32)).astype(jnp.bfloat16)

    place.greet(prepare)

    sizes, lows, lands, shifts = [], [0], [], []
    size, landed, shift = n, 0, 0
    for at, side, _ in stages:
        size //= side
        sizes.append(size)
        lows.append(lows[-1] + at * size)
        lands.append(landed)
        shifts.append(shift)
        landed += (side - 1) * size
        shift += side - 1
    started, scatter, gather = [], {}, {}

    def push_sums(stage):
        at, side, peer = stages[stage]
        part = sizes[stage]
        scatter[stage] = []
        for k in range(1, side):
            p, device = peer(k)
            sem = shifts[stage] + k - 1
            start = pl.multiple_of(lows[stage] + p * part, 8)
            scatter[stage].append(
                remote(
                    mine.at[pl.ds(start, part)],
                    arrived.at[pl.ds(lands[stage] + (k - 1) * part, part)],
                    wsend.at[sem],
                    wrecv.at[sem],
                    device,
                )
            )
            scatter[stage].append(
                remote(
                    losses.at[stage, at],
                    losses.at[stage, at],
                    lsend.at[sem],
                    lrecv.at[sem],
                    device,
                )
            )
        started.extend(scatter[stage])

    def add_sums(stage):
        at, side, _ = stages[stage]
        part = sizes[stage]
        for copy in scatter[stage]:
            copy.wait_recv()
        here = pl.ds(pl.multiple_of(lows[stage + 1], 8), part)
        total = mine[here, :]
        for k in range(1, side):
            total += arrived[pl.ds(lands[stage] + (k - 1) * part, part), :]
        loss = losses[stage, 0]
        for p in range(1, side):
            loss += losses[stage, p]
        if stage + 1 < len(stages):
            mine[here, :] = total
            losses[stage + 1, pl.ds(stages[stage + 1][0], 1)] = loss[None]
        else:
            weights_ref[here, :] = total * (1.0 / 256)
            loss_out[...] = loss

    def push_whole(stage):
        at, side, peer = stages[stage]
        here = pl.ds(pl.multiple_of(lows[stage + 1], 8), sizes[stage])
        gather[stage] = []
        for k in range(1, side):
            sem = shifts[stage] + k - 1
            gather[stage].append(
                remote(
                    weights_ref.at[here], weights_ref.at[here], gsend.at[sem], grecv.at[sem], peer(k)[1]
                )
            )
        started.extend(gather[stage])

    def wait_whole(stage):
        for copy in gather[stage]:
            copy.wait_recv()

    def slot_tile(c):
        first = lax.rem(place.x + c, 4) * 64
        wanted = slots_ref[...] - first * PITCH
        shape = (64 * PITCH, wanted.shape[1])
        picks = jnp.where(lax.broadcasted_iota(jnp.int32, shape, 0) == wanted, 1.0, 0.0)
        both = jnp.dot(
            picks.astype(jnp.bfloat16), pieces[...], preferred_element_type=jnp.float32
        )
        total = (both[:, 0:width] + both[:, width : 2 * width]).astype(jnp.bfloat16)
        leaving[pl.ds(first, 64)] = total.reshape(64, PITCH // 2, 2, width)

    def send_tile(c):
        def step(k, carry):
            dev, device = place.any_peer(k)
            remote(leaving.at[dev], back.at[place.dev], send_rows.at[0], recv_rows.at[0], device)
            return carry

        low = 64 * c + (1 if c == 0 else 0)
        lax.fori_loop(low, 64 * (c + 1), step, 0, unroll=3 if c == 0 else 4)

    group_rows = delta_ref.shape[0] // GROUPS

    def pick_rows(step):
        wanted = lax.rem(row_ref[...], group_rows) - step * RT
        shape = (RT, wanted.shape[1])
        picks = jnp.where(lax.broadcasted_iota(jnp.int32, shape, 0) == wanted, 1.0, 0.0)
        return picks.astype(jnp.bfloat16)

    def spread_out():
        grads = back[...].reshape(-1, width).astype(jnp.float32)
        group = column_ref[...] // group_rows
        for g in range(GROUPS):
            spread[:, g * width : (g + 1) * width] = jnp.where(group == g, grads, 0.0).astype(
                jnp.bfloat16
            )

    def update(step):
        every = jnp.dot(pick_rows(step), spread[...], preferred_element_type=jnp.float32)
        lanes = pl.ds(step * RT, RT)
        for g in range(GROUPS):
            total = every[:, g * width : (g + 1) * width]
            before = jnp.broadcast_to(state_ref[pl.ds(g, 1), lanes], (width, RT)).T
            after = before + jnp.sum(total * total, axis=1, keepdims=True) * (1.0 / width)
            delta_ref[pl.ds(g * group_rows + step * RT, RT), :] = (
                learn_rate * total / (jnp.sqrt(after) + epsilon)
            )
            state_out[pl.ds(g, 1), lanes] = after.T[0:1, :]

    push_sums(0)
    place.pass_on(all_in)
    slot_tile(0)
    back[pl.ds(place.dev, 1)] = leaving[pl.ds(place.dev, 1)]
    pl.semaphore_wait(all_in, 15)
    send_tile(0)
    add_sums(0)
    push_sums(1)
    for c in (1, 2, 3):
        slot_tile(c)
        send_tile(c)
    add_sums(1)
    push_sums(2)
    add_sums(2)
    push_whole(2)
    wait_whole(2)
    push_whole(1)
    wait_all(back, recv_rows.at[0])
    spread_out()
    steps = group_rows // RT
    for step in range(steps - 1):
        update(step)
    wait_whole(1)
    push_whole(0)
    update(steps - 1)
    for copy in started:
        copy.wait_send()
    wait_all(back, send_rows.at[0])
    wait_whole(0)


def tail(slot_index, look_grads, weights, loss_part, asked, state):
    n_look, width = look_grads.shape
    n_dev = asked.shape[0]
    n_rows = state.shape[0]
    n = sum(w.shape[0] for w in weights)
    f32, bf16 = jnp.float32, jnp.bfloat16
    rows = asked[:, :PITCH].reshape(-1)
    vmem = pl.BlockSpec(memory_space=pltpu.VMEM)
    dma = pltpu.SemaphoreType.DMA
    blocks = (n_dev, PITCH // 2, 2, width)
    delta, new_state, summed, loss = pl.pallas_call(
        tail_kernel,
        out_shape=(
            jax.ShapeDtypeStruct((n_rows, width), f32),
            jax.ShapeDtypeStruct((GROUPS, n_rows // GROUPS), f32),
            jax.ShapeDtypeStruct((n, width), f32),
            jax.ShapeDtypeStruct((8, 128), f32),
        ),
        in_specs=[vmem] * 10,
        out_specs=(vmem,) * 4,
        scratch_shapes=[
            pltpu.VMEM((n_look, 2 * width), bf16),
            pltpu.VMEM(blocks, bf16),
            pltpu.VMEM(blocks, bf16),
            pltpu.VMEM((n_dev * PITCH, GROUPS * width), bf16),
            pltpu.VMEM((n, width), f32),
            pltpu.VMEM((n, width), f32),
            pltpu.VMEM((3, 16, 8, 128), f32),
            *[dma((23,)) for _ in range(6)],
            pltpu.SemaphoreType.REGULAR,
            *[dma((1,)) for _ in range(2)],
        ],
        compiler_params=pltpu.CompilerParams(
            collective_id=2, has_side_effects=True, vmem_limit_bytes=56 * 2**20
        ),
        name="tail",
    )(
        slot_index.reshape(1, n_look),
        look_grads,
        *weights,
        jnp.broadcast_to(loss_part, (8, 128)),
        rows.reshape(1, -1),
        rows.reshape(-1, 1),
        state.reshape(GROUPS, -1),
    )
    return delta, new_state.reshape(n_rows), summed, loss[0, 0]


UT = 1024
CT = 256
IT = 1024

USER_GATHER, ITEM_GATHER, TOTALS, PULLED, ITEM_SUMS = range(5)


def nt(a, b):
    return lax.dot_general(a, b, (((1,), (1,)), ((), ())), preferred_element_type=jnp.float32)


def score_kernel(
    user_ref,
    item_ref,
    pulled_ref,
    totals_ref,
    isum_ref,
    users,
    items,
    acc,
    pull,
    pull_in,
    tot,
    tot_in,
    lz,
    part,
    part_in,
    send_sem,
    recv_sem,
):
    n_user = user_ref.shape[0]
    n_item = item_ref.shape[0]
    side = 4
    x = lax.axis_index("dp_0")
    y = lax.axis_index("dp_1")

    def peer(axis, k):
        if axis == "dp_0":
            return {"dp_0": lax.rem(x + k, side)}
        return {"dp_1": lax.rem(y + k, side)}

    def push(kind, axis, k, src, dst):
        copy = pltpu.make_async_remote_copy(
            src_ref=src,
            dst_ref=dst,
            send_sem=send_sem.at[kind, k - 1],
            recv_sem=recv_sem.at[kind, k - 1],
            device_id=peer(axis, k),
            device_id_type=MESH,
        )
        copy.start()
        return copy

    barrier = pltpu.get_barrier_semaphore()
    for axis in ("dp_0", "dp_1"):
        for k in range(1, side):
            pl.semaphore_signal(barrier, inc=1, device_id=peer(axis, k), device_id_type=MESH)
    pl.semaphore_wait(barrier, 2 * (side - 1))

    item_copies, user_copies = {}, {}
    for k in (1, 3, 2):
        user_copies[side - k] = push(
            USER_GATHER, "dp_0", k, user_ref, users.at[pl.ds((side - k) * n_user, n_user)]
        )
        item_copies[side - k] = push(
            ITEM_GATHER, "dp_1", k, item_ref, items.at[pl.ds((side - k) * n_item, n_item)]
        )
    users[pl.ds(0, n_user), :] = user_ref[...]
    items[pl.ds(0, n_item), :] = item_ref[...]

    def pass_one(j, low, high):
        def step(n, carry):
            rows = pl.ds(pl.multiple_of(n * UT, UT), UT)
            u = users[rows, :]
            total = jnp.zeros((UT, 128), jnp.float32) if j == 0 else acc[rows, :]
            pulled = jnp.zeros((UT, 128), jnp.float32) if j == 0 else pull[rows, :]
            for c in range(n_item // CT):
                cand = items[pl.ds(j * n_item + c * CT, CT), :]
                e = jnp.exp2(nt(u, cand) * LOG2_SCALE)
                for lane in range(CT // 128):
                    total += e[:, lane * 128 : (lane + 1) * 128]
                pulled += jnp.dot(
                    e.astype(jnp.bfloat16), cand, preferred_element_type=jnp.float32
                )
            acc[rows, :] = total
            pull[rows, :] = pulled
            return carry

        lax.fori_loop(low, high, step, 0)

    steps = side * n_user // UT
    for i in (3, 1, 2):
        user_copies[i].wait_recv()
    pass_one(0, 0, steps)
    for j in (3, 1, 2):
        item_copies[j].wait_recv()
        pass_one(j, 0, steps)

    for s in range(side):
        sums = acc[pl.ds(s * n_user, n_user), :]
        tot[pl.ds(s, 1), :] = jnp.sum(sums.T, axis=0, keepdims=True)
    total_copies = [push(TOTALS, "dp_0", k, tot, tot_in.at[k - 1]) for k in (1, 3, 2)]
    pull_copies = [
        push(PULLED, "dp_0", k, pull.at[pl.ds(k * n_user, n_user)], pull_in.at[k - 1])
        for k in (1, 3, 2)
    ]
    for copy in total_copies:
        copy.wait_recv()
    for s in range(side):
        whole = tot[pl.ds(s, 1), :]
        for k in range(1, side):
            whole += tot_in[k - 1, pl.ds((s + k) % side, 1), :]
        if s == 0:
            totals_ref[...] = whole
        lz[pl.ds(s, 1), :] = jnp.log2(whole)

    def pass_two(j):
        def step(n, carry):
            rows = pl.ds(pl.multiple_of(n * IT, IT), IT)
            cand = items[pl.ds(pl.multiple_of(j * n_item + n * IT, IT), IT), :]
            sums = jnp.zeros((IT, 128), jnp.float32)
            for s in range(side):
                u = users[pl.ds(s * n_user, n_user), :]
                p = jnp.exp2(nt(cand, u) * LOG2_SCALE - lz[pl.ds(s, 1), :])
                sums += jnp.dot(p.astype(jnp.bfloat16), u, preferred_element_type=jnp.float32)
            if j == 0:
                isum_ref[rows, :] = sums
            else:
                part[j - 1, rows, :] = sums.astype(jnp.bfloat16)
            return carry

        lax.fori_loop(0, n_item // IT, step, 0)

    sum_copies = []
    for j in (2, 1, 3):
        pass_two(j)
        sum_copies.append(push(ITEM_SUMS, "dp_1", j, part.at[j - 1], part_in.at[j - 1]))
    pass_two(0)
    for copy in pull_copies:
        copy.wait_recv()
    pulled_ref[...] = pull[pl.ds(0, n_user), :] + pull_in[0] + pull_in[1] + pull_in[2]
    for copy in sum_copies:
        copy.wait_recv()
    isum_ref[...] += (
        part_in[0].astype(jnp.float32)
        + part_in[1].astype(jnp.float32)
        + part_in[2].astype(jnp.float32)
    )
    for copy in [
        *user_copies.values(),
        *item_copies.values(),
        *total_copies,
        *pull_copies,
        *sum_copies,
    ]:
        copy.wait_send()


def group_scores(user_bf, item_bf):
    n_user, width = user_bf.shape
    n_item = item_bf.shape[0]
    f32, bf16 = jnp.float32, jnp.bfloat16
    vmem = pl.BlockSpec(memory_space=pltpu.VMEM)
    return pl.pallas_call(
        score_kernel,
        out_shape=(
            jax.ShapeDtypeStruct((n_user, width), f32),
            jax.ShapeDtypeStruct((1, n_user), f32),
            jax.ShapeDtypeStruct((n_item, width), f32),
        ),
        in_specs=[vmem] * 2,
        out_specs=(vmem,) * 3,
        scratch_shapes=[
            pltpu.VMEM((4 * n_user, width), bf16),
            pltpu.VMEM((4 * n_item, width), bf16),
            pltpu.VMEM((4 * n_user, width), f32),
            pltpu.VMEM((4 * n_user, width), f32),
            pltpu.VMEM((3, n_user, width), f32),
            pltpu.VMEM((4, n_user), f32),
            pltpu.VMEM((3, 4, n_user), f32),
            pltpu.VMEM((4, n_user), f32),
            pltpu.VMEM((3, n_item, width), bf16),
            pltpu.VMEM((3, n_item, width), bf16),
            pltpu.SemaphoreType.DMA((5, 3)),
            pltpu.SemaphoreType.DMA((5, 3)),
        ],
        compiler_params=pltpu.CompilerParams(
            collective_id=0, has_side_effects=True, vmem_limit_bytes=40 * 2**20
        ),
        name="group_scores",
    )(user_bf, item_bf)


def per_device(
    id_table, ada_state, user_first, user_second, item_first, item_second, fetch_rows, lookup_slots
):
    cap = fetch_rows.shape[3]
    hidden = user_first.shape[1]
    slot_rows, asked = fetch(fetch_rows[0], id_table)
    slot_index = lookup_slots[0]
    looked = jnp.take(slot_rows, slot_index, axis=0, mode="clip")
    user_vec, user_pull = jax.vjp(tower_pass, looked[:EXAMPLES], user_first.T, user_second)
    item_vec, item_pull = jax.vjp(tower_pass, looked[EXAMPLES:], item_first.T, item_second)
    user_bf = user_vec.astype(jnp.bfloat16)
    item_bf = item_vec.astype(jnp.bfloat16)
    user_f32 = user_bf.astype(jnp.float32)
    positive = item_bf[:EXAMPLES].astype(jnp.float32)
    pos_score = jnp.sum(user_f32 * positive, axis=1) / logit_divisor
    pulled, totals, item_sum = group_scores(user_bf, item_bf)
    totals = totals.reshape(-1)
    user_cot = (pulled / totals[:, None] - positive) / logit_divisor
    item_cot = item_sum.at[:EXAMPLES].add(-user_f32) / logit_divisor
    user_look, user_first_g, user_second_g = user_pull(user_cot)
    item_look, item_first_g, item_second_g = item_pull(item_cot)
    look_grads = jnp.concatenate([user_look, item_look], axis=0)
    n_dev = slot_rows.shape[0] // cap
    wide_index = slot_index // cap * PITCH + slot_index % cap
    loss_part = jnp.sum(jnp.log(totals) - pos_score)
    weight_grads = (user_first_g, user_second_g, item_first_g, item_second_g)
    delta, new_state, weights, loss = tail(
        wide_index, look_grads, weight_grads, loss_part, asked, ada_state
    )
    new_table = id_table - delta
    return (
        new_table,
        new_state,
        weights[:hidden].T,
        weights[hidden : 2 * hidden],
        weights[2 * hidden : 3 * hidden].T,
        weights[3 * hidden :],
        loss / (n_dev * EXAMPLES),
    )


def solution(mesh):
    finer = Mesh(mesh.devices.reshape(4, 4, 8, 2), DP_SHARD)
    in_specs = (
        P(DP_SHARD, None),
        P(DP_SHARD),
        P(),
        P(),
        P(),
        P(),
        P(DP_SHARD, None, None, None),
        P(DP_SHARD, None),
    )
    out_specs = (P(DP_SHARD, None), P(DP_SHARD), P(), P(), P(), P(), P())
    return jax.shard_map(
        per_device, mesh=finer, in_specs=in_specs, out_specs=out_specs, check_vma=False
    )
```

```python
import functools
import math

import jax
import jax.numpy as jnp
from jax import lax
from jax.experimental import pallas as pl
from jax.experimental.pallas import tpu as pltpu
from jax.sharding import Mesh
from jax.sharding import PartitionSpec as P

DP_SHARD = ("dp_0", "dp_1", "shard_0", "shard_1")
DP = ("dp_0", "dp_1")
SHARD = ("shard_0", "shard_1")
MESH = pl.DeviceIdType.MESH
EXAMPLES = 512

logit_divisor = 0.025
learn_rate = 0.1
epsilon = 1e-08
LOG2_SCALE = math.log2(math.e) / logit_divisor


ROWS = 512
NN, NT, TN = ((1,), (0,)), ((1,), (1,)), ((0,), (0,))


def halves(x):
    high = x.astype(jnp.bfloat16)
    return high, (x - high.astype(jnp.float32)).astype(jnp.bfloat16)


def dot3(a, b, dims):
    (ah, al), (bh, bl) = a, b

    def product(x, y):
        return lax.dot_general(x, y, (dims, ((), ())), preferred_element_type=jnp.float32)

    return product(ah, bh) + (product(ah, bl) + product(al, bh))


def forward_kernel(looked_ref, uf, us, tf, ts, user_ref, item_ref, out_ref):
    weights = [(halves(uf[...]), halves(us[...])), (halves(tf[...]), halves(ts[...]))]
    for tile in range(looked_ref.shape[0] // ROWS):
        first, second = weights[min(tile, 1)]
        rows = pl.ds(tile * ROWS, ROWS)
        pre = dot3(halves(looked_ref[rows, :]), first, NN)
        z = dot3(halves(pre * lax.logistic(pre)), second, NN)
        out_ref[rows, :] = z
        vec = z / jnp.sqrt(jnp.sum(z * z, axis=1, keepdims=True) + 1e-06)
        if tile == 0:
            user_ref[...] = vec.astype(jnp.bfloat16)
        else:
            item_ref[pl.ds((tile - 1) * ROWS, ROWS), :] = vec.astype(jnp.bfloat16)


def towers_forward(looked, user_first, user_second, item_first, item_second):
    n, width = looked.shape
    vmem = pl.BlockSpec(memory_space=pltpu.VMEM)
    return pl.pallas_call(
        forward_kernel,
        out_shape=(
            jax.ShapeDtypeStruct((EXAMPLES, width), jnp.bfloat16),
            jax.ShapeDtypeStruct((n - EXAMPLES, width), jnp.bfloat16),
            jax.ShapeDtypeStruct((n, width), jnp.float32),
        ),
        in_specs=[vmem] * 5,
        out_specs=(vmem,) * 3,
        compiler_params=pltpu.CompilerParams(vmem_limit_bytes=24 * 2**20),
        name="towers_forward",
    )(looked, user_first, user_second, item_first, item_second)


def backward_kernel(
    looked_ref,
    out_ref,
    uf,
    us,
    tf,
    ts,
    user_ref,
    item_ref,
    pulled_ref,
    totals_ref,
    isum_ref,
    look_ref,
    ufg,
    usg,
    tfg,
    tsg,
    loss_ref,
):
    weights = [(halves(uf[...]), halves(us[...])), (halves(tf[...]), halves(ts[...]))]
    users = user_ref[...].astype(jnp.float32)
    positive = item_ref[pl.ds(0, EXAMPLES), :].astype(jnp.float32)
    totals = totals_ref[...]
    width = users.shape[1]
    loss = jnp.sum(jnp.log(totals)) - jnp.sum(users * positive) / logit_divisor
    loss_ref[...] = jnp.full(loss_ref.shape, 1.0, jnp.float32) * loss
    for tile in range(looked_ref.shape[0] // ROWS):
        first, second = weights[min(tile, 1)]
        rows = pl.ds(tile * ROWS, ROWS)
        if tile == 0:
            spread = jnp.broadcast_to(totals, (width, EXAMPLES)).T
            cot = pulled_ref[...] / spread - positive
        else:
            cot = isum_ref[pl.ds((tile - 1) * ROWS, ROWS), :]
            if tile == 1:
                cot = cot - users
        cot = cot / logit_divisor
        z = out_ref[rows, :]
        scale = 1.0 / jnp.sqrt(jnp.sum(z * z, axis=1, keepdims=True) + 1e-06)
        vec = z * scale
        dz = halves(scale * (cot - vec * jnp.sum(cot * vec, axis=1, keepdims=True)))
        x = halves(looked_ref[rows, :])
        pre = dot3(x, first, NN)
        gate = lax.logistic(pre)
        hidden = halves(pre * gate)
        dpre = halves(dot3(dz, second, NT) * (gate * (1.0 + pre * (1.0 - gate))))
        look_ref[rows, :] = dot3(dpre, first, NT)
        second_grad = dot3(hidden, dz, TN)
        first_grad = dot3(dpre, x, TN)
        if tile == 0:
            usg[...], ufg[...] = second_grad, first_grad
        elif tile == 1:
            tsg[...], tfg[...] = second_grad, first_grad
        else:
            tsg[...] += second_grad
            tfg[...] += first_grad


def towers_backward(looked, out, weights, user_bf, item_bf, pulled, totals, item_sum):
    n, width = looked.shape
    hidden = weights[1].shape[0]
    f32 = jnp.float32
    vmem = pl.BlockSpec(memory_space=pltpu.VMEM)
    results = pl.pallas_call(
        backward_kernel,
        out_shape=(
            jax.ShapeDtypeStruct((n, width), f32),
            *[jax.ShapeDtypeStruct((hidden, width), f32) for _ in range(4)],
            jax.ShapeDtypeStruct((8, 128), f32),
        ),
        in_specs=[vmem] * 11,
        out_specs=(vmem,) * 6,
        compiler_params=pltpu.CompilerParams(vmem_limit_bytes=32 * 2**20),
        name="towers_backward",
    )(looked, out, *weights, user_bf, item_bf, pulled, totals, item_sum)
    return results[0], results[1:5], results[5]


class Place:
    def __init__(self):
        self.x, self.y = lax.axis_index("dp_0"), lax.axis_index("dp_1")
        self.z, self.core = lax.axis_index("shard_0"), lax.axis_index("shard_1")
        self.dp = self.x * 4 + self.y
        self.shard = self.z * 2 + self.core
        self.dev = self.dp * 16 + self.shard

    def shard_peer(self, k):
        p = lax.rem(self.shard + k, 16)
        return p, {"shard_0": lax.div(p, 2), "shard_1": lax.rem(p, 2)}

    def dp_peer(self, k):
        px, py = lax.rem(self.x + k // 4, 4), lax.rem(self.y + k % 4, 4)
        return px * 4 + py, {"dp_0": px, "dp_1": py}

    def any_peer(self, n):
        px = lax.rem(self.x + lax.div(n, 64), 4)
        py = lax.rem(self.y + lax.rem(lax.div(n, 16), 4), 4)
        pz = lax.rem(self.z + lax.div(lax.rem(n, 16), 2), 8)
        pc = lax.rem(self.core + lax.rem(n, 2), 2)
        device = {"dp_0": px, "dp_1": py, "shard_0": pz, "shard_1": pc}
        return (px * 4 + py) * 16 + pz * 2 + pc, device

    def greet(self, meanwhile=lambda: None):
        barrier = pltpu.get_barrier_semaphore()
        for peer in (self.shard_peer, self.dp_peer):
            for k in range(1, 16):
                pl.semaphore_signal(barrier, inc=1, device_id=peer(k)[1], device_id_type=MESH)
        meanwhile()
        pl.semaphore_wait(barrier, 30)

    def pass_on(self, sem):
        for k in range(1, 16):
            pl.semaphore_signal(sem, inc=1, device_id=self.dp_peer(k)[1], device_id_type=MESH)


def remote(src, dst, send, recv, device):
    copy = pltpu.make_async_remote_copy(
        src_ref=src,
        dst_ref=dst,
        send_sem=send,
        recv_sem=recv,
        device_id=device,
        device_id_type=MESH,
    )
    copy.start()
    return copy


def wait_all(ref, sem):
    others = ref.at[pl.ds(0, ref.shape[0] - 1)]
    pltpu.make_async_copy(others, others, sem).wait()


LANES = 16


def fetch_kernel(
    ids_ref,
    table_ref,
    rows_ref,
    asked_ref,
    table,
    held,
    sorted_ids,
    arrived,
    wanted,
    fetched,
    load_sem,
    all_in,
    send_s,
    recv_s,
    send_d,
    recv_d,
    send_rows,
    recv_rows,
):
    place = Place()
    cap = rows_ref.shape[1]
    whole = pltpu.make_async_copy(table_ref, table, load_sem.at[0])
    whole.start()
    place.greet()
    copies = []
    for k in range(1, 16):
        p, device = place.shard_peer(k)
        copies.append(
            remote(ids_ref.at[p], held.at[place.shard], send_s.at[k], recv_s.at[k], device)
        )
    place.pass_on(all_in)
    held[pl.ds(place.shard, 1)] = ids_ref[pl.ds(place.shard, 1)]
    for copy in copies:
        copy.wait_recv()
    per = 128 // LANES
    for half in range(2):
        lines = held[:, half, :]
        for d in range(per):
            sorted_ids[half * per + d] = (
                lines if d == 0 else pltpu.roll(lines, 128 - d * LANES, axis=1)
            )
    late = []
    for k in range(1, 16):
        d, device = place.dp_peer(k)
        late.append(
            remote(
                sorted_ids.at[d], arrived.at[place.dp], send_d.at[k], recv_d.at[k], device
            )
        )
    arrived[pl.ds(place.dp, 1)] = sorted_ids[pl.ds(place.dp, 1)]
    for copy in late:
        copy.wait_recv()
    n_dp = sorted_ids.shape[0]
    field = lax.broadcasted_iota(jnp.int32, (n_dp, 128), 1) // LANES
    for half in range(2):
        lines = arrived[:, half * per, :]
        for q in range(1, per):
            line = pltpu.roll(arrived[:, half * per + q, :], q * LANES, axis=1)
            lines = jnp.where(field == q, line, lines)
        asked_ref[half] = lines
    scalars = pltpu.make_async_copy(asked_ref, wanted, load_sem.at[1])
    scalars.start()
    pl.semaphore_wait(all_in, 15)
    scalars.wait()
    whole.wait()

    def asked_at(dev):
        s = lax.rem(dev, 16)
        return lax.div(s, per), lax.div(dev, 16), lax.rem(s, per) * LANES

    def step(n, carry):
        dev, device = place.any_peer(n)
        half, d, low = asked_at(dev)
        for k in range(cap):
            fetched[dev, k] = table[wanted[half, d, low + k]]
        remote(
            fetched.at[dev], rows_ref.at[place.dev], send_rows.at[0], recv_rows.at[0], device
        )
        return carry

    lax.fori_loop(1, 256, step, 0, unroll=3)
    half, d, low = asked_at(place.dev)
    for k in range(cap):
        rows_ref[place.dev, k] = table[wanted[half, d, low + k]]
    for copy in copies + late:
        copy.wait_send()
    wait_all(rows_ref, recv_rows.at[0])
    wait_all(rows_ref, send_rows.at[0])


def fetch(ids, table):
    n_dp, n_shard, cap = ids.shape
    n_rows, width = table.shape
    n_dev = n_dp * n_shard
    vmem = pl.BlockSpec(memory_space=pltpu.VMEM)
    dma = pltpu.SemaphoreType.DMA
    lines = jnp.pad(ids, ((0, 0), (0, 0), (0, LANES - cap)), constant_values=n_rows)
    lines = jnp.swapaxes(lines, 0, 1).reshape(n_shard, n_dp * LANES // 128, 128)
    rows, asked = pl.pallas_call(
        fetch_kernel,
        out_shape=(
            jax.ShapeDtypeStruct((n_dev, cap, 1, width), jnp.float32),
            jax.ShapeDtypeStruct((2, n_dp, 128), jnp.int32),
        ),
        in_specs=[vmem, pl.BlockSpec(memory_space=pltpu.HBM)],
        out_specs=(vmem, vmem),
        scratch_shapes=[
            pltpu.VMEM((n_rows, 1, width), jnp.float32),
            pltpu.VMEM(lines.shape, jnp.int32),
            pltpu.VMEM((n_dp, n_shard, 128), jnp.int32),
            pltpu.VMEM((n_dp, n_shard, 128), jnp.int32),
            pltpu.SMEM((2, n_dp, 128), jnp.int32),
            pltpu.VMEM((n_dev, cap, 1, width), jnp.float32),
            dma((2,)),
            pltpu.SemaphoreType.REGULAR,
            *[dma((16,)) for _ in range(4)],
            *[dma((1,)) for _ in range(2)],
        ],
        compiler_params=pltpu.CompilerParams(
            collective_id=1, has_side_effects=True, vmem_limit_bytes=20 * 2**20
        ),
        name="fetch",
    )(
        lines,
        pltpu.with_memory_space_constraint(table.reshape(n_rows, 1, width), pltpu.HBM),
    )
    asked = jnp.swapaxes(asked, 0, 1).reshape(n_dev, LANES)
    return rows.reshape(-1, width), asked


PITCH = 10
GROUPS = 4
RT = 1024


def stages_of(place):
    def core_peer(k):
        p = lax.rem(place.core + k, 2)
        return p, {"shard_1": p}

    def z_peer(k):
        p = lax.rem(place.z + k, 8)
        return p, {"shard_0": p}

    return (place.core, 2, core_peer), (place.dp, 16, place.dp_peer), (place.z, 8, z_peer)


def tail_kernel(
    slots_ref,
    grads_ref,
    w0,
    w1,
    w2,
    w3,
    loss_ref,
    row_ref,
    column_ref,
    state_ref,
    delta_ref,
    state_out,
    weights_ref,
    loss_out,
    pieces,
    leaving,
    back,
    spread,
    mine,
    arrived,
    losses,
    wsend,
    wrecv,
    gsend,
    grecv,
    lsend,
    lrecv,
    all_in,
    send_rows,
    recv_rows,
):
    place = Place()
    width = grads_ref.shape[1]
    stages = stages_of(place)
    n = sum(w.shape[0] for w in (w0, w1, w2, w3))

    def prepare():
        row = 0
        for w in (w0, w1, w2, w3):
            mine[pl.ds(row, w.shape[0]), :] = w[...]
            row += w.shape[0]
        losses[0, pl.ds(place.core, 1)] = loss_ref[...][None]
        grads = grads_ref[...]
        high = grads.astype(jnp.bfloat16)
        pieces[:, 0:width] = high
        pieces[:, width : 2 * width] = (grads - high.astype(jnp.float32)).astype(jnp.bfloat16)

    place.greet(prepare)

    sizes, lows, lands, shifts = [], [0], [], []
    size, landed, shift = n, 0, 0
    for at, side, _ in stages:
        size //= side
        sizes.append(size)
        lows.append(lows[-1] + at * size)
        lands.append(landed)
        shifts.append(shift)
        landed += (side - 1) * size
        shift += side - 1
    started, scatter, gather = [], {}, {}

    def push_sums(stage):
        at, side, peer = stages[stage]
        part = sizes[stage]
        scatter[stage] = []
        for k in range(1, side):
            p, device = peer(k)
            sem = shifts[stage] + k - 1
            start = pl.multiple_of(lows[stage] + p * part, 8)
            scatter[stage].append(
                remote(
                    mine.at[pl.ds(start, part)],
                    arrived.at[pl.ds(lands[stage] + (k - 1) * part, part)],
                    wsend.at[sem],
                    wrecv.at[sem],
                    device,
                )
            )
            scatter[stage].append(
                remote(
                    losses.at[stage, at],
                    losses.at[stage, at],
                    lsend.at[sem],
                    lrecv.at[sem],
                    device,
                )
            )
        started.extend(scatter[stage])

    def add_sums(stage):
        at, side, _ = stages[stage]
        part = sizes[stage]
        for copy in scatter[stage]:
            copy.wait_recv()
        here = pl.ds(pl.multiple_of(lows[stage + 1], 8), part)
        total = mine[here, :]
        for k in range(1, side):
            total += arrived[pl.ds(lands[stage] + (k - 1) * part, part), :]
        loss = losses[stage, 0]
        for p in range(1, side):
            loss += losses[stage, p]
        if stage + 1 < len(stages):
            mine[here, :] = total
            losses[stage + 1, pl.ds(stages[stage + 1][0], 1)] = loss[None]
        else:
            weights_ref[here, :] = total * (1.0 / 256)
            loss_out[...] = loss

    def push_whole(stage):
        at, side, peer = stages[stage]
        here = pl.ds(pl.multiple_of(lows[stage + 1], 8), sizes[stage])
        gather[stage] = []
        for k in range(1, side):
            sem = shifts[stage] + k - 1
            gather[stage].append(
                remote(
                    weights_ref.at[here], weights_ref.at[here], gsend.at[sem], grecv.at[sem], peer(k)[1]
                )
            )
        started.extend(gather[stage])

    def wait_whole(stage):
        for copy in gather[stage]:
            copy.wait_recv()

    def slot_tile(c):
        first = lax.rem(place.x + c, 4) * 64
        wanted = slots_ref[...] - first * PITCH
        shape = (64 * PITCH, wanted.shape[1])
        picks = jnp.where(lax.broadcasted_iota(jnp.int32, shape, 0) == wanted, 1.0, 0.0)
        both = jnp.dot(
            picks.astype(jnp.bfloat16), pieces[...], preferred_element_type=jnp.float32
        )
        total = (both[:, 0:width] + both[:, width : 2 * width]).astype(jnp.bfloat16)
        leaving[pl.ds(first, 64)] = total.reshape(64, PITCH // 2, 2, width)

    def send_tile(c):
        def step(k, carry):
            dev, device = place.any_peer(k)
            remote(leaving.at[dev], back.at[place.dev], send_rows.at[0], recv_rows.at[0], device)
            return carry

        low = 64 * c + (1 if c == 0 else 0)
        lax.fori_loop(low, 64 * (c + 1), step, 0, unroll=3 if c == 0 else 4)

    group_rows = delta_ref.shape[0] // GROUPS

    def pick_rows(step):
        wanted = lax.rem(row_ref[...], group_rows) - step * RT
        shape = (RT, wanted.shape[1])
        picks = jnp.where(lax.broadcasted_iota(jnp.int32, shape, 0) == wanted, 1.0, 0.0)
        return picks.astype(jnp.bfloat16)

    def spread_out():
        grads = back[...].reshape(-1, width).astype(jnp.float32)
        group = column_ref[...] // group_rows
        for g in range(GROUPS):
            spread[:, g * width : (g + 1) * width] = jnp.where(group == g, grads, 0.0).astype(
                jnp.bfloat16
            )

    def update(step):
        every = jnp.dot(pick_rows(step), spread[...], preferred_element_type=jnp.float32)
        lanes = pl.ds(step * RT, RT)
        for g in range(GROUPS):
            total = every[:, g * width : (g + 1) * width]
            before = jnp.broadcast_to(state_ref[pl.ds(g, 1), lanes], (width, RT)).T
            after = before + jnp.sum(total * total, axis=1, keepdims=True) * (1.0 / width)
            delta_ref[pl.ds(g * group_rows + step * RT, RT), :] = (
                learn_rate * total / (jnp.sqrt(after) + epsilon)
            )
            state_out[pl.ds(g, 1), lanes] = after.T[0:1, :]

    push_sums(0)
    place.pass_on(all_in)
    slot_tile(0)
    back[pl.ds(place.dev, 1)] = leaving[pl.ds(place.dev, 1)]
    add_sums(0)
    push_sums(1)
    pl.semaphore_wait(all_in, 15)
    send_tile(0)
    for c in (1, 2, 3):
        slot_tile(c)
        send_tile(c)
    add_sums(1)
    push_sums(2)
    add_sums(2)
    push_whole(2)
    wait_whole(2)
    push_whole(1)
    wait_all(back, recv_rows.at[0])
    spread_out()
    steps = group_rows // RT
    for step in range(steps - 1):
        update(step)
    wait_whole(1)
    push_whole(0)
    update(steps - 1)
    for copy in started:
        copy.wait_send()
    wait_all(back, send_rows.at[0])
    wait_whole(0)


def tail(slot_index, look_grads, weights, loss_part, asked, state):
    n_look, width = look_grads.shape
    n_dev = asked.shape[0]
    n_rows = state.shape[0]
    n = sum(w.shape[0] for w in weights)
    f32, bf16 = jnp.float32, jnp.bfloat16
    rows = asked[:, :PITCH].reshape(-1)
    vmem = pl.BlockSpec(memory_space=pltpu.VMEM)
    dma = pltpu.SemaphoreType.DMA
    blocks = (n_dev, PITCH // 2, 2, width)
    delta, new_state, summed, loss = pl.pallas_call(
        tail_kernel,
        out_shape=(
            jax.ShapeDtypeStruct((n_rows, width), f32),
            jax.ShapeDtypeStruct((GROUPS, n_rows // GROUPS), f32),
            jax.ShapeDtypeStruct((n, width), f32),
            jax.ShapeDtypeStruct((8, 128), f32),
        ),
        in_specs=[vmem] * 10,
        out_specs=(vmem,) * 4,
        scratch_shapes=[
            pltpu.VMEM((n_look, 2 * width), bf16),
            pltpu.VMEM(blocks, bf16),
            pltpu.VMEM(blocks, bf16),
            pltpu.VMEM((n_dev * PITCH, GROUPS * width), bf16),
            pltpu.VMEM((n, width), f32),
            pltpu.VMEM((n, width), f32),
            pltpu.VMEM((3, 16, 8, 128), f32),
            *[dma((23,)) for _ in range(6)],
            pltpu.SemaphoreType.REGULAR,
            *[dma((1,)) for _ in range(2)],
        ],
        compiler_params=pltpu.CompilerParams(
            collective_id=2, has_side_effects=True, vmem_limit_bytes=40 * 2**20
        ),
        name="tail",
    )(
        slot_index.reshape(1, n_look),
        look_grads,
        *weights,
        loss_part,
        rows.reshape(1, -1),
        rows.reshape(-1, 1),
        state.reshape(GROUPS, -1),
    )
    return delta, new_state.reshape(n_rows), summed, loss[0, 0]


UT = 1024
CT = 256
IT = 1024

USER_GATHER, ITEM_GATHER, TOTALS, PULLED, ITEM_SUMS = range(5)


def nt(a, b):
    return lax.dot_general(a, b, (((1,), (1,)), ((), ())), preferred_element_type=jnp.float32)


def score_kernel(
    user_ref,
    item_ref,
    pulled_ref,
    totals_ref,
    isum_ref,
    users,
    items,
    acc,
    pull,
    pull_in,
    tot,
    tot_in,
    lz,
    part,
    part_in,
    send_sem,
    recv_sem,
):
    n_user = user_ref.shape[0]
    n_item = item_ref.shape[0]
    side = 4
    x = lax.axis_index("dp_0")
    y = lax.axis_index("dp_1")

    def peer(axis, k):
        if axis == "dp_0":
            return {"dp_0": lax.rem(x + k, side)}
        return {"dp_1": lax.rem(y + k, side)}

    def push(kind, axis, k, src, dst):
        copy = pltpu.make_async_remote_copy(
            src_ref=src,
            dst_ref=dst,
            send_sem=send_sem.at[kind, k - 1],
            recv_sem=recv_sem.at[kind, k - 1],
            device_id=peer(axis, k),
            device_id_type=MESH,
        )
        copy.start()
        return copy

    barrier = pltpu.get_barrier_semaphore()
    for axis in ("dp_0", "dp_1"):
        for k in range(1, side):
            pl.semaphore_signal(barrier, inc=1, device_id=peer(axis, k), device_id_type=MESH)
    pl.semaphore_wait(barrier, 2 * (side - 1))

    item_copies, user_copies = {}, {}
    for k in (1, 3, 2):
        user_copies[side - k] = push(
            USER_GATHER, "dp_0", k, user_ref, users.at[pl.ds((side - k) * n_user, n_user)]
        )
        item_copies[side - k] = push(
            ITEM_GATHER, "dp_1", k, item_ref, items.at[pl.ds((side - k) * n_item, n_item)]
        )
    users[pl.ds(0, n_user), :] = user_ref[...]
    items[pl.ds(0, n_item), :] = item_ref[...]

    def pass_one(j, low, high):
        def step(n, carry):
            rows = pl.ds(pl.multiple_of(n * UT, UT), UT)
            u = users[rows, :]
            total = jnp.zeros((UT, 128), jnp.float32) if j == 0 else acc[rows, :]
            pulled = jnp.zeros((UT, 128), jnp.float32) if j == 0 else pull[rows, :]
            for c in range(n_item // CT):
                cand = items[pl.ds(j * n_item + c * CT, CT), :]
                e = jnp.exp2(nt(u, cand) * LOG2_SCALE)
                for lane in range(CT // 128):
                    total += e[:, lane * 128 : (lane + 1) * 128]
                pulled += jnp.dot(
                    e.astype(jnp.bfloat16), cand, preferred_element_type=jnp.float32
                )
            acc[rows, :] = total
            pull[rows, :] = pulled
            return carry

        lax.fori_loop(low, high, step, 0)

    steps = side * n_user // UT
    for i in (3, 1, 2):
        user_copies[i].wait_recv()
    pass_one(0, 0, steps)
    for j in (3, 1, 2):
        item_copies[j].wait_recv()
        pass_one(j, 0, steps)

    for s in range(side):
        sums = acc[pl.ds(s * n_user, n_user), :]
        tot[pl.ds(s, 1), :] = jnp.sum(sums.T, axis=0, keepdims=True)
    total_copies = [push(TOTALS, "dp_0", k, tot, tot_in.at[k - 1]) for k in (1, 3, 2)]
    pull_copies = [
        push(PULLED, "dp_0", k, pull.at[pl.ds(k * n_user, n_user)], pull_in.at[k - 1])
        for k in (1, 3, 2)
    ]
    for copy in total_copies:
        copy.wait_recv()
    for s in range(side):
        whole = tot[pl.ds(s, 1), :]
        for k in range(1, side):
            whole += tot_in[k - 1, pl.ds((s + k) % side, 1), :]
        if s == 0:
            totals_ref[...] = whole
        lz[pl.ds(s, 1), :] = jnp.log2(whole)

    def pass_two(j):
        def step(n, carry):
            rows = pl.ds(pl.multiple_of(n * IT, IT), IT)
            cand = items[pl.ds(pl.multiple_of(j * n_item + n * IT, IT), IT), :]
            sums = jnp.zeros((IT, 128), jnp.float32)
            for s in range(side):
                u = users[pl.ds(s * n_user, n_user), :]
                p = jnp.exp2(nt(cand, u) * LOG2_SCALE - lz[pl.ds(s, 1), :])
                sums += jnp.dot(p.astype(jnp.bfloat16), u, preferred_element_type=jnp.float32)
            if j == 0:
                isum_ref[rows, :] = sums
            else:
                part[j - 1, rows, :] = sums.astype(jnp.bfloat16)
            return carry

        lax.fori_loop(0, n_item // IT, step, 0)

    sum_copies = []
    for j in (2, 1, 3):
        pass_two(j)
        sum_copies.append(push(ITEM_SUMS, "dp_1", j, part.at[j - 1], part_in.at[j - 1]))
    pass_two(0)
    for copy in pull_copies:
        copy.wait_recv()
    pulled_ref[...] = pull[pl.ds(0, n_user), :] + pull_in[0] + pull_in[1] + pull_in[2]
    for copy in sum_copies:
        copy.wait_recv()
    isum_ref[...] += (
        part_in[0].astype(jnp.float32)
        + part_in[1].astype(jnp.float32)
        + part_in[2].astype(jnp.float32)
    )
    for copy in [
        *user_copies.values(),
        *item_copies.values(),
        *total_copies,
        *pull_copies,
        *sum_copies,
    ]:
        copy.wait_send()


def group_scores(user_bf, item_bf):
    n_user, width = user_bf.shape
    n_item = item_bf.shape[0]
    f32, bf16 = jnp.float32, jnp.bfloat16
    vmem = pl.BlockSpec(memory_space=pltpu.VMEM)
    return pl.pallas_call(
        score_kernel,
        out_shape=(
            jax.ShapeDtypeStruct((n_user, width), f32),
            jax.ShapeDtypeStruct((1, n_user), f32),
            jax.ShapeDtypeStruct((n_item, width), f32),
        ),
        in_specs=[vmem] * 2,
        out_specs=(vmem,) * 3,
        scratch_shapes=[
            pltpu.VMEM((4 * n_user, width), bf16),
            pltpu.VMEM((4 * n_item, width), bf16),
            pltpu.VMEM((4 * n_user, width), f32),
            pltpu.VMEM((4 * n_user, width), f32),
            pltpu.VMEM((3, n_user, width), f32),
            pltpu.VMEM((4, n_user), f32),
            pltpu.VMEM((3, 4, n_user), f32),
            pltpu.VMEM((4, n_user), f32),
            pltpu.VMEM((3, n_item, width), bf16),
            pltpu.VMEM((3, n_item, width), bf16),
            pltpu.SemaphoreType.DMA((5, 3)),
            pltpu.SemaphoreType.DMA((5, 3)),
        ],
        compiler_params=pltpu.CompilerParams(
            collective_id=0, has_side_effects=True, vmem_limit_bytes=40 * 2**20
        ),
        name="group_scores",
    )(user_bf, item_bf)


def per_device(
    id_table, ada_state, user_first, user_second, item_first, item_second, fetch_rows, lookup_slots
):
    cap = fetch_rows.shape[3]
    hidden = user_first.shape[1]
    slot_rows, asked = fetch(fetch_rows[0], id_table)
    slot_index = lookup_slots[0]
    looked = jnp.take(slot_rows, slot_index, axis=0, mode="clip")
    towers = (user_first, user_second, item_first, item_second)
    user_bf, item_bf, out = towers_forward(looked, *towers)
    pulled, totals, item_sum = group_scores(user_bf, item_bf)
    look_grads, weight_grads, loss_part = towers_backward(
        looked, out, towers, user_bf, item_bf, pulled, totals, item_sum
    )
    n_dev = slot_rows.shape[0] // cap
    wide_index = slot_index // cap * PITCH + slot_index % cap
    delta, new_state, weights, loss = tail(
        wide_index, look_grads, weight_grads, loss_part, asked, ada_state
    )
    new_table = id_table - delta
    return (
        new_table,
        new_state,
        weights[:hidden].T,
        weights[hidden : 2 * hidden],
        weights[2 * hidden : 3 * hidden].T,
        weights[3 * hidden :],
        loss / (n_dev * EXAMPLES),
    )


def solution(mesh):
    finer = Mesh(mesh.devices.reshape(4, 4, 8, 2), DP_SHARD)
    in_specs = (
        P(DP_SHARD, None),
        P(DP_SHARD),
        P(),
        P(),
        P(),
        P(),
        P(DP_SHARD, None, None, None),
        P(DP_SHARD, None),
    )
    out_specs = (P(DP_SHARD, None), P(DP_SHARD), P(), P(), P(), P(), P())
    return jax.shard_map(
        per_device, mesh=finer, in_specs=in_specs, out_specs=out_specs, check_vma=False
    )
```

```python
import functools
import math

import jax
import jax.numpy as jnp
from jax import lax
from jax.experimental import pallas as pl
from jax.experimental.pallas import tpu as pltpu
from jax.sharding import Mesh
from jax.sharding import PartitionSpec as P

DP_SHARD = ("dp_0", "dp_1", "shard_0", "shard_1")
DP = ("dp_0", "dp_1")
SHARD = ("shard_0", "shard_1")
MESH = pl.DeviceIdType.MESH
EXAMPLES = 512

logit_divisor = 0.025
learn_rate = 0.1
epsilon = 1e-08
LOG2_SCALE = math.log2(math.e) / logit_divisor


ROWS = 512
NN, NT, TN = ((1,), (0,)), ((1,), (1,)), ((0,), (0,))


def halves(x):
    high = x.astype(jnp.bfloat16)
    return high, (x - high.astype(jnp.float32)).astype(jnp.bfloat16)


def dot3(a, b, dims):
    (ah, al), (bh, bl) = a, b

    def product(x, y):
        return lax.dot_general(x, y, (dims, ((), ())), preferred_element_type=jnp.float32)

    return product(ah, bh) + (product(ah, bl) + product(al, bh))


def fetched_weights(refs, held, sems):
    copies = [
        pltpu.make_async_copy(ref, into, sems.at[n]) for n, (ref, into) in enumerate(zip(refs, held))
    ]
    for copy in copies:
        copy.start()
    return copies


def in_hbm(arrays):
    return [pltpu.with_memory_space_constraint(a, pltpu.HBM) for a in arrays]


def forward_tile(looked, first, second):
    pre = dot3(halves(looked), first, NN)
    z = dot3(halves(pre * lax.logistic(pre)), second, NN)
    return z, z / jnp.sqrt(jnp.sum(z * z, axis=1, keepdims=True) + 1e-06)


def backward_tile(looked, z, cot, first, second):
    scale = 1.0 / jnp.sqrt(jnp.sum(z * z, axis=1, keepdims=True) + 1e-06)
    vec = z * scale
    dz = halves(scale * (cot - vec * jnp.sum(cot * vec, axis=1, keepdims=True)))
    x = halves(looked)
    pre = dot3(x, first, NN)
    gate = lax.logistic(pre)
    hidden = halves(pre * gate)
    dpre = halves(dot3(dz, second, NT) * (gate * (1.0 + pre * (1.0 - gate))))
    return dot3(dpre, first, NT), dot3(dpre, x, TN), dot3(hidden, dz, TN)


class Place:
    def __init__(self):
        self.x, self.y = lax.axis_index("dp_0"), lax.axis_index("dp_1")
        self.z, self.core = lax.axis_index("shard_0"), lax.axis_index("shard_1")
        self.dp = self.x * 4 + self.y
        self.shard = self.z * 2 + self.core
        self.dev = self.dp * 16 + self.shard

    def shard_peer(self, k):
        p = lax.rem(self.shard + k, 16)
        return p, {"shard_0": lax.div(p, 2), "shard_1": lax.rem(p, 2)}

    def dp_peer(self, k):
        px, py = lax.rem(self.x + k // 4, 4), lax.rem(self.y + k % 4, 4)
        return px * 4 + py, {"dp_0": px, "dp_1": py}

    def any_peer(self, n):
        px = lax.rem(self.x + lax.div(n, 64), 4)
        py = lax.rem(self.y + lax.rem(lax.div(n, 16), 4), 4)
        pz = lax.rem(self.z + lax.div(lax.rem(n, 16), 2), 8)
        pc = lax.rem(self.core + lax.rem(n, 2), 2)
        device = {"dp_0": px, "dp_1": py, "shard_0": pz, "shard_1": pc}
        return (px * 4 + py) * 16 + pz * 2 + pc, device

    def greet(self, meanwhile=lambda: None):
        barrier = pltpu.get_barrier_semaphore()
        for peer in (self.shard_peer, self.dp_peer):
            for k in range(1, 16):
                pl.semaphore_signal(barrier, inc=1, device_id=peer(k)[1], device_id_type=MESH)
        meanwhile()
        pl.semaphore_wait(barrier, 30)

    def pass_on(self, sem):
        for k in range(1, 16):
            pl.semaphore_signal(sem, inc=1, device_id=self.dp_peer(k)[1], device_id_type=MESH)


def remote(src, dst, send, recv, device):
    copy = pltpu.make_async_remote_copy(
        src_ref=src,
        dst_ref=dst,
        send_sem=send,
        recv_sem=recv,
        device_id=device,
        device_id_type=MESH,
    )
    copy.start()
    return copy


def wait_all(ref, sem):
    others = ref.at[pl.ds(0, ref.shape[0] - 1)]
    pltpu.make_async_copy(others, others, sem).wait()


LANES = 16


def fetch_kernel(
    ids_ref,
    table_ref,
    rows_ref,
    asked_ref,
    table,
    held,
    sorted_ids,
    arrived,
    wanted,
    fetched,
    load_sem,
    all_in,
    send_s,
    recv_s,
    send_d,
    recv_d,
    send_rows,
    recv_rows,
):
    place = Place()
    cap = rows_ref.shape[1]
    whole = pltpu.make_async_copy(table_ref, table, load_sem.at[0])
    whole.start()
    place.greet()
    copies = []
    for k in range(1, 16):
        p, device = place.shard_peer(k)
        copies.append(
            remote(ids_ref.at[p], held.at[place.shard], send_s.at[k], recv_s.at[k], device)
        )
    place.pass_on(all_in)
    held[pl.ds(place.shard, 1)] = ids_ref[pl.ds(place.shard, 1)]
    for copy in copies:
        copy.wait_recv()
    per = 128 // LANES
    for half in range(2):
        lines = held[:, half, :]
        for d in range(per):
            sorted_ids[half * per + d] = (
                lines if d == 0 else pltpu.roll(lines, 128 - d * LANES, axis=1)
            )
    late = []
    for k in range(1, 16):
        d, device = place.dp_peer(k)
        late.append(
            remote(
                sorted_ids.at[d], arrived.at[place.dp], send_d.at[k], recv_d.at[k], device
            )
        )
    arrived[pl.ds(place.dp, 1)] = sorted_ids[pl.ds(place.dp, 1)]
    for copy in late:
        copy.wait_recv()
    n_dp = sorted_ids.shape[0]
    field = lax.broadcasted_iota(jnp.int32, (n_dp, 128), 1) // LANES
    for half in range(2):
        lines = arrived[:, half * per, :]
        for q in range(1, per):
            line = pltpu.roll(arrived[:, half * per + q, :], q * LANES, axis=1)
            lines = jnp.where(field == q, line, lines)
        asked_ref[half] = lines
    scalars = pltpu.make_async_copy(asked_ref, wanted, load_sem.at[1])
    scalars.start()
    pl.semaphore_wait(all_in, 15)
    scalars.wait()
    whole.wait()

    def asked_at(dev):
        s = lax.rem(dev, 16)
        return lax.div(s, per), lax.div(dev, 16), lax.rem(s, per) * LANES

    def step(n, carry):
        dev, device = place.any_peer(n)
        half, d, low = asked_at(dev)
        for k in range(cap):
            fetched[dev, k] = table[wanted[half, d, low + k]]
        remote(
            fetched.at[dev], rows_ref.at[place.dev], send_rows.at[0], recv_rows.at[0], device
        )
        return carry

    lax.fori_loop(1, 256, step, 0, unroll=3)
    half, d, low = asked_at(place.dev)
    for k in range(cap):
        rows_ref[place.dev, k] = table[wanted[half, d, low + k]]
    for copy in copies + late:
        copy.wait_send()
    wait_all(rows_ref, recv_rows.at[0])
    wait_all(rows_ref, send_rows.at[0])


def fetch(ids, table):
    n_dp, n_shard, cap = ids.shape
    n_rows, width = table.shape
    n_dev = n_dp * n_shard
    vmem = pl.BlockSpec(memory_space=pltpu.VMEM)
    dma = pltpu.SemaphoreType.DMA
    lines = jnp.pad(ids, ((0, 0), (0, 0), (0, LANES - cap)), constant_values=n_rows)
    lines = jnp.swapaxes(lines, 0, 1).reshape(n_shard, n_dp * LANES // 128, 128)
    rows, asked = pl.pallas_call(
        fetch_kernel,
        out_shape=(
            jax.ShapeDtypeStruct((n_dev, cap, 1, width), jnp.float32),
            jax.ShapeDtypeStruct((2, n_dp, 128), jnp.int32),
        ),
        in_specs=[vmem, pl.BlockSpec(memory_space=pltpu.HBM)],
        out_specs=(vmem, vmem),
        scratch_shapes=[
            pltpu.VMEM((n_rows, 1, width), jnp.float32),
            pltpu.VMEM(lines.shape, jnp.int32),
            pltpu.VMEM((n_dp, n_shard, 128), jnp.int32),
            pltpu.VMEM((n_dp, n_shard, 128), jnp.int32),
            pltpu.SMEM((2, n_dp, 128), jnp.int32),
            pltpu.VMEM((n_dev, cap, 1, width), jnp.float32),
            dma((2,)),
            pltpu.SemaphoreType.REGULAR,
            *[dma((16,)) for _ in range(4)],
            *[dma((1,)) for _ in range(2)],
        ],
        compiler_params=pltpu.CompilerParams(
            collective_id=1, has_side_effects=True, vmem_limit_bytes=20 * 2**20
        ),
        name="fetch",
    )(
        lines,
        pltpu.with_memory_space_constraint(table.reshape(n_rows, 1, width), pltpu.HBM),
    )
    asked = jnp.swapaxes(asked, 0, 1).reshape(n_dev, LANES)
    return rows.reshape(-1, width), asked


PITCH = 10
GROUPS = 4
RT = 1024


def stages_of(place):
    def core_peer(k):
        p = lax.rem(place.core + k, 2)
        return p, {"shard_1": p}

    def z_peer(k):
        p = lax.rem(place.z + k, 8)
        return p, {"shard_0": p}

    return (place.core, 2, core_peer), (place.dp, 16, place.dp_peer), (place.z, 8, z_peer)


def tail_kernel(
    slots_ref,
    looked_ref,
    out_ref,
    user_ref,
    item_ref,
    pulled_ref,
    totals_ref,
    isum_ref,
    uf,
    us,
    tf,
    ts,
    row_ref,
    column_ref,
    state_ref,
    delta_ref,
    state_out,
    weights_ref,
    loss_out,
    uf_held,
    us_held,
    tf_held,
    ts_held,
    load_sem,
    pieces,
    leaving,
    back,
    spread,
    mine,
    arrived,
    losses,
    wsend,
    wrecv,
    gsend,
    grecv,
    lsend,
    lrecv,
    all_in,
    send_rows,
    recv_rows,
):
    place = Place()
    width = looked_ref.shape[1]
    stages = stages_of(place)
    hidden = us_held.shape[0]
    n = 4 * hidden
    held = (uf_held, us_held, tf_held, ts_held)
    loads = fetched_weights((uf, us, tf, ts), held, load_sem)

    def prepare():
        users = user_ref[...].astype(jnp.float32)
        positive = item_ref[pl.ds(0, EXAMPLES), :].astype(jnp.float32)
        totals = totals_ref[...]
        loss = jnp.sum(jnp.log(totals)) - jnp.sum(users * positive) / logit_divisor
        losses[0, pl.ds(place.core, 1)] = jnp.full((1, 8, 128), 1.0, jnp.float32) * loss
        for copy in loads:
            copy.wait()
        weights = [(halves(a[...]), halves(b[...])) for a, b in (held[:2], held[2:])]
        for tile in range(looked_ref.shape[0] // ROWS):
            rows = pl.ds(tile * ROWS, ROWS)
            if tile == 0:
                cot = pulled_ref[...] / jnp.broadcast_to(totals, (width, EXAMPLES)).T - positive
            else:
                cot = isum_ref[pl.ds((tile - 1) * ROWS, ROWS), :]
                if tile == 1:
                    cot = cot - users
            look, first_grad, second_grad = backward_tile(
                looked_ref[rows, :], out_ref[rows, :], cot / logit_divisor, *weights[min(tile, 1)]
            )
            high, low = halves(look)
            pieces[rows, 0:width] = high
            pieces[rows, width : 2 * width] = low
            at = pl.ds(min(tile, 1) * 2 * hidden, hidden)
            after = pl.ds((min(tile, 1) * 2 + 1) * hidden, hidden)
            if tile < 2:
                mine[at, :] = first_grad
                mine[after, :] = second_grad
            else:
                mine[at, :] += first_grad
                mine[after, :] += second_grad

    place.greet(prepare)

    sizes, lows, lands, shifts = [], [0], [], []
    size, landed, shift = n, 0, 0
    for at, side, _ in stages:
        size //= side
        sizes.append(size)
        lows.append(lows[-1] + at * size)
        lands.append(landed)
        shifts.append(shift)
        landed += (side - 1) * size
        shift += side - 1
    started, scatter, gather = [], {}, {}

    def push_sums(stage):
        at, side, peer = stages[stage]
        part = sizes[stage]
        scatter[stage] = []
        for k in range(1, side):
            p, device = peer(k)
            sem = shifts[stage] + k - 1
            start = pl.multiple_of(lows[stage] + p * part, 8)
            scatter[stage].append(
                remote(
                    mine.at[pl.ds(start, part)],
                    arrived.at[pl.ds(lands[stage] + (k - 1) * part, part)],
                    wsend.at[sem],
                    wrecv.at[sem],
                    device,
                )
            )
            scatter[stage].append(
                remote(
                    losses.at[stage, at],
                    losses.at[stage, at],
                    lsend.at[sem],
                    lrecv.at[sem],
                    device,
                )
            )
        started.extend(scatter[stage])

    def add_sums(stage):
        at, side, _ = stages[stage]
        part = sizes[stage]
        for copy in scatter[stage]:
            copy.wait_recv()
        here = pl.ds(pl.multiple_of(lows[stage + 1], 8), part)
        total = mine[here, :]
        for k in range(1, side):
            total += arrived[pl.ds(lands[stage] + (k - 1) * part, part), :]
        loss = losses[stage, 0]
        for p in range(1, side):
            loss += losses[stage, p]
        if stage + 1 < len(stages):
            mine[here, :] = total
            losses[stage + 1, pl.ds(stages[stage + 1][0], 1)] = loss[None]
        else:
            weights_ref[here, :] = total * (1.0 / 256)
            loss_out[...] = loss

    def push_whole(stage):
        at, side, peer = stages[stage]
        here = pl.ds(pl.multiple_of(lows[stage + 1], 8), sizes[stage])
        gather[stage] = []
        for k in range(1, side):
            sem = shifts[stage] + k - 1
            gather[stage].append(
                remote(
                    weights_ref.at[here], weights_ref.at[here], gsend.at[sem], grecv.at[sem], peer(k)[1]
                )
            )
        started.extend(gather[stage])

    def wait_whole(stage):
        for copy in gather[stage]:
            copy.wait_recv()

    def slot_tile(c):
        first = lax.rem(place.x + c, 4) * 64
        wanted = slots_ref[...] - first * PITCH
        shape = (64 * PITCH, wanted.shape[1])
        picks = jnp.where(lax.broadcasted_iota(jnp.int32, shape, 0) == wanted, 1.0, 0.0)
        both = jnp.dot(
            picks.astype(jnp.bfloat16), pieces[...], preferred_element_type=jnp.float32
        )
        total = (both[:, 0:width] + both[:, width : 2 * width]).astype(jnp.bfloat16)
        leaving[pl.ds(first, 64)] = total.reshape(64, PITCH // 2, 2, width)

    def send_tile(c):
        def step(k, carry):
            dev, device = place.any_peer(k)
            remote(leaving.at[dev], back.at[place.dev], send_rows.at[0], recv_rows.at[0], device)
            return carry

        low = 64 * c + (1 if c == 0 else 0)
        lax.fori_loop(low, 64 * (c + 1), step, 0, unroll=3 if c == 0 else 4)

    group_rows = delta_ref.shape[0] // GROUPS

    def pick_rows(step):
        wanted = lax.rem(row_ref[...], group_rows) - step * RT
        shape = (RT, wanted.shape[1])
        picks = jnp.where(lax.broadcasted_iota(jnp.int32, shape, 0) == wanted, 1.0, 0.0)
        return picks.astype(jnp.bfloat16)

    def spread_out():
        grads = back[...].reshape(-1, width).astype(jnp.float32)
        group = column_ref[...] // group_rows
        for g in range(GROUPS):
            spread[:, g * width : (g + 1) * width] = jnp.where(group == g, grads, 0.0).astype(
                jnp.bfloat16
            )

    def update(step):
        every = jnp.dot(pick_rows(step), spread[...], preferred_element_type=jnp.float32)
        for g in range(GROUPS):
            total = every[:, g * width : (g + 1) * width]
            lines = (g * group_rows + step * RT) // width
            before = jnp.concatenate(
                [
                    jnp.broadcast_to(state_ref[pl.ds(lines + i, 1), :], (width, width)).T
                    for i in range(RT // width)
                ],
                axis=0,
            )
            after = before + jnp.sum(total * total, axis=1, keepdims=True) * (1.0 / width)
            delta_ref[pl.ds(g * group_rows + step * RT, RT), :] = (
                learn_rate * total / (jnp.sqrt(after) + epsilon)
            )
            for i in range(RT // width):
                state_out[pl.ds(lines + i, 1), :] = after[i * width : (i + 1) * width].T[0:1, :]

    push_sums(0)
    place.pass_on(all_in)
    slot_tile(0)
    back[pl.ds(place.dev, 1)] = leaving[pl.ds(place.dev, 1)]
    add_sums(0)
    push_sums(1)
    pl.semaphore_wait(all_in, 15)
    send_tile(0)
    for c in (1, 2, 3):
        slot_tile(c)
        send_tile(c)
    add_sums(1)
    push_sums(2)
    add_sums(2)
    push_whole(2)
    wait_whole(2)
    push_whole(1)
    wait_all(back, recv_rows.at[0])
    spread_out()
    steps = group_rows // RT
    for step in range(steps - 1):
        update(step)
    wait_whole(1)
    push_whole(0)
    update(steps - 1)
    for copy in started:
        copy.wait_send()
    wait_all(back, send_rows.at[0])
    wait_whole(0)


def tail(slot_index, looked, results, weights, asked, state):
    n_look, width = looked.shape
    n_dev = asked.shape[0]
    n_rows = state.shape[0]
    n = sum(w.size for w in weights) // width
    f32, bf16 = jnp.float32, jnp.bfloat16
    rows = asked[:, :PITCH].reshape(-1)
    vmem = pl.BlockSpec(memory_space=pltpu.VMEM)
    dma = pltpu.SemaphoreType.DMA
    blocks = (n_dev, PITCH // 2, 2, width)
    delta, new_state, summed, loss = pl.pallas_call(
        tail_kernel,
        out_shape=(
            jax.ShapeDtypeStruct((n_rows, width), f32),
            jax.ShapeDtypeStruct((n_rows // width, width), f32),
            jax.ShapeDtypeStruct((n, width), f32),
            jax.ShapeDtypeStruct((8, 128), f32),
        ),
        in_specs=[*[vmem] * 8, *[pl.BlockSpec(memory_space=pltpu.HBM)] * 4, *[vmem] * 3],
        out_specs=(vmem,) * 4,
        scratch_shapes=[
            *[pltpu.VMEM(w.shape, f32) for w in weights],
            dma((4,)),
            pltpu.VMEM((n_look, 2 * width), bf16),
            pltpu.VMEM(blocks, bf16),
            pltpu.VMEM(blocks, bf16),
            pltpu.VMEM((n_dev * PITCH, GROUPS * width), bf16),
            pltpu.VMEM((n, width), f32),
            pltpu.VMEM((n, width), f32),
            pltpu.VMEM((3, 16, 8, 128), f32),
            *[dma((23,)) for _ in range(6)],
            pltpu.SemaphoreType.REGULAR,
            *[dma((1,)) for _ in range(2)],
        ],
        compiler_params=pltpu.CompilerParams(
            collective_id=2, has_side_effects=True, vmem_limit_bytes=40 * 2**20
        ),
        name="tail",
    )(
        slot_index.reshape(1, n_look),
        looked,
        *results,
        *in_hbm(weights),
        rows.reshape(1, -1),
        rows.reshape(-1, 1),
        state.reshape(-1, width),
    )
    return delta, new_state, summed, loss[0, 0]


def finish_kernel(table_ref, delta_ref, state_ref, weights_ref, new_ref, state_out, *grads):
    new_ref[...] = table_ref[...] - delta_ref[...]

    @pl.when(pl.program_id(0) == 0)
    def _():
        state_out[...] = state_ref[...]
        hidden = grads[1].shape[0]
        for n, grad in enumerate(grads):
            part = weights_ref[pl.ds(n * hidden, hidden), :]
            grad[...] = part if n % 2 else part.T


def finish(table, delta, state, summed, weights):
    n_rows, width = table.shape
    step = n_rows // 8

    def kept(shape):
        return pl.BlockSpec(shape, lambda i: (0, 0))

    lines = pl.BlockSpec((step, width), lambda i: (i, 0))
    f32 = jnp.float32
    return pl.pallas_call(
        finish_kernel,
        out_shape=tuple(
            jax.ShapeDtypeStruct(shape, f32)
            for shape in (table.shape, state.shape, *[w.shape for w in weights])
        ),
        grid=(8,),
        in_specs=[lines, lines, kept(state.shape), kept(summed.shape)],
        out_specs=(lines, kept(state.shape), *[kept(w.shape) for w in weights]),
        compiler_params=pltpu.CompilerParams(vmem_limit_bytes=20 * 2**20),
        name="finish",
    )(table, delta, state, summed)


UT = 1024
CT = 256
IT = 1024

USER_GATHER, ITEM_GATHER, ITEM_GATHER_2, TOTALS, PULLED, ITEM_SUMS = range(6)


def nt(a, b):
    return lax.dot_general(a, b, (((1,), (1,)), ((), ())), preferred_element_type=jnp.float32)


def score_kernel(
    looked_ref,
    uf,
    us,
    tf,
    ts,
    user_ref,
    item_ref,
    out_ref,
    pulled_ref,
    totals_ref,
    isum_ref,
    uf_held,
    us_held,
    tf_held,
    ts_held,
    load_sem,
    users,
    items,
    acc,
    pull,
    pull_in,
    tot,
    tot_in,
    lz,
    part,
    part_in,
    send_sem,
    recv_sem,
):
    n_user = user_ref.shape[0]
    n_item = item_ref.shape[0]
    side = 4
    x = lax.axis_index("dp_0")
    y = lax.axis_index("dp_1")

    def peer(axis, k):
        if axis == "dp_0":
            return {"dp_0": lax.rem(x + k, side)}
        return {"dp_1": lax.rem(y + k, side)}

    def push(kind, axis, k, src, dst):
        copy = pltpu.make_async_remote_copy(
            src_ref=src,
            dst_ref=dst,
            send_sem=send_sem.at[kind, k - 1],
            recv_sem=recv_sem.at[kind, k - 1],
            device_id=peer(axis, k),
            device_id_type=MESH,
        )
        copy.start()
        return copy

    held = (uf_held, us_held, tf_held, ts_held)
    loads = fetched_weights((uf, us, tf, ts), held, load_sem)
    barrier = pltpu.get_barrier_semaphore()
    for axis in ("dp_0", "dp_1"):
        for k in range(1, side):
            pl.semaphore_signal(barrier, inc=1, device_id=peer(axis, k), device_id_type=MESH)
    for copy in loads:
        copy.wait()
    weights = [(halves(a[...]), halves(b[...])) for a, b in (held[:2], held[2:])]

    def forward(tile):
        rows = pl.ds(tile * ROWS, ROWS)
        z, vec = forward_tile(looked_ref[rows, :], *weights[min(tile, 1)])
        out_ref[rows, :] = z
        if tile == 0:
            user_ref[...] = vec.astype(jnp.bfloat16)
        else:
            item_ref[pl.ds((tile - 1) * ROWS, ROWS), :] = vec.astype(jnp.bfloat16)

    forward(0)
    pl.semaphore_wait(barrier, 2 * (side - 1))

    item_copies, user_copies = {1: [], 2: [], 3: []}, {}
    for k in (1, 3, 2):
        user_copies[side - k] = push(
            USER_GATHER, "dp_0", k, user_ref, users.at[pl.ds((side - k) * n_user, n_user)]
        )
    for half, kind in enumerate((ITEM_GATHER, ITEM_GATHER_2)):
        forward(half + 1)
        for k in (1, 3, 2):
            item_copies[side - k].append(
                push(
                    kind,
                    "dp_1",
                    k,
                    item_ref.at[pl.ds(half * ROWS, ROWS)],
                    items.at[pl.ds((side - k) * n_item + half * ROWS, ROWS)],
                )
            )
    users[pl.ds(0, n_user), :] = user_ref[...]
    items[pl.ds(0, n_item), :] = item_ref[...]

    def pass_one(j, low, high):
        def step(n, carry):
            rows = pl.ds(pl.multiple_of(n * UT, UT), UT)
            u = users[rows, :]
            total = jnp.zeros((UT, 128), jnp.float32) if j == 0 else acc[rows, :]
            pulled = jnp.zeros((UT, 128), jnp.float32) if j == 0 else pull[rows, :]
            for c in range(n_item // CT):
                cand = items[pl.ds(j * n_item + c * CT, CT), :]
                e = jnp.exp2(nt(u, cand) * LOG2_SCALE)
                for lane in range(CT // 128):
                    total += e[:, lane * 128 : (lane + 1) * 128]
                pulled += jnp.dot(
                    e.astype(jnp.bfloat16), cand, preferred_element_type=jnp.float32
                )
            acc[rows, :] = total
            pull[rows, :] = pulled
            return carry

        lax.fori_loop(low, high, step, 0)

    steps = side * n_user // UT
    for i in (3, 1, 2):
        user_copies[i].wait_recv()
    pass_one(0, 0, steps)
    for j in (3, 1, 2):
        for copy in item_copies[j]:
            copy.wait_recv()
        pass_one(j, 0, steps)

    for s in range(side):
        sums = acc[pl.ds(s * n_user, n_user), :]
        tot[pl.ds(s, 1), :] = jnp.sum(sums.T, axis=0, keepdims=True)
    total_copies = [push(TOTALS, "dp_0", k, tot, tot_in.at[k - 1]) for k in (1, 3, 2)]
    pull_copies = [
        push(PULLED, "dp_0", k, pull.at[pl.ds(k * n_user, n_user)], pull_in.at[k - 1])
        for k in (1, 3, 2)
    ]
    for copy in total_copies:
        copy.wait_recv()
    for s in range(side):
        whole = tot[pl.ds(s, 1), :]
        for k in range(1, side):
            whole += tot_in[k - 1, pl.ds((s + k) % side, 1), :]
        if s == 0:
            totals_ref[...] = whole
        lz[pl.ds(s, 1), :] = jnp.log2(whole)

    def pass_two(j):
        def step(n, carry):
            rows = pl.ds(pl.multiple_of(n * IT, IT), IT)
            cand = items[pl.ds(pl.multiple_of(j * n_item + n * IT, IT), IT), :]
            sums = jnp.zeros((IT, 128), jnp.float32)
            for s in range(side):
                u = users[pl.ds(s * n_user, n_user), :]
                p = jnp.exp2(nt(cand, u) * LOG2_SCALE - lz[pl.ds(s, 1), :])
                sums += jnp.dot(p.astype(jnp.bfloat16), u, preferred_element_type=jnp.float32)
            if j == 0:
                isum_ref[rows, :] = sums
            else:
                part[j - 1, rows, :] = sums.astype(jnp.bfloat16)
            return carry

        lax.fori_loop(0, n_item // IT, step, 0)

    sum_copies = []
    for j in (2, 1, 3):
        pass_two(j)
        sum_copies.append(push(ITEM_SUMS, "dp_1", j, part.at[j - 1], part_in.at[j - 1]))
    pass_two(0)
    for copy in pull_copies:
        copy.wait_recv()
    pulled_ref[...] = pull[pl.ds(0, n_user), :] + pull_in[0] + pull_in[1] + pull_in[2]
    for copy in sum_copies:
        copy.wait_recv()
    isum_ref[...] += (
        part_in[0].astype(jnp.float32)
        + part_in[1].astype(jnp.float32)
        + part_in[2].astype(jnp.float32)
    )
    for copy in [
        *user_copies.values(),
        *item_copies[1],
        *item_copies[2],
        *item_copies[3],
        *total_copies,
        *pull_copies,
        *sum_copies,
    ]:
        copy.wait_send()


def group_scores(looked, weights):
    n, width = looked.shape
    n_user, n_item = EXAMPLES, n - EXAMPLES
    f32, bf16 = jnp.float32, jnp.bfloat16
    vmem = pl.BlockSpec(memory_space=pltpu.VMEM)
    return pl.pallas_call(
        score_kernel,
        out_shape=(
            jax.ShapeDtypeStruct((n_user, width), bf16),
            jax.ShapeDtypeStruct((n_item, width), bf16),
            jax.ShapeDtypeStruct((n, width), f32),
            jax.ShapeDtypeStruct((n_user, width), f32),
            jax.ShapeDtypeStruct((1, n_user), f32),
            jax.ShapeDtypeStruct((n_item, width), f32),
        ),
        in_specs=[vmem, *[pl.BlockSpec(memory_space=pltpu.HBM)] * 4],
        out_specs=(vmem,) * 6,
        scratch_shapes=[
            *[pltpu.VMEM(w.shape, f32) for w in weights],
            pltpu.SemaphoreType.DMA((4,)),
            pltpu.VMEM((4 * n_user, width), bf16),
            pltpu.VMEM((4 * n_item, width), bf16),
            pltpu.VMEM((4 * n_user, width), f32),
            pltpu.VMEM((4 * n_user, width), f32),
            pltpu.VMEM((3, n_user, width), f32),
            pltpu.VMEM((4, n_user), f32),
            pltpu.VMEM((3, 4, n_user), f32),
            pltpu.VMEM((4, n_user), f32),
            pltpu.VMEM((3, n_item, width), bf16),
            pltpu.VMEM((3, n_item, width), bf16),
            pltpu.SemaphoreType.DMA((6, 3)),
            pltpu.SemaphoreType.DMA((6, 3)),
        ],
        compiler_params=pltpu.CompilerParams(
            collective_id=0, has_side_effects=True, vmem_limit_bytes=40 * 2**20
        ),
        name="group_scores",
    )(looked, *in_hbm(weights))


def per_device(
    id_table, ada_state, user_first, user_second, item_first, item_second, fetch_rows, lookup_slots
):
    cap = fetch_rows.shape[3]
    slot_rows, asked = fetch(fetch_rows[0], id_table)
    slot_index = lookup_slots[0]
    looked = jnp.take(slot_rows, slot_index, axis=0, mode="clip")
    towers = (user_first, user_second, item_first, item_second)
    user_bf, item_bf, out, *sums = group_scores(looked, towers)
    n_dev = slot_rows.shape[0] // cap
    wide_index = slot_index // cap * PITCH + slot_index % cap
    delta, state, summed, loss = tail(
        wide_index, looked, (out, user_bf, item_bf, *sums), towers, asked, ada_state
    )
    new_table, new_state, *grads = finish(id_table, delta, state, summed, towers)
    return (new_table, new_state.reshape(-1), *grads, loss / (n_dev * EXAMPLES))


def solution(mesh):
    finer = Mesh(mesh.devices.reshape(4, 4, 8, 2), DP_SHARD)
    in_specs = (
        P(DP_SHARD, None),
        P(DP_SHARD),
        P(),
        P(),
        P(),
        P(),
        P(DP_SHARD, None, None, None),
        P(DP_SHARD, None),
    )
    out_specs = (P(DP_SHARD, None), P(DP_SHARD), P(), P(), P(), P(), P())
    return jax.shard_map(
        per_device, mesh=finer, in_specs=in_specs, out_specs=out_specs, check_vma=False
    )
```

```python
import functools
import math

import jax
import jax.numpy as jnp
from jax import lax
from jax.experimental import pallas as pl
from jax.experimental.pallas import tpu as pltpu
from jax.sharding import Mesh
from jax.sharding import PartitionSpec as P

DP_SHARD = ("dp_0", "dp_1", "shard_0", "shard_1")
DP = ("dp_0", "dp_1")
SHARD = ("shard_0", "shard_1")
MESH = pl.DeviceIdType.MESH
EXAMPLES = 512

logit_divisor = 0.025
learn_rate = 0.1
epsilon = 1e-08
LOG2_SCALE = math.log2(math.e) / logit_divisor


ROWS = 512
NN, NT, TN = ((1,), (0,)), ((1,), (1,)), ((0,), (0,))


def halves(x):
    high = x.astype(jnp.bfloat16)
    return high, (x - high.astype(jnp.float32)).astype(jnp.bfloat16)


def dot3(a, b, dims):
    (ah, al), (bh, bl) = a, b

    def product(x, y):
        return lax.dot_general(x, y, (dims, ((), ())), preferred_element_type=jnp.float32)

    return product(ah, bh) + (product(ah, bl) + product(al, bh))


def fetched_weights(refs, held, sems):
    copies = [
        pltpu.make_async_copy(ref, into, sems.at[n]) for n, (ref, into) in enumerate(zip(refs, held))
    ]
    for copy in copies:
        copy.start()
    return copies


def in_hbm(arrays):
    return [pltpu.with_memory_space_constraint(a, pltpu.HBM) for a in arrays]


def forward_tile(looked, first, second):
    pre = dot3(halves(looked), first, NN)
    z = dot3(halves(pre * lax.logistic(pre)), second, NN)
    return z, z / jnp.sqrt(jnp.sum(z * z, axis=1, keepdims=True) + 1e-06)


def backward_tile(looked, z, cot, first, second):
    scale = 1.0 / jnp.sqrt(jnp.sum(z * z, axis=1, keepdims=True) + 1e-06)
    vec = z * scale
    dz = halves(scale * (cot - vec * jnp.sum(cot * vec, axis=1, keepdims=True)))
    x = halves(looked)
    pre = dot3(x, first, NN)
    gate = lax.logistic(pre)
    hidden = halves(pre * gate)
    dpre = halves(dot3(dz, second, NT) * (gate * (1.0 + pre * (1.0 - gate))))
    return dot3(dpre, first, NT), dot3(dpre, x, TN), dot3(hidden, dz, TN)


class Place:
    def __init__(self):
        self.x, self.y = lax.axis_index("dp_0"), lax.axis_index("dp_1")
        self.z, self.core = lax.axis_index("shard_0"), lax.axis_index("shard_1")
        self.dp = self.x * 4 + self.y
        self.shard = self.z * 2 + self.core
        self.dev = self.dp * 16 + self.shard

    def shard_peer(self, k):
        p = lax.rem(self.shard + k, 16)
        return p, {"shard_0": lax.div(p, 2), "shard_1": lax.rem(p, 2)}

    def dp_peer(self, k):
        px, py = lax.rem(self.x + k // 4, 4), lax.rem(self.y + k % 4, 4)
        return px * 4 + py, {"dp_0": px, "dp_1": py}

    def any_peer(self, n):
        px = lax.rem(self.x + lax.div(n, 64), 4)
        py = lax.rem(self.y + lax.rem(lax.div(n, 16), 4), 4)
        pz = lax.rem(self.z + lax.div(lax.rem(n, 16), 2), 8)
        pc = lax.rem(self.core + lax.rem(n, 2), 2)
        device = {"dp_0": px, "dp_1": py, "shard_0": pz, "shard_1": pc}
        return (px * 4 + py) * 16 + pz * 2 + pc, device

    def greet(self, meanwhile=lambda: None):
        barrier = pltpu.get_barrier_semaphore()
        for peer in (self.shard_peer, self.dp_peer):
            for k in range(1, 16):
                pl.semaphore_signal(barrier, inc=1, device_id=peer(k)[1], device_id_type=MESH)
        meanwhile()
        pl.semaphore_wait(barrier, 30)

    def pass_on(self, sem):
        for k in range(1, 16):
            pl.semaphore_signal(sem, inc=1, device_id=self.dp_peer(k)[1], device_id_type=MESH)


def remote(src, dst, send, recv, device):
    copy = pltpu.make_async_remote_copy(
        src_ref=src,
        dst_ref=dst,
        send_sem=send,
        recv_sem=recv,
        device_id=device,
        device_id_type=MESH,
    )
    copy.start()
    return copy


def wait_all(ref, sem):
    others = ref.at[pl.ds(0, ref.shape[0] - 1)]
    pltpu.make_async_copy(others, others, sem).wait()


LANES = 16


def fetch_kernel(
    ids_ref,
    table_ref,
    slots_ref,
    looked_ref,
    asked_ref,
    rows,
    table,
    held,
    sorted_ids,
    arrived,
    wanted,
    fetched,
    load_sem,
    all_in,
    send_s,
    recv_s,
    send_d,
    recv_d,
    send_rows,
    recv_rows,
):
    place = Place()
    cap = fetched.shape[1]
    n_dev = fetched.shape[0]
    whole = pltpu.make_async_copy(table_ref, table, load_sem.at[0])
    whole.start()
    place.greet()
    copies = []
    for k in range(1, 16):
        p, device = place.shard_peer(k)
        copies.append(
            remote(ids_ref.at[p], held.at[place.shard], send_s.at[k], recv_s.at[k], device)
        )
    place.pass_on(all_in)
    held[pl.ds(place.shard, 1)] = ids_ref[pl.ds(place.shard, 1)]
    for copy in copies:
        copy.wait_recv()
    per = 128 // LANES
    for half in range(2):
        lines = held[:, half, :]
        for d in range(per):
            sorted_ids[half * per + d] = (
                lines if d == 0 else pltpu.roll(lines, 128 - d * LANES, axis=1)
            )
    late = []
    for k in range(1, 16):
        d, device = place.dp_peer(k)
        late.append(
            remote(
                sorted_ids.at[d], arrived.at[place.dp], send_d.at[k], recv_d.at[k], device
            )
        )
    arrived[pl.ds(place.dp, 1)] = sorted_ids[pl.ds(place.dp, 1)]
    for copy in late:
        copy.wait_recv()
    n_dp = sorted_ids.shape[0]
    field = lax.broadcasted_iota(jnp.int32, (n_dp, 128), 1) // LANES
    for half in range(2):
        lines = arrived[:, half * per, :]
        for q in range(1, per):
            line = pltpu.roll(arrived[:, half * per + q, :], q * LANES, axis=1)
            lines = jnp.where(field == q, line, lines)
        asked_ref[half] = lines
    scalars = pltpu.make_async_copy(asked_ref, wanted, load_sem.at[1])
    scalars.start()
    pl.semaphore_wait(all_in, 15)
    scalars.wait()
    whole.wait()

    def asked_at(dev):
        s = lax.rem(dev, 16)
        return lax.div(s, per), lax.div(dev, 16), lax.rem(s, per) * LANES

    def step(n, carry):
        dev, device = place.any_peer(n)
        half, d, low = asked_at(dev)
        for k in range(cap):
            fetched[dev, k] = table[wanted[half, d, low + k]]
        remote(
            fetched.at[dev],
            rows.at[pl.ds(place.dev * cap, cap)],
            send_rows.at[0],
            recv_rows.at[0],
            device,
        )
        return carry

    lax.fori_loop(1, 256, step, 0, unroll=3)
    half, d, low = asked_at(place.dev)
    for k in range(cap):
        rows[place.dev * cap + k] = table[wanted[half, d, low + k]]
    for copy in copies + late:
        copy.wait_send()
    landed = rows.at[pl.ds(0, (n_dev - 1) * cap)]
    pltpu.make_async_copy(landed, landed, recv_rows.at[0]).wait()

    def look(n, carry):
        looked_ref[n] = rows[slots_ref[n]]
        return carry

    lax.fori_loop(0, looked_ref.shape[0], look, 0, unroll=8)
    wait_all(fetched, send_rows.at[0])


def fetch(ids, table, slots):
    n_dp, n_shard, cap = ids.shape
    n_rows, width = table.shape
    n_dev = n_dp * n_shard
    vmem = pl.BlockSpec(memory_space=pltpu.VMEM)
    dma = pltpu.SemaphoreType.DMA
    lines = jnp.pad(ids, ((0, 0), (0, 0), (0, LANES - cap)), constant_values=n_rows)
    lines = jnp.swapaxes(lines, 0, 1).reshape(n_shard, n_dp * LANES // 128, 128)
    looked, asked = pl.pallas_call(
        fetch_kernel,
        out_shape=(
            jax.ShapeDtypeStruct((slots.shape[0], 1, width), jnp.float32),
            jax.ShapeDtypeStruct((2, n_dp, 128), jnp.int32),
        ),
        in_specs=[
            vmem,
            pl.BlockSpec(memory_space=pltpu.HBM),
            pl.BlockSpec(memory_space=pltpu.SMEM),
        ],
        out_specs=(vmem, vmem),
        scratch_shapes=[
            pltpu.VMEM((n_dev * cap, 1, width), jnp.float32),
            pltpu.VMEM((n_rows, 1, width), jnp.float32),
            pltpu.VMEM(lines.shape, jnp.int32),
            pltpu.VMEM((n_dp, n_shard, 128), jnp.int32),
            pltpu.VMEM((n_dp, n_shard, 128), jnp.int32),
            pltpu.SMEM((2, n_dp, 128), jnp.int32),
            pltpu.VMEM((n_dev, cap, 1, width), jnp.float32),
            dma((2,)),
            pltpu.SemaphoreType.REGULAR,
            *[dma((16,)) for _ in range(4)],
            *[dma((1,)) for _ in range(2)],
        ],
        compiler_params=pltpu.CompilerParams(
            collective_id=1, has_side_effects=True, vmem_limit_bytes=20 * 2**20
        ),
        name="fetch",
    )(
        lines,
        pltpu.with_memory_space_constraint(table.reshape(n_rows, 1, width), pltpu.HBM),
        slots,
    )
    asked = jnp.swapaxes(asked, 0, 1).reshape(n_dev, LANES)
    return looked.reshape(-1, width), asked


PITCH = 10
GROUPS = 4
RT = 1024


def stages_of(place):
    def core_peer(k):
        p = lax.rem(place.core + k, 2)
        return p, {"shard_1": p}

    def z_peer(k):
        p = lax.rem(place.z + k, 8)
        return p, {"shard_0": p}

    return (place.core, 2, core_peer), (place.dp, 16, place.dp_peer), (place.z, 8, z_peer)


def tail_kernel(
    slots_ref,
    looked_ref,
    out_ref,
    user_ref,
    item_ref,
    pulled_ref,
    totals_ref,
    isum_ref,
    uf,
    us,
    tf,
    ts,
    row_ref,
    column_ref,
    state_ref,
    delta_ref,
    state_out,
    weights_ref,
    loss_out,
    uf_held,
    us_held,
    tf_held,
    ts_held,
    load_sem,
    pieces,
    leaving,
    back,
    spread,
    mine,
    arrived,
    losses,
    wsend,
    wrecv,
    gsend,
    grecv,
    lsend,
    lrecv,
    all_in,
    send_rows,
    recv_rows,
):
    place = Place()
    width = looked_ref.shape[1]
    stages = stages_of(place)
    hidden = us_held.shape[0]
    n = 4 * hidden
    held = (uf_held, us_held, tf_held, ts_held)
    loads = fetched_weights((uf, us, tf, ts), held, load_sem)

    def prepare():
        users = user_ref[...].astype(jnp.float32)
        positive = item_ref[pl.ds(0, EXAMPLES), :].astype(jnp.float32)
        totals = totals_ref[...]
        loss = jnp.sum(jnp.log(totals)) - jnp.sum(users * positive) / logit_divisor
        losses[0, pl.ds(place.core, 1)] = jnp.full((1, 8, 128), 1.0, jnp.float32) * loss
        for copy in loads:
            copy.wait()
        weights = [(halves(a[...]), halves(b[...])) for a, b in (held[:2], held[2:])]
        for tile in range(looked_ref.shape[0] // ROWS):
            rows = pl.ds(tile * ROWS, ROWS)
            if tile == 0:
                cot = pulled_ref[...] / jnp.broadcast_to(totals, (width, EXAMPLES)).T - positive
            else:
                cot = isum_ref[pl.ds((tile - 1) * ROWS, ROWS), :]
                if tile == 1:
                    cot = cot - users
            look, first_grad, second_grad = backward_tile(
                looked_ref[rows, :], out_ref[rows, :], cot / logit_divisor, *weights[min(tile, 1)]
            )
            high, low = halves(look)
            pieces[rows, 0:width] = high
            pieces[rows, width : 2 * width] = low
            at = pl.ds(min(tile, 1) * 2 * hidden, hidden)
            after = pl.ds((min(tile, 1) * 2 + 1) * hidden, hidden)
            if tile < 2:
                mine[at, :] = first_grad
                mine[after, :] = second_grad
            else:
                mine[at, :] += first_grad
                mine[after, :] += second_grad

    place.greet(prepare)

    sizes, lows, lands, shifts = [], [0], [], []
    size, landed, shift = n, 0, 0
    for at, side, _ in stages:
        size //= side
        sizes.append(size)
        lows.append(lows[-1] + at * size)
        lands.append(landed)
        shifts.append(shift)
        landed += (side - 1) * size
        shift += side - 1
    started, scatter, gather = [], {}, {}

    def push_sums(stage):
        at, side, peer = stages[stage]
        part = sizes[stage]
        scatter[stage] = []
        for k in range(1, side):
            p, device = peer(k)
            sem = shifts[stage] + k - 1
            start = pl.multiple_of(lows[stage] + p * part, 8)
            scatter[stage].append(
                remote(
                    mine.at[pl.ds(start, part)],
                    arrived.at[pl.ds(lands[stage] + (k - 1) * part, part)],
                    wsend.at[sem],
                    wrecv.at[sem],
                    device,
                )
            )
            scatter[stage].append(
                remote(
                    losses.at[stage, at],
                    losses.at[stage, at],
                    lsend.at[sem],
                    lrecv.at[sem],
                    device,
                )
            )
        started.extend(scatter[stage])

    def add_sums(stage):
        at, side, _ = stages[stage]
        part = sizes[stage]
        for copy in scatter[stage]:
            copy.wait_recv()
        here = pl.ds(pl.multiple_of(lows[stage + 1], 8), part)
        total = mine[here, :]
        for k in range(1, side):
            total += arrived[pl.ds(lands[stage] + (k - 1) * part, part), :]
        loss = losses[stage, 0]
        for p in range(1, side):
            loss += losses[stage, p]
        if stage + 1 < len(stages):
            mine[here, :] = total
            losses[stage + 1, pl.ds(stages[stage + 1][0], 1)] = loss[None]
        else:
            weights_ref[here, :] = total * (1.0 / 256)
            loss_out[...] = loss

    def push_whole(stage):
        at, side, peer = stages[stage]
        here = pl.ds(pl.multiple_of(lows[stage + 1], 8), sizes[stage])
        gather[stage] = []
        for k in range(1, side):
            sem = shifts[stage] + k - 1
            gather[stage].append(
                remote(
                    weights_ref.at[here], weights_ref.at[here], gsend.at[sem], grecv.at[sem], peer(k)[1]
                )
            )
        started.extend(gather[stage])

    def wait_whole(stage):
        for copy in gather[stage]:
            copy.wait_recv()

    def slot_tile(c):
        first = lax.rem(place.x + c, 4) * 64
        slots = slots_ref[...]
        owner = lax.shift_right_logical(slots * 7282, 16)
        wanted = slots + owner - first * PITCH
        shape = (64 * PITCH, wanted.shape[1])
        picks = jnp.where(lax.broadcasted_iota(jnp.int32, shape, 0) == wanted, 1.0, 0.0)
        both = jnp.dot(
            picks.astype(jnp.bfloat16), pieces[...], preferred_element_type=jnp.float32
        )
        total = (both[:, 0:width] + both[:, width : 2 * width]).astype(jnp.bfloat16)
        leaving[pl.ds(first, 64)] = total.reshape(64, PITCH // 2, 2, width)

    def send_tile(c):
        def step(k, carry):
            dev, device = place.any_peer(k)
            remote(leaving.at[dev], back.at[place.dev], send_rows.at[0], recv_rows.at[0], device)
            return carry

        low = 64 * c + (1 if c == 0 else 0)
        lax.fori_loop(low, 64 * (c + 1), step, 0, unroll=3 if c == 0 else 4)

    group_rows = delta_ref.shape[0] // GROUPS

    def pick_rows(step):
        wanted = lax.rem(row_ref[...], group_rows) - step * RT
        shape = (RT, wanted.shape[1])
        picks = jnp.where(lax.broadcasted_iota(jnp.int32, shape, 0) == wanted, 1.0, 0.0)
        return picks.astype(jnp.bfloat16)

    def spread_out():
        grads = back[...].reshape(-1, width).astype(jnp.float32)
        group = column_ref[...] // group_rows
        for g in range(GROUPS):
            spread[:, g * width : (g + 1) * width] = jnp.where(group == g, grads, 0.0).astype(
                jnp.bfloat16
            )

    def update(step):
        every = jnp.dot(pick_rows(step), spread[...], preferred_element_type=jnp.float32)
        for g in range(GROUPS):
            total = every[:, g * width : (g + 1) * width]
            lines = (g * group_rows + step * RT) // width
            before = jnp.concatenate(
                [
                    jnp.broadcast_to(state_ref[pl.ds(lines + i, 1), :], (width, width)).T
                    for i in range(RT // width)
                ],
                axis=0,
            )
            after = before + jnp.sum(total * total, axis=1, keepdims=True) * (1.0 / width)
            delta_ref[pl.ds(g * group_rows + step * RT, RT), :] = (
                learn_rate * total / (jnp.sqrt(after) + epsilon)
            )
            for i in range(RT // width):
                state_out[pl.ds(lines + i, 1), :] = after[i * width : (i + 1) * width].T[0:1, :]

    push_sums(0)
    place.pass_on(all_in)
    slot_tile(0)
    back[pl.ds(place.dev, 1)] = leaving[pl.ds(place.dev, 1)]
    add_sums(0)
    push_sums(1)
    pl.semaphore_wait(all_in, 15)
    send_tile(0)
    slot_tile(1)
    send_tile(1)
    slot_tile(2)
    add_sums(1)
    push_sums(2)
    send_tile(2)
    slot_tile(3)
    add_sums(2)
    push_whole(2)
    send_tile(3)
    wait_whole(2)
    push_whole(1)
    wait_all(back, recv_rows.at[0])
    spread_out()
    steps = group_rows // RT
    for step in range(steps - 1):
        update(step)
    wait_whole(1)
    push_whole(0)
    update(steps - 1)
    for copy in started:
        copy.wait_send()
    wait_all(back, send_rows.at[0])
    wait_whole(0)


def tail(slot_index, looked, results, weights, asked, state):
    n_look, width = looked.shape
    n_dev = asked.shape[0]
    n_rows = state.shape[0]
    n = sum(w.size for w in weights) // width
    f32, bf16 = jnp.float32, jnp.bfloat16
    rows = asked[:, :PITCH].reshape(-1)
    vmem = pl.BlockSpec(memory_space=pltpu.VMEM)
    dma = pltpu.SemaphoreType.DMA
    blocks = (n_dev, PITCH // 2, 2, width)
    delta, new_state, summed, loss = pl.pallas_call(
        tail_kernel,
        out_shape=(
            jax.ShapeDtypeStruct((n_rows, width), f32),
            jax.ShapeDtypeStruct((n_rows // width, width), f32),
            jax.ShapeDtypeStruct((n, width), f32),
            jax.ShapeDtypeStruct((8, 128), f32),
        ),
        in_specs=[*[vmem] * 8, *[pl.BlockSpec(memory_space=pltpu.HBM)] * 4, *[vmem] * 3],
        out_specs=(vmem,) * 4,
        scratch_shapes=[
            *[pltpu.VMEM(w.shape, f32) for w in weights],
            dma((4,)),
            pltpu.VMEM((n_look, 2 * width), bf16),
            pltpu.VMEM(blocks, bf16),
            pltpu.VMEM(blocks, bf16),
            pltpu.VMEM((n_dev * PITCH, GROUPS * width), bf16),
            pltpu.VMEM((n, width), f32),
            pltpu.VMEM((n, width), f32),
            pltpu.VMEM((3, 16, 8, 128), f32),
            *[dma((23,)) for _ in range(6)],
            pltpu.SemaphoreType.REGULAR,
            *[dma((1,)) for _ in range(2)],
        ],
        compiler_params=pltpu.CompilerParams(
            collective_id=2, has_side_effects=True, vmem_limit_bytes=40 * 2**20
        ),
        name="tail",
    )(
        slot_index.reshape(1, n_look),
        looked,
        *results,
        *in_hbm(weights),
        rows.reshape(1, -1),
        rows.reshape(-1, 1),
        state.reshape(-1, width),
    )
    return delta, new_state, summed, loss[0, 0]


def finish_kernel(table_ref, delta_ref, state_ref, weights_ref, new_ref, state_out, *grads):
    new_ref[...] = table_ref[...] - delta_ref[...]

    @pl.when(pl.program_id(0) == 0)
    def _():
        state_out[...] = state_ref[...]
        hidden = grads[1].shape[0]
        for n, grad in enumerate(grads):
            part = weights_ref[pl.ds(n * hidden, hidden), :]
            grad[...] = part if n % 2 else part.T


def finish(table, delta, state, summed, weights):
    n_rows, width = table.shape
    step = n_rows // 4

    def kept(shape):
        return pl.BlockSpec(shape, lambda i: (0, 0))

    lines = pl.BlockSpec((step, width), lambda i: (i, 0))
    f32 = jnp.float32
    return pl.pallas_call(
        finish_kernel,
        out_shape=tuple(
            jax.ShapeDtypeStruct(shape, f32)
            for shape in (table.shape, state.shape, *[w.shape for w in weights])
        ),
        grid=(4,),
        in_specs=[lines, lines, kept(state.shape), kept(summed.shape)],
        out_specs=(lines, kept(state.shape), *[kept(w.shape) for w in weights]),
        compiler_params=pltpu.CompilerParams(vmem_limit_bytes=20 * 2**20),
        name="finish",
    )(table, delta, state, summed)


UT = 1024
CT = 256
IT = 1024

USER_GATHER, ITEM_GATHER, ITEM_GATHER_2, TOTALS, PULLED, ITEM_SUMS = range(6)


def nt(a, b):
    return lax.dot_general(a, b, (((1,), (1,)), ((), ())), preferred_element_type=jnp.float32)


def score_kernel(
    looked_ref,
    uf,
    us,
    tf,
    ts,
    user_ref,
    item_ref,
    out_ref,
    pulled_ref,
    totals_ref,
    isum_ref,
    uf_held,
    us_held,
    tf_held,
    ts_held,
    load_sem,
    users,
    items,
    acc,
    pull,
    pull_in,
    tot,
    tot_in,
    lz,
    part,
    part_in,
    send_sem,
    recv_sem,
):
    n_user = user_ref.shape[0]
    n_item = item_ref.shape[0]
    side = 4
    x = lax.axis_index("dp_0")
    y = lax.axis_index("dp_1")

    def peer(axis, k):
        if axis == "dp_0":
            return {"dp_0": lax.rem(x + k, side)}
        return {"dp_1": lax.rem(y + k, side)}

    def push(kind, axis, k, src, dst):
        copy = pltpu.make_async_remote_copy(
            src_ref=src,
            dst_ref=dst,
            send_sem=send_sem.at[kind, k - 1],
            recv_sem=recv_sem.at[kind, k - 1],
            device_id=peer(axis, k),
            device_id_type=MESH,
        )
        copy.start()
        return copy

    held = (uf_held, us_held, tf_held, ts_held)
    loads = fetched_weights((uf, us, tf, ts), held, load_sem)
    barrier = pltpu.get_barrier_semaphore()
    for axis in ("dp_0", "dp_1"):
        for k in range(1, side):
            pl.semaphore_signal(barrier, inc=1, device_id=peer(axis, k), device_id_type=MESH)
    for copy in loads:
        copy.wait()
    weights = [(halves(a[...]), halves(b[...])) for a, b in (held[:2], held[2:])]

    def forward(tile):
        rows = pl.ds(tile * ROWS, ROWS)
        z, vec = forward_tile(looked_ref[rows, :], *weights[min(tile, 1)])
        out_ref[rows, :] = z
        if tile == 0:
            user_ref[...] = vec.astype(jnp.bfloat16)
        else:
            item_ref[pl.ds((tile - 1) * ROWS, ROWS), :] = vec.astype(jnp.bfloat16)

    forward(0)
    pl.semaphore_wait(barrier, 2 * (side - 1))

    item_copies, user_copies = {1: [], 2: [], 3: []}, {}
    for k in (1, 3, 2):
        user_copies[side - k] = push(
            USER_GATHER, "dp_0", k, user_ref, users.at[pl.ds((side - k) * n_user, n_user)]
        )
    for half, kind in enumerate((ITEM_GATHER, ITEM_GATHER_2)):
        forward(half + 1)
        for k in (1, 3, 2):
            item_copies[side - k].append(
                push(
                    kind,
                    "dp_1",
                    k,
                    item_ref.at[pl.ds(half * ROWS, ROWS)],
                    items.at[pl.ds((side - k) * n_item + half * ROWS, ROWS)],
                )
            )
    users[pl.ds(0, n_user), :] = user_ref[...]
    items[pl.ds(0, n_item), :] = item_ref[...]

    def pass_one(j, low, high):
        def step(n, carry):
            rows = pl.ds(pl.multiple_of(n * UT, UT), UT)
            u = users[rows, :]
            total = jnp.zeros((UT, 128), jnp.float32) if j == 0 else acc[rows, :]
            pulled = jnp.zeros((UT, 128), jnp.float32) if j == 0 else pull[rows, :]
            for c in range(n_item // CT):
                cand = items[pl.ds(j * n_item + c * CT, CT), :]
                e = jnp.exp2(nt(u, cand) * LOG2_SCALE)
                for lane in range(CT // 128):
                    total += e[:, lane * 128 : (lane + 1) * 128]
                pulled += jnp.dot(
                    e.astype(jnp.bfloat16), cand, preferred_element_type=jnp.float32
                )
            acc[rows, :] = total
            pull[rows, :] = pulled
            return carry

        lax.fori_loop(low, high, step, 0)

    steps = side * n_user // UT
    for i in (3, 1, 2):
        user_copies[i].wait_recv()
    pass_one(0, 0, steps)
    for j in (3, 1, 2):
        for copy in item_copies[j]:
            copy.wait_recv()
        pass_one(j, 0, steps)

    for s in range(side):
        sums = acc[pl.ds(s * n_user, n_user), :]
        tot[pl.ds(s, 1), :] = jnp.sum(sums.T, axis=0, keepdims=True)
    total_copies = [push(TOTALS, "dp_0", k, tot, tot_in.at[k - 1]) for k in (1, 3, 2)]
    pull_copies = [
        push(PULLED, "dp_0", k, pull.at[pl.ds(k * n_user, n_user)], pull_in.at[k - 1])
        for k in (1, 3, 2)
    ]
    for copy in total_copies:
        copy.wait_recv()
    for s in range(side):
        whole = tot[pl.ds(s, 1), :]
        for k in range(1, side):
            whole += tot_in[k - 1, pl.ds((s + k) % side, 1), :]
        if s == 0:
            totals_ref[...] = whole
        lz[pl.ds(s, 1), :] = jnp.log2(whole)

    def pass_two(j):
        def step(n, carry):
            rows = pl.ds(pl.multiple_of(n * IT, IT), IT)
            cand = items[pl.ds(pl.multiple_of(j * n_item + n * IT, IT), IT), :]
            sums = jnp.zeros((IT, 128), jnp.float32)
            for s in range(side):
                u = users[pl.ds(s * n_user, n_user), :]
                p = jnp.exp2(nt(cand, u) * LOG2_SCALE - lz[pl.ds(s, 1), :])
                sums += jnp.dot(p.astype(jnp.bfloat16), u, preferred_element_type=jnp.float32)
            if j == 0:
                isum_ref[rows, :] = sums
            else:
                part[j - 1, rows, :] = sums.astype(jnp.bfloat16)
            return carry

        lax.fori_loop(0, n_item // IT, step, 0)

    sum_copies = []
    for j in (2, 1, 3):
        pass_two(j)
        sum_copies.append(push(ITEM_SUMS, "dp_1", j, part.at[j - 1], part_in.at[j - 1]))
    pass_two(0)
    for copy in pull_copies:
        copy.wait_recv()
    pulled_ref[...] = pull[pl.ds(0, n_user), :] + pull_in[0] + pull_in[1] + pull_in[2]
    for copy in sum_copies:
        copy.wait_recv()
    isum_ref[...] += (
        part_in[0].astype(jnp.float32)
        + part_in[1].astype(jnp.float32)
        + part_in[2].astype(jnp.float32)
    )
    for copy in [
        *user_copies.values(),
        *item_copies[1],
        *item_copies[2],
        *item_copies[3],
        *total_copies,
        *pull_copies,
        *sum_copies,
    ]:
        copy.wait_send()


def group_scores(looked, weights):
    n, width = looked.shape
    n_user, n_item = EXAMPLES, n - EXAMPLES
    f32, bf16 = jnp.float32, jnp.bfloat16
    vmem = pl.BlockSpec(memory_space=pltpu.VMEM)
    return pl.pallas_call(
        score_kernel,
        out_shape=(
            jax.ShapeDtypeStruct((n_user, width), bf16),
            jax.ShapeDtypeStruct((n_item, width), bf16),
            jax.ShapeDtypeStruct((n, width), f32),
            jax.ShapeDtypeStruct((n_user, width), f32),
            jax.ShapeDtypeStruct((1, n_user), f32),
            jax.ShapeDtypeStruct((n_item, width), f32),
        ),
        in_specs=[vmem, *[pl.BlockSpec(memory_space=pltpu.HBM)] * 4],
        out_specs=(vmem,) * 6,
        scratch_shapes=[
            *[pltpu.VMEM(w.shape, f32) for w in weights],
            pltpu.SemaphoreType.DMA((4,)),
            pltpu.VMEM((4 * n_user, width), bf16),
            pltpu.VMEM((4 * n_item, width), bf16),
            pltpu.VMEM((4 * n_user, width), f32),
            pltpu.VMEM((4 * n_user, width), f32),
            pltpu.VMEM((3, n_user, width), f32),
            pltpu.VMEM((4, n_user), f32),
            pltpu.VMEM((3, 4, n_user), f32),
            pltpu.VMEM((4, n_user), f32),
            pltpu.VMEM((3, n_item, width), bf16),
            pltpu.VMEM((3, n_item, width), bf16),
            pltpu.SemaphoreType.DMA((6, 3)),
            pltpu.SemaphoreType.DMA((6, 3)),
        ],
        compiler_params=pltpu.CompilerParams(
            collective_id=0, has_side_effects=True, vmem_limit_bytes=40 * 2**20
        ),
        name="group_scores",
    )(looked, *in_hbm(weights))


def per_device(
    id_table, ada_state, user_first, user_second, item_first, item_second, fetch_rows, lookup_slots
):
    cap = fetch_rows.shape[3]
    slot_index = lookup_slots[0]
    looked, asked = fetch(fetch_rows[0], id_table, slot_index)
    towers = (user_first, user_second, item_first, item_second)
    user_bf, item_bf, out, *sums = group_scores(looked, towers)
    n_dev = asked.shape[0]
    delta, state, summed, loss = tail(
        slot_index, looked, (out, user_bf, item_bf, *sums), towers, asked, ada_state
    )
    new_table, new_state, *grads = finish(id_table, delta, state, summed, towers)
    return (new_table, new_state.reshape(-1), *grads, loss / (n_dev * EXAMPLES))


def solution(mesh):
    finer = Mesh(mesh.devices.reshape(4, 4, 8, 2), DP_SHARD)
    in_specs = (
        P(DP_SHARD, None),
        P(DP_SHARD),
        P(),
        P(),
        P(),
        P(),
        P(DP_SHARD, None, None, None),
        P(DP_SHARD, None),
    )
    out_specs = (P(DP_SHARD, None), P(DP_SHARD), P(), P(), P(), P(), P())
    return jax.shard_map(
        per_device, mesh=finer, in_specs=in_specs, out_specs=out_specs, check_vma=False
    )
```

```python
import functools
import math

import jax
import jax.numpy as jnp
from jax import lax
from jax.experimental import pallas as pl
from jax.experimental.pallas import tpu as pltpu
from jax.sharding import Mesh
from jax.sharding import PartitionSpec as P

DP_SHARD = ("dp_0", "dp_1", "shard_0", "shard_1")
DP = ("dp_0", "dp_1")
SHARD = ("shard_0", "shard_1")
MESH = pl.DeviceIdType.MESH
EXAMPLES = 512

logit_divisor = 0.025
learn_rate = 0.1
epsilon = 1e-08
LOG2_SCALE = math.log2(math.e) / logit_divisor


ROWS = 512
NN, NT, TN = ((1,), (0,)), ((1,), (1,)), ((0,), (0,))


def halves(x):
    high = x.astype(jnp.bfloat16)
    return high, (x - high.astype(jnp.float32)).astype(jnp.bfloat16)


def dot3(a, b, dims):
    (ah, al), (bh, bl) = a, b

    def product(x, y):
        return lax.dot_general(x, y, (dims, ((), ())), preferred_element_type=jnp.float32)

    return product(ah, bh) + (product(ah, bl) + product(al, bh))


def fetched_weights(refs, held, sems):
    copies = [
        pltpu.make_async_copy(ref, into, sems.at[n]) for n, (ref, into) in enumerate(zip(refs, held))
    ]
    for copy in copies:
        copy.start()
    return copies


def in_hbm(arrays):
    return [pltpu.with_memory_space_constraint(a, pltpu.HBM) for a in arrays]


def forward_tile(looked, first, second):
    pre = dot3(halves(looked), first, NN)
    z = dot3(halves(pre * lax.logistic(pre)), second, NN)
    return z, z / jnp.sqrt(jnp.sum(z * z, axis=1, keepdims=True) + 1e-06)


def backward_tile(looked, z, cot, first, second):
    scale = 1.0 / jnp.sqrt(jnp.sum(z * z, axis=1, keepdims=True) + 1e-06)
    vec = z * scale
    dz = halves(scale * (cot - vec * jnp.sum(cot * vec, axis=1, keepdims=True)))
    x = halves(looked)
    pre = dot3(x, first, NN)
    gate = lax.logistic(pre)
    hidden = halves(pre * gate)
    dpre = halves(dot3(dz, second, NT) * (gate * (1.0 + pre * (1.0 - gate))))
    return dot3(dpre, first, NT), dot3(dpre, x, TN), dot3(hidden, dz, TN)


class Place:
    def __init__(self):
        self.x, self.y = lax.axis_index("dp_0"), lax.axis_index("dp_1")
        self.z, self.core = lax.axis_index("shard_0"), lax.axis_index("shard_1")
        self.dp = self.x * 4 + self.y
        self.shard = self.z * 2 + self.core
        self.dev = self.dp * 16 + self.shard

    def shard_peer(self, k):
        p = lax.rem(self.shard + k, 16)
        return p, {"shard_0": lax.div(p, 2), "shard_1": lax.rem(p, 2)}

    def dp_peer(self, k):
        px, py = lax.rem(self.x + k // 4, 4), lax.rem(self.y + k % 4, 4)
        return px * 4 + py, {"dp_0": px, "dp_1": py}

    def any_peer(self, n):
        px = lax.rem(self.x + lax.div(n, 64), 4)
        py = lax.rem(self.y + lax.rem(lax.div(n, 16), 4), 4)
        pz = lax.rem(self.z + lax.div(lax.rem(n, 16), 2), 8)
        pc = lax.rem(self.core + lax.rem(n, 2), 2)
        device = {"dp_0": px, "dp_1": py, "shard_0": pz, "shard_1": pc}
        return (px * 4 + py) * 16 + pz * 2 + pc, device

    def greet(self, meanwhile=lambda: None):
        barrier = pltpu.get_barrier_semaphore()
        for peer in (self.shard_peer, self.dp_peer):
            for k in range(1, 16):
                pl.semaphore_signal(barrier, inc=1, device_id=peer(k)[1], device_id_type=MESH)
        meanwhile()
        pl.semaphore_wait(barrier, 30)

    def pass_on(self, sem):
        for k in range(1, 16):
            pl.semaphore_signal(sem, inc=1, device_id=self.dp_peer(k)[1], device_id_type=MESH)


def remote(src, dst, send, recv, device):
    copy = pltpu.make_async_remote_copy(
        src_ref=src,
        dst_ref=dst,
        send_sem=send,
        recv_sem=recv,
        device_id=device,
        device_id_type=MESH,
    )
    copy.start()
    return copy


def wait_all(ref, sem):
    others = ref.at[pl.ds(0, ref.shape[0] - 1)]
    pltpu.make_async_copy(others, others, sem).wait()


LANES = 16


def fetch_kernel(
    ids_ref,
    table_ref,
    slots_ref,
    looked_ref,
    asked_ref,
    rows,
    table,
    held,
    sorted_ids,
    arrived,
    wanted,
    fetched,
    load_sem,
    all_in,
    send_s,
    recv_s,
    send_d,
    recv_d,
    send_rows,
    recv_rows,
):
    place = Place()
    cap = fetched.shape[1]
    n_dev = fetched.shape[0]
    whole = pltpu.make_async_copy(table_ref, table, load_sem.at[0])
    whole.start()
    place.greet()
    copies = []
    for k in range(1, 16):
        p, device = place.shard_peer(k)
        copies.append(
            remote(ids_ref.at[p], held.at[place.shard], send_s.at[k], recv_s.at[k], device)
        )
    place.pass_on(all_in)
    held[pl.ds(place.shard, 1)] = ids_ref[pl.ds(place.shard, 1)]
    for copy in copies:
        copy.wait_recv()
    per = 128 // LANES
    for half in range(2):
        lines = held[:, half, :]
        for d in range(per):
            sorted_ids[half * per + d] = (
                lines if d == 0 else pltpu.roll(lines, 128 - d * LANES, axis=1)
            )
    late = []
    for k in range(1, 16):
        d, device = place.dp_peer(k)
        late.append(
            remote(
                sorted_ids.at[d], arrived.at[place.dp], send_d.at[k], recv_d.at[k], device
            )
        )
    arrived[pl.ds(place.dp, 1)] = sorted_ids[pl.ds(place.dp, 1)]
    for copy in late:
        copy.wait_recv()
    n_dp = sorted_ids.shape[0]
    field = lax.broadcasted_iota(jnp.int32, (n_dp, 128), 1) // LANES
    for half in range(2):
        lines = arrived[:, half * per, :]
        for q in range(1, per):
            line = pltpu.roll(arrived[:, half * per + q, :], q * LANES, axis=1)
            lines = jnp.where(field == q, line, lines)
        asked_ref[half] = lines
    scalars = pltpu.make_async_copy(asked_ref, wanted, load_sem.at[1])
    scalars.start()
    pl.semaphore_wait(all_in, 15)
    scalars.wait()
    whole.wait()

    def asked_at(dev):
        s = lax.rem(dev, 16)
        return lax.div(s, per), lax.div(dev, 16), lax.rem(s, per) * LANES

    def step(n, carry):
        dev, device = place.any_peer(n)
        half, d, low = asked_at(dev)
        for k in range(cap):
            fetched[dev, k] = table[wanted[half, d, low + k]]
        remote(
            fetched.at[dev],
            rows.at[pl.ds(place.dev * cap, cap)],
            send_rows.at[0],
            recv_rows.at[0],
            device,
        )
        return carry

    lax.fori_loop(1, 256, step, 0, unroll=3)
    half, d, low = asked_at(place.dev)
    for k in range(cap):
        rows[place.dev * cap + k] = table[wanted[half, d, low + k]]
    for copy in copies + late:
        copy.wait_send()
    landed = rows.at[pl.ds(0, (n_dev - 1) * cap)]
    pltpu.make_async_copy(landed, landed, recv_rows.at[0]).wait()

    def look(n, carry):
        looked_ref[n] = rows[slots_ref[n]]
        return carry

    lax.fori_loop(0, looked_ref.shape[0], look, 0, unroll=8)
    wait_all(fetched, send_rows.at[0])


def fetch(ids, table, slots):
    n_dp, n_shard, cap = ids.shape
    n_rows, width = table.shape
    n_dev = n_dp * n_shard
    vmem = pl.BlockSpec(memory_space=pltpu.VMEM)
    dma = pltpu.SemaphoreType.DMA
    lines = jnp.pad(ids, ((0, 0), (0, 0), (0, LANES - cap)), constant_values=n_rows)
    lines = jnp.swapaxes(lines, 0, 1).reshape(n_shard, n_dp * LANES // 128, 128)
    looked, asked = pl.pallas_call(
        fetch_kernel,
        out_shape=(
            jax.ShapeDtypeStruct((slots.shape[0], 1, width), jnp.float32),
            jax.ShapeDtypeStruct((2, n_dp, 128), jnp.int32),
        ),
        in_specs=[
            vmem,
            pl.BlockSpec(memory_space=pltpu.HBM),
            pl.BlockSpec(memory_space=pltpu.SMEM),
        ],
        out_specs=(vmem, vmem),
        scratch_shapes=[
            pltpu.VMEM((n_dev * cap, 1, width), jnp.float32),
            pltpu.VMEM((n_rows, 1, width), jnp.float32),
            pltpu.VMEM(lines.shape, jnp.int32),
            pltpu.VMEM((n_dp, n_shard, 128), jnp.int32),
            pltpu.VMEM((n_dp, n_shard, 128), jnp.int32),
            pltpu.SMEM((2, n_dp, 128), jnp.int32),
            pltpu.VMEM((n_dev, cap, 1, width), jnp.float32),
            dma((2,)),
            pltpu.SemaphoreType.REGULAR,
            *[dma((16,)) for _ in range(4)],
            *[dma((1,)) for _ in range(2)],
        ],
        compiler_params=pltpu.CompilerParams(
            collective_id=1, has_side_effects=True, vmem_limit_bytes=20 * 2**20
        ),
        name="fetch",
    )(
        lines,
        pltpu.with_memory_space_constraint(table.reshape(n_rows, 1, width), pltpu.HBM),
        slots,
    )
    asked = jnp.swapaxes(asked, 0, 1).reshape(n_dev, LANES)
    return looked.reshape(-1, width), asked


PITCH = 10
GROUPS = 4
RT = 1024


def stages_of(place):
    def core_peer(k):
        p = lax.rem(place.core + k, 2)
        return p, {"shard_1": p}

    def z_peer(k):
        p = lax.rem(place.z + k, 8)
        return p, {"shard_0": p}

    return (place.core, 2, core_peer), (place.dp, 16, place.dp_peer), (place.z, 8, z_peer)


def tail_kernel(
    slots_ref,
    looked_ref,
    out_ref,
    user_ref,
    item_ref,
    pulled_ref,
    totals_ref,
    isum_ref,
    uf,
    us,
    tf,
    ts,
    row_ref,
    column_ref,
    state_ref,
    delta_ref,
    state_out,
    weights_ref,
    loss_out,
    uf_held,
    us_held,
    tf_held,
    ts_held,
    load_sem,
    pieces,
    leaving,
    back,
    spread,
    mine,
    arrived,
    losses,
    wsend,
    wrecv,
    gsend,
    grecv,
    lsend,
    lrecv,
    all_in,
    send_rows,
    recv_rows,
):
    place = Place()
    width = looked_ref.shape[1]
    stages = stages_of(place)
    hidden = us_held.shape[0]
    n = 4 * hidden
    held = (uf_held, us_held, tf_held, ts_held)
    loads = fetched_weights((uf, us, tf, ts), held, load_sem)

    def prepare():
        users = user_ref[...].astype(jnp.float32)
        positive = item_ref[pl.ds(0, EXAMPLES), :].astype(jnp.float32)
        totals = totals_ref[...]
        loss = jnp.sum(jnp.log(totals)) - jnp.sum(users * positive) / logit_divisor
        losses[0, pl.ds(place.core, 1)] = jnp.full((1, 8, 128), 1.0, jnp.float32) * loss
        for copy in loads:
            copy.wait()
        weights = [(halves(a[...]), halves(b[...])) for a, b in (held[:2], held[2:])]
        for tile in range(looked_ref.shape[0] // ROWS):
            rows = pl.ds(tile * ROWS, ROWS)
            if tile == 0:
                cot = pulled_ref[...] / jnp.broadcast_to(totals, (width, EXAMPLES)).T - positive
            else:
                cot = isum_ref[pl.ds((tile - 1) * ROWS, ROWS), :]
                if tile == 1:
                    cot = cot - users
            look, first_grad, second_grad = backward_tile(
                looked_ref[rows, :], out_ref[rows, :], cot / logit_divisor, *weights[min(tile, 1)]
            )
            high, low = halves(look)
            pieces[rows, 0:width] = high
            pieces[rows, width : 2 * width] = low
            at = pl.ds(min(tile, 1) * 2 * hidden, hidden)
            after = pl.ds((min(tile, 1) * 2 + 1) * hidden, hidden)
            if tile < 2:
                mine[at, :] = first_grad
                mine[after, :] = second_grad
            else:
                mine[at, :] += first_grad
                mine[after, :] += second_grad

    place.greet(prepare)

    sizes, lows, lands, shifts = [], [0], [], []
    size, landed, shift = n, 0, 0
    for at, side, _ in stages:
        size //= side
        sizes.append(size)
        lows.append(lows[-1] + at * size)
        lands.append(landed)
        shifts.append(shift)
        landed += (side - 1) * size
        shift += side - 1
    started, scatter, gather = [], {}, {}

    def push_sums(stage):
        at, side, peer = stages[stage]
        part = sizes[stage]
        scatter[stage] = []
        for k in range(1, side):
            p, device = peer(k)
            sem = shifts[stage] + k - 1
            start = pl.multiple_of(lows[stage] + p * part, 8)
            scatter[stage].append(
                remote(
                    mine.at[pl.ds(start, part)],
                    arrived.at[pl.ds(lands[stage] + (k - 1) * part, part)],
                    wsend.at[sem],
                    wrecv.at[sem],
                    device,
                )
            )
            scatter[stage].append(
                remote(
                    losses.at[stage, at],
                    losses.at[stage, at],
                    lsend.at[sem],
                    lrecv.at[sem],
                    device,
                )
            )
        started.extend(scatter[stage])

    def add_sums(stage):
        at, side, _ = stages[stage]
        part = sizes[stage]
        for copy in scatter[stage]:
            copy.wait_recv()
        here = pl.ds(pl.multiple_of(lows[stage + 1], 8), part)
        total = mine[here, :]
        for k in range(1, side):
            total += arrived[pl.ds(lands[stage] + (k - 1) * part, part), :]
        loss = losses[stage, 0]
        for p in range(1, side):
            loss += losses[stage, p]
        if stage + 1 < len(stages):
            mine[here, :] = total
            losses[stage + 1, pl.ds(stages[stage + 1][0], 1)] = loss[None]
        else:
            weights_ref[here, :] = total * (1.0 / 256)
            loss_out[...] = loss

    def push_whole(stage):
        at, side, peer = stages[stage]
        here = pl.ds(pl.multiple_of(lows[stage + 1], 8), sizes[stage])
        gather[stage] = []
        for k in range(1, side):
            sem = shifts[stage] + k - 1
            gather[stage].append(
                remote(
                    weights_ref.at[here], weights_ref.at[here], gsend.at[sem], grecv.at[sem], peer(k)[1]
                )
            )
        started.extend(gather[stage])

    def wait_whole(stage):
        for copy in gather[stage]:
            copy.wait_recv()

    def slot_tile(c):
        first = lax.rem(place.x + c, 4) * 64
        slots = slots_ref[...]
        owner = lax.shift_right_logical(slots * 7282, 16)
        wanted = slots + owner - first * PITCH
        shape = (64 * PITCH, wanted.shape[1])
        picks = jnp.where(lax.broadcasted_iota(jnp.int32, shape, 0) == wanted, 1.0, 0.0)
        both = jnp.dot(
            picks.astype(jnp.bfloat16), pieces[...], preferred_element_type=jnp.float32
        )
        total = (both[:, 0:width] + both[:, width : 2 * width]).astype(jnp.bfloat16)
        leaving[pl.ds(first, 64)] = total.reshape(64, PITCH // 2, 2, width)

    def send_tile(c):
        def step(k, carry):
            dev, device = place.any_peer(k)
            remote(leaving.at[dev], back.at[place.dev], send_rows.at[0], recv_rows.at[0], device)
            return carry

        low = 64 * c + (1 if c == 0 else 0)
        lax.fori_loop(low, 64 * (c + 1), step, 0, unroll=3 if c == 0 else 4)

    group_rows = delta_ref.shape[0] // GROUPS

    def pick_rows(step):
        wanted = lax.rem(row_ref[...], group_rows) - step * RT
        shape = (RT, wanted.shape[1])
        picks = jnp.where(lax.broadcasted_iota(jnp.int32, shape, 0) == wanted, 1.0, 0.0)
        return picks.astype(jnp.bfloat16)

    def spread_out():
        grads = back[...].reshape(-1, width).astype(jnp.float32)
        group = column_ref[...] // group_rows
        for g in range(GROUPS):
            spread[:, g * width : (g + 1) * width] = jnp.where(group == g, grads, 0.0).astype(
                jnp.bfloat16
            )

    def update(step):
        every = jnp.dot(pick_rows(step), spread[...], preferred_element_type=jnp.float32)
        for g in range(GROUPS):
            total = every[:, g * width : (g + 1) * width]
            lines = (g * group_rows + step * RT) // width
            before = jnp.concatenate(
                [
                    jnp.broadcast_to(state_ref[pl.ds(lines + i, 1), :], (width, width)).T
                    for i in range(RT // width)
                ],
                axis=0,
            )
            after = before + jnp.sum(total * total, axis=1, keepdims=True) * (1.0 / width)
            delta_ref[pl.ds(g * group_rows + step * RT, RT), :] = (
                learn_rate * total / (jnp.sqrt(after) + epsilon)
            )
            for i in range(RT // width):
                state_out[pl.ds(lines + i, 1), :] = after[i * width : (i + 1) * width].T[0:1, :]

    push_sums(0)
    place.pass_on(all_in)
    slot_tile(0)
    back[pl.ds(place.dev, 1)] = leaving[pl.ds(place.dev, 1)]
    add_sums(0)
    push_sums(1)
    pl.semaphore_wait(all_in, 15)
    send_tile(0)
    for c in (1, 2, 3):
        slot_tile(c)
        send_tile(c)
    add_sums(1)
    push_sums(2)
    add_sums(2)
    push_whole(2)
    wait_whole(2)
    push_whole(1)
    wait_all(back, recv_rows.at[0])
    spread_out()
    steps = group_rows // RT
    for step in range(steps - 1):
        update(step)
    wait_whole(1)
    push_whole(0)
    update(steps - 1)
    for copy in started:
        copy.wait_send()
    wait_all(back, send_rows.at[0])
    wait_whole(0)


def tail(slot_index, looked, results, weights, asked, state):
    n_look, width = looked.shape
    n_dev = asked.shape[0]
    n_rows = state.shape[0]
    n = sum(w.size for w in weights) // width
    f32, bf16 = jnp.float32, jnp.bfloat16
    rows = asked[:, :PITCH].reshape(-1)
    vmem = pl.BlockSpec(memory_space=pltpu.VMEM)
    dma = pltpu.SemaphoreType.DMA
    blocks = (n_dev, PITCH // 2, 2, width)
    delta, new_state, summed, loss = pl.pallas_call(
        tail_kernel,
        out_shape=(
            jax.ShapeDtypeStruct((n_rows, width), f32),
            jax.ShapeDtypeStruct((n_rows // width, width), f32),
            jax.ShapeDtypeStruct((n, width), f32),
            jax.ShapeDtypeStruct((8, 128), f32),
        ),
        in_specs=[*[vmem] * 8, *[pl.BlockSpec(memory_space=pltpu.HBM)] * 4, *[vmem] * 3],
        out_specs=(vmem,) * 4,
        scratch_shapes=[
            *[pltpu.VMEM(w.shape, f32) for w in weights],
            dma((4,)),
            pltpu.VMEM((n_look, 2 * width), bf16),
            pltpu.VMEM(blocks, bf16),
            pltpu.VMEM(blocks, bf16),
            pltpu.VMEM((n_dev * PITCH, GROUPS * width), bf16),
            pltpu.VMEM((n, width), f32),
            pltpu.VMEM((n, width), f32),
            pltpu.VMEM((3, 16, 8, 128), f32),
            *[dma((23,)) for _ in range(6)],
            pltpu.SemaphoreType.REGULAR,
            *[dma((1,)) for _ in range(2)],
        ],
        compiler_params=pltpu.CompilerParams(
            collective_id=2, has_side_effects=True, vmem_limit_bytes=40 * 2**20
        ),
        name="tail",
    )(
        slot_index.reshape(1, n_look),
        looked,
        *results,
        *in_hbm(weights),
        rows.reshape(1, -1),
        rows.reshape(-1, 1),
        state.reshape(-1, width),
    )
    return delta, new_state, summed, loss[0, 0]


def finish_kernel(table_ref, delta_ref, state_ref, weights_ref, new_ref, state_out, *grads):
    new_ref[...] = table_ref[...] - delta_ref[...]

    @pl.when(pl.program_id(0) == 0)
    def _():
        state_out[...] = state_ref[...]
        hidden = grads[1].shape[0]
        for n, grad in enumerate(grads):
            part = weights_ref[pl.ds(n * hidden, hidden), :]
            grad[...] = part if n % 2 else part.T


def finish(table, delta, state, summed, weights):
    n_rows, width = table.shape
    step = n_rows // 4

    def kept(shape):
        return pl.BlockSpec(shape, lambda i: (0, 0))

    lines = pl.BlockSpec((step, width), lambda i: (i, 0))
    f32 = jnp.float32
    return pl.pallas_call(
        finish_kernel,
        out_shape=tuple(
            jax.ShapeDtypeStruct(shape, f32)
            for shape in (table.shape, state.shape, *[w.shape for w in weights])
        ),
        grid=(4,),
        in_specs=[lines, lines, kept(state.shape), kept(summed.shape)],
        out_specs=(lines, kept(state.shape), *[kept(w.shape) for w in weights]),
        compiler_params=pltpu.CompilerParams(vmem_limit_bytes=20 * 2**20),
        name="finish",
    )(table, delta, state, summed)


UT = 1024
CT = 256
IT = 1024

USER_GATHER, ITEM_GATHER, ITEM_GATHER_2, TOTALS, PULLED, ITEM_SUMS = range(6)


def nt(a, b):
    return lax.dot_general(a, b, (((1,), (1,)), ((), ())), preferred_element_type=jnp.float32)


def score_kernel(
    looked_ref,
    uf,
    us,
    tf,
    ts,
    user_ref,
    item_ref,
    out_ref,
    pulled_ref,
    totals_ref,
    isum_ref,
    uf_held,
    us_held,
    tf_held,
    ts_held,
    load_sem,
    users,
    items,
    acc,
    pull,
    pull_in,
    tot,
    tot_in,
    lz,
    part,
    part_in,
    send_sem,
    recv_sem,
):
    n_user = user_ref.shape[0]
    n_item = item_ref.shape[0]
    side = 4
    x = lax.axis_index("dp_0")
    y = lax.axis_index("dp_1")

    def peer(axis, k):
        if axis == "dp_0":
            return {"dp_0": lax.rem(x + k, side)}
        return {"dp_1": lax.rem(y + k, side)}

    def push(kind, axis, k, src, dst):
        copy = pltpu.make_async_remote_copy(
            src_ref=src,
            dst_ref=dst,
            send_sem=send_sem.at[kind, k - 1],
            recv_sem=recv_sem.at[kind, k - 1],
            device_id=peer(axis, k),
            device_id_type=MESH,
        )
        copy.start()
        return copy

    held = (uf_held, us_held, tf_held, ts_held)
    loads = fetched_weights((uf, us, tf, ts), held, load_sem)
    barrier = pltpu.get_barrier_semaphore()
    for axis in ("dp_0", "dp_1"):
        for k in range(1, side):
            pl.semaphore_signal(barrier, inc=1, device_id=peer(axis, k), device_id_type=MESH)
    for copy in loads:
        copy.wait()
    weights = [(halves(a[...]), halves(b[...])) for a, b in (held[:2], held[2:])]

    def forward(tile):
        rows = pl.ds(tile * ROWS, ROWS)
        z, vec = forward_tile(looked_ref[rows, :], *weights[min(tile, 1)])
        out_ref[rows, :] = z
        if tile == 0:
            user_ref[...] = vec.astype(jnp.bfloat16)
        else:
            item_ref[pl.ds((tile - 1) * ROWS, ROWS), :] = vec.astype(jnp.bfloat16)

    forward(0)
    pl.semaphore_wait(barrier, 2 * (side - 1))

    item_copies, user_copies = {1: [], 2: [], 3: []}, {}
    for k in (1, 3, 2):
        user_copies[side - k] = push(
            USER_GATHER, "dp_0", k, user_ref, users.at[pl.ds((side - k) * n_user, n_user)]
        )
    for half, kind in enumerate((ITEM_GATHER, ITEM_GATHER_2)):
        forward(half + 1)
        for k in (1, 3, 2):
            item_copies[side - k].append(
                push(
                    kind,
                    "dp_1",
                    k,
                    item_ref.at[pl.ds(half * ROWS, ROWS)],
                    items.at[pl.ds((side - k) * n_item + half * ROWS, ROWS)],
                )
            )
    users[pl.ds(0, n_user), :] = user_ref[...]
    items[pl.ds(0, n_item), :] = item_ref[...]

    def pass_one(j, low, high):
        def step(n, carry):
            rows = pl.ds(pl.multiple_of(n * UT, UT), UT)
            u = users[rows, :]
            total = jnp.zeros((UT, 128), jnp.float32) if j == 0 else acc[rows, :]
            pulled = jnp.zeros((UT, 128), jnp.float32) if j == 0 else pull[rows, :]
            for c in range(n_item // CT):
                cand = items[pl.ds(j * n_item + c * CT, CT), :]
                e = jnp.exp2(nt(u, cand) * LOG2_SCALE)
                for lane in range(CT // 128):
                    total += e[:, lane * 128 : (lane + 1) * 128]
                pulled += jnp.dot(
                    e.astype(jnp.bfloat16), cand, preferred_element_type=jnp.float32
                )
            acc[rows, :] = total
            pull[rows, :] = pulled
            return carry

        lax.fori_loop(low, high, step, 0)

    steps = side * n_user // UT
    for i in (3, 1, 2):
        user_copies[i].wait_recv()
    pass_one(0, 0, steps)
    for j in (3, 1, 2):
        for copy in item_copies[j]:
            copy.wait_recv()
        pass_one(j, 0, steps)

    for s in range(side):
        sums = acc[pl.ds(s * n_user, n_user), :]
        tot[pl.ds(s, 1), :] = jnp.sum(sums.T, axis=0, keepdims=True)
    total_copies = [push(TOTALS, "dp_0", k, tot, tot_in.at[k - 1]) for k in (1, 3, 2)]
    pull_copies = [
        push(PULLED, "dp_0", k, pull.at[pl.ds(k * n_user, n_user)], pull_in.at[k - 1])
        for k in (1, 3, 2)
    ]
    for copy in total_copies:
        copy.wait_recv()
    for s in range(side):
        whole = tot[pl.ds(s, 1), :]
        for k in range(1, side):
            whole += tot_in[k - 1, pl.ds((s + k) % side, 1), :]
        if s == 0:
            totals_ref[...] = whole
        lz[pl.ds(s, 1), :] = jnp.log2(whole)

    def pass_two(j):
        def step(n, carry):
            rows = pl.ds(pl.multiple_of(n * IT, IT), IT)
            cand = items[pl.ds(pl.multiple_of(j * n_item + n * IT, IT), IT), :]
            sums = jnp.zeros((IT, 128), jnp.float32)
            for s in range(side):
                u = users[pl.ds(s * n_user, n_user), :]
                p = jnp.exp2(nt(cand, u) * LOG2_SCALE - lz[pl.ds(s, 1), :])
                sums += jnp.dot(p.astype(jnp.bfloat16), u, preferred_element_type=jnp.float32)
            if j == 0:
                isum_ref[rows, :] = sums
            else:
                part[j - 1, rows, :] = sums.astype(jnp.bfloat16)
            return carry

        lax.fori_loop(0, n_item // IT, step, 0)

    sum_copies = []
    for j in (2, 1, 3):
        pass_two(j)
        sum_copies.append(push(ITEM_SUMS, "dp_1", j, part.at[j - 1], part_in.at[j - 1]))
    pass_two(0)
    for copy in pull_copies:
        copy.wait_recv()
    pulled_ref[...] = pull[pl.ds(0, n_user), :] + pull_in[0] + pull_in[1] + pull_in[2]
    for copy in sum_copies:
        copy.wait_recv()
    isum_ref[...] += (
        part_in[0].astype(jnp.float32)
        + part_in[1].astype(jnp.float32)
        + part_in[2].astype(jnp.float32)
    )
    for copy in [
        *user_copies.values(),
        *item_copies[1],
        *item_copies[2],
        *item_copies[3],
        *total_copies,
        *pull_copies,
        *sum_copies,
    ]:
        copy.wait_send()


def group_scores(looked, weights):
    n, width = looked.shape
    n_user, n_item = EXAMPLES, n - EXAMPLES
    f32, bf16 = jnp.float32, jnp.bfloat16
    vmem = pl.BlockSpec(memory_space=pltpu.VMEM)
    return pl.pallas_call(
        score_kernel,
        out_shape=(
            jax.ShapeDtypeStruct((n_user, width), bf16),
            jax.ShapeDtypeStruct((n_item, width), bf16),
            jax.ShapeDtypeStruct((n, width), f32),
            jax.ShapeDtypeStruct((n_user, width), f32),
            jax.ShapeDtypeStruct((1, n_user), f32),
            jax.ShapeDtypeStruct((n_item, width), f32),
        ),
        in_specs=[vmem, *[pl.BlockSpec(memory_space=pltpu.HBM)] * 4],
        out_specs=(vmem,) * 6,
        scratch_shapes=[
            *[pltpu.VMEM(w.shape, f32) for w in weights],
            pltpu.SemaphoreType.DMA((4,)),
            pltpu.VMEM((4 * n_user, width), bf16),
            pltpu.VMEM((4 * n_item, width), bf16),
            pltpu.VMEM((4 * n_user, width), f32),
            pltpu.VMEM((4 * n_user, width), f32),
            pltpu.VMEM((3, n_user, width), f32),
            pltpu.VMEM((4, n_user), f32),
            pltpu.VMEM((3, 4, n_user), f32),
            pltpu.VMEM((4, n_user), f32),
            pltpu.VMEM((3, n_item, width), bf16),
            pltpu.VMEM((3, n_item, width), bf16),
            pltpu.SemaphoreType.DMA((6, 3)),
            pltpu.SemaphoreType.DMA((6, 3)),
        ],
        compiler_params=pltpu.CompilerParams(
            collective_id=0, has_side_effects=True, vmem_limit_bytes=40 * 2**20
        ),
        name="group_scores",
    )(looked, *in_hbm(weights))


def per_device(
    id_table, ada_state, user_first, user_second, item_first, item_second, fetch_rows, lookup_slots
):
    cap = fetch_rows.shape[3]
    slot_index = lookup_slots[0]
    looked, asked = fetch(fetch_rows[0], id_table, slot_index)
    towers = (user_first, user_second, item_first, item_second)
    user_bf, item_bf, out, *sums = group_scores(looked, towers)
    n_dev = asked.shape[0]
    delta, state, summed, loss = tail(
        slot_index, looked, (out, user_bf, item_bf, *sums), towers, asked, ada_state
    )
    new_table, new_state, *grads = finish(id_table, delta, state, summed, towers)
    return (new_table, new_state.reshape(-1), *grads, loss / (n_dev * EXAMPLES))


def solution(mesh):
    finer = Mesh(mesh.devices.reshape(4, 4, 8, 2), DP_SHARD)
    in_specs = (
        P(DP_SHARD, None),
        P(DP_SHARD),
        P(),
        P(),
        P(),
        P(),
        P(DP_SHARD, None, None, None),
        P(DP_SHARD, None),
    )
    out_specs = (P(DP_SHARD, None), P(DP_SHARD), P(), P(), P(), P(), P())
    return jax.shard_map(
        per_device, mesh=finer, in_specs=in_specs, out_specs=out_specs, check_vma=False
    )
```
